32 devices in a mesh: fsdp: 4 (over y, x), rep: 8 (over z, core).
Axes of the slice: x: 2, y: 2, z: 4, core: 2. Of those that a mesh axis runs over, the one named last changes fastest.
Arguments:
- tokens: bfloat16 [64, 256, 384], P(('fsdp', 'rep')), may hold values from -6 to 6
- conditions: bfloat16 [64, 384], P(('fsdp', 'rep')), may hold values from -6 to 6
- assignment: int32 [64], P(('fsdp', 'rep')), may hold values from 0 to 63, each once
- params: float32 [2654208], P('fsdp')
- momentum: float32 [2654208], P('fsdp'), may hold values from -24 to 24
- cotangent: bfloat16 [64, 256, 384], P(('fsdp', 'rep')), may hold values from -6 to 6
Outputs:
- blended: bfloat16 [64, 256, 384], P(('fsdp', 'rep'))
- grad_tokens: float32 [64, 256, 384], P(('fsdp', 'rep'))
- grad_params: float32 [2654208], P('fsdp')
- new_params: float32 [2654208], P('fsdp')
- new_momentum: float32 [2654208], P('fsdp')
The draws below stay inside these ranges and needn't reach their ends.
Inputs may be any that keep to these rules, and one draw needn't show every extreme that they name: assignment is a permutation of the latent numbers.
All inputs are finite; a program needn't handle non-finite values.
Results may differ from the reference program's by a relative error of at most 0.014.
The reference program's roundings to bfloat16 on the way count: a program that leaves them out, or rounds other values in their place, can miss the bound.
Values may be sent and summed in bfloat16 or wider, within the bound.
No kernel may reach another device: no remote copies, remote signals or barrier semaphores. Data moves between devices by JAX's collectives and lax.ppermute only.
A program may use at most 192 MiB of HBM per device.

```python
import math
import jax
import jax.numpy as jnp
from jax import lax

D = 384
HEADS = 6
HD = 64
FF = 1536
SEQ = 256
NS_ITERS = 3
LATENTS = 64
TOKENS = 16384
P_SIZE = 2654208


def draw_block(key, rows_count, cols_count, fan_in, factor):
    values = jax.random.normal(key, (rows_count, cols_count), jnp.float32)
    return values * factor * fan_in ** (-0.5)


def draw_params(key, part):
    subkeys = jax.random.split(key, 6)
    adaln_part = draw_block(subkeys[0], D, 6 * D, D, 1.0)
    qkv_part = draw_block(subkeys[1], D, 3 * D, D, 1.0)
    out_part = draw_block(subkeys[3], D, D, D, 4.0)
    up_part = draw_block(subkeys[4], D, FF, D, 1.0)
    down_part = draw_block(subkeys[5], FF, D, FF, 1.0)
    return jnp.concatenate([adaln_part.reshape(-1), qkv_part.reshape(-1), out_part.reshape(-1), up_part.reshape(-1), down_part.reshape(-1)])


def steps_of(own_key, shape, cuts, least, top_value):
    level = 1.0
    for axis_at, parts in cuts:
        steps = jax.random.uniform(jax.random.fold_in(jax.random.fold_in(own_key, 6), axis_at), (parts,), jnp.float32, least / len(cuts), top_value / len(cuts))
        level = level * jnp.repeat(jnp.exp(steps), shape[axis_at] // parts).reshape((-1,) + (1,) * (len(shape) - 1 - axis_at))
    return level


def centred(stream_key, dims, scale, reach, shards=(), kind=jnp.bfloat16):
    entries = jax.random.normal(stream_key, dims, jnp.float32) * scale
    if len(shards) > 0:
        entries = steps_of(stream_key, dims, shards, -0.22, 0.18) * entries
    return jnp.clip(entries, min=-reach, max=reach).astype(kind)


def setup_inputs(seed: int = 0) -> dict:
    key_of = jax.random.split(jax.random.key(seed), 7)
    tokens = centred(key_of[0], (LATENTS, SEQ, D), 1.0, 6.0, ((0, 32),))
    conditions = centred(key_of[1], (LATENTS, D), 1.0, 6.0, ((0, 32),))
    assignment = jax.random.permutation(key_of[2], LATENTS).astype(jnp.int32)
    params = draw_params(jax.random.fold_in(key_of[6], 71), 0)
    momentum = centred(key_of[4], (P_SIZE,), (0.03 * TOKENS ** 0.5), 24.0, ((0, 4),), jnp.float32)
    cotangent = centred(key_of[5], (LATENTS, SEQ, D), 1.0, 6.0, ((0, 32),))
    return dict(tokens=tokens, conditions=conditions, assignment=assignment, params=params, momentum=momentum, cotangent=cotangent)


LN_EPSILON = 1e-06
MOMENTUM_RATE = 0.95
LEARN_RATE = 0.2
COEFF_A = 3.4445
COEFF_B = -4.775
COEFF_C = 2.0315

def matrix_shapes():
    return [(D, 6 * D), (D, 3 * D), (D, D), (D, FF), (FF, D)]

def unpack(flat_vec):
    pieces = []
    offset = 0
    for rows_count, cols_count in matrix_shapes():
        pieces.append(flat_vec[offset:offset + rows_count * cols_count].reshape(rows_count, cols_count))
        offset += rows_count * cols_count
    return pieces

def matmul(lhs_array, rhs_array):
    return jnp.dot(lhs_array, rhs_array, preferred_element_type=jnp.float32)

def contract(pattern, lhs_array, rhs_array):
    return jnp.einsum(pattern, lhs_array.astype(jnp.float32), rhs_array.astype(jnp.float32))

def modulate(hidden, shifts, scales):
    center = lax.optimization_barrier(jnp.mean(hidden, axis=-1, keepdims=True))
    spread = lax.optimization_barrier(jnp.mean(jnp.square(hidden - center), axis=-1, keepdims=True))
    return (hidden - center) * lax.rsqrt(spread + LN_EPSILON) * (1.0 + scales) + shifts

def gelu_tanh(values_in):
    return jax.nn.gelu(values_in, approximate=True)

def orthogonalize(matrix):
    flipped = matrix.shape[0] > matrix.shape[1]
    current = matrix.T if flipped else matrix
    current = current / (jnp.sqrt(jnp.sum(current * current)) + 1e-07)
    for newton_step in range(NS_ITERS):
        square = jnp.dot(current, current.T, precision=lax.Precision.HIGHEST)
        polynomial = COEFF_B * square + COEFF_C * jnp.dot(square, square, precision=lax.Precision.HIGHEST)
        current = COEFF_A * current + jnp.dot(polynomial, current, precision=lax.Precision.HIGHEST)
    return current.T if flipped else current

def update_scale(rows_count, cols_count):
    return LEARN_RATE * 0.2 * math.sqrt(max(rows_count, cols_count))

def forward_pass(tokens, cond_rows, weights):
    adaln_weight, qkv_weight, out_weight, up_weight, down_weight = weights
    batch_size = tokens.shape[0]
    row_count = batch_size * SEQ
    silu_cond = jax.nn.silu(cond_rows.astype(jnp.float32)).astype(jnp.bfloat16)
    modulation = matmul(silu_cond, adaln_weight).reshape(batch_size, 6, 1, D)
    mod_parts = tuple((modulation[:, position] for position in range(6)))
    shift_attn, scale_attn, gate_attn, shift_mlp, scale_mlp, gate_mlp = mod_parts
    residual = tokens.astype(jnp.float32)
    attn_input = modulate(residual, shift_attn, scale_attn).astype(jnp.bfloat16)
    qkv_all = matmul(attn_input.reshape(row_count, D), qkv_weight).astype(jnp.bfloat16)
    qkv_heads = qkv_all.reshape(batch_size, SEQ, 3, HEADS, HD).transpose(2, 0, 3, 1, 4)
    queries, key_vecs, value_vecs = (qkv_heads[0], qkv_heads[1], qkv_heads[2])
    scores = contract('bhqd,bhkd->bhqk', queries, key_vecs) * HD ** (-0.5)
    log_total = jax.nn.logsumexp(scores, axis=-1, keepdims=True)
    attn_probs = jnp.exp(scores - log_total).astype(jnp.bfloat16)
    attn_mixed = contract('bhqk,bhkd->bhqd', attn_probs, value_vecs).astype(jnp.bfloat16)
    attn_mixed = attn_mixed.transpose(0, 2, 1, 3).reshape(row_count, D)
    attn_out = matmul(attn_mixed, out_weight).reshape(batch_size, SEQ, D)
    after_attn = residual + gate_attn * attn_out
    mlp_input = modulate(after_attn, shift_mlp, scale_mlp).astype(jnp.bfloat16).reshape(row_count, D)
    pre_act = matmul(mlp_input, up_weight)
    activated = gelu_tanh(pre_act).astype(jnp.bfloat16)
    mlp_out = matmul(activated, down_weight).reshape(batch_size, SEQ, D)
    blended = (after_attn + gate_mlp * mlp_out).astype(jnp.bfloat16)
    kept_state = (silu_cond, mod_parts, residual, attn_input, queries, key_vecs, value_vecs, log_total, attn_mixed, attn_out, after_attn, mlp_input, pre_act, activated, mlp_out)
    return (blended, kept_state)

def backward_pass(kept_state, weights, cotangent):
    silu_cond, mod_parts, residual, attn_input, queries, key_vecs, value_vecs, log_total, attn_mixed, attn_out, after_attn, mlp_input, pre_act, activated, mlp_out = kept_state
    adaln_weight, qkv_weight, out_weight, up_weight, down_weight = weights
    shift_attn, scale_attn, gate_attn, shift_mlp, scale_mlp, gate_mlp = mod_parts
    batch_size = cotangent.shape[0]
    row_count = batch_size * SEQ
    upstream = cotangent.astype(jnp.float32)
    grad_gate_mlp = lax.optimization_barrier(jnp.sum(upstream * mlp_out, axis=1, keepdims=True))
    grad_mlp_out = (upstream * gate_mlp).astype(jnp.bfloat16).reshape(row_count, D)
    grad_down = matmul(activated.T, grad_mlp_out)
    grad_act = matmul(grad_mlp_out, down_weight.T)
    grad_pre = jax.vjp(gelu_tanh, pre_act)[1](grad_act)[0].astype(jnp.bfloat16)
    grad_up = matmul(mlp_input.T, grad_pre)
    grad_mlp_in = matmul(grad_pre, up_weight.T).reshape(batch_size, SEQ, D)
    grad_after, grad_shift_mlp, grad_scale_mlp = jax.vjp(modulate, after_attn, shift_mlp, scale_mlp)[1](grad_mlp_in)
    grad_after = upstream + grad_after
    grad_gate_attn = lax.optimization_barrier(jnp.sum(grad_after * attn_out, axis=1, keepdims=True))
    grad_attn_out = (grad_after * gate_attn).astype(jnp.bfloat16).reshape(row_count, D)
    grad_outw = matmul(attn_mixed.T, grad_attn_out)
    grad_mixed = matmul(grad_attn_out, out_weight.T).astype(jnp.bfloat16)
    grad_mixed = grad_mixed.reshape(batch_size, SEQ, HEADS, HD).transpose(0, 2, 1, 3)
    scores = contract('bhqd,bhkd->bhqk', queries, key_vecs) * HD ** (-0.5)
    probs_full = jnp.exp(scores - log_total)
    grad_values = contract('bhqk,bhqd->bhkd', probs_full.astype(jnp.bfloat16), grad_mixed)
    grad_probs = contract('bhqd,bhkd->bhqk', grad_mixed, value_vecs)
    row_dots = lax.optimization_barrier(jnp.sum(probs_full * grad_probs, axis=-1, keepdims=True))
    grad_scores = (probs_full * (grad_probs - row_dots) * HD ** (-0.5)).astype(jnp.bfloat16)
    grad_queries = contract('bhqk,bhkd->bhqd', grad_scores, key_vecs)
    grad_keys = contract('bhqk,bhqd->bhkd', grad_scores, queries)
    grad_qkv = jnp.stack([grad_queries, grad_keys, grad_values], axis=0).transpose(1, 3, 0, 2, 4)
    grad_qkv = grad_qkv.reshape(row_count, 3 * D).astype(jnp.bfloat16)
    grad_qkvw = matmul(attn_input.reshape(row_count, D).T, grad_qkv)
    grad_attn_in = matmul(grad_qkv, qkv_weight.T).reshape(batch_size, SEQ, D)
    grad_resid, grad_shift_attn, grad_scale_attn = jax.vjp(modulate, residual, shift_attn, scale_attn)[1](grad_attn_in)
    grad_tokens = grad_after + grad_resid
    grad_mod = jnp.concatenate([grad_shift_attn, grad_scale_attn, grad_gate_attn, grad_shift_mlp, grad_scale_mlp, grad_gate_mlp], axis=1)
    grad_mod = grad_mod.reshape(batch_size, 6 * D).astype(jnp.bfloat16)
    grad_adaln = matmul(silu_cond.T, grad_mod)
    flat_grads = jnp.concatenate([grad_adaln.reshape(-1), grad_qkvw.reshape(-1), grad_outw.reshape(-1), grad_up.reshape(-1), grad_down.reshape(-1)])
    return (grad_tokens, flat_grads)

def reference(tokens, conditions, assignment, params, momentum, cotangent):
    weights = [matrix.astype(jnp.bfloat16) for matrix in unpack(params)]
    cond_rows = conditions[assignment]
    per_block = 16
    block_count = LATENTS // per_block

    def scan_step(total, block_inputs):
        tok_block, cond_block, cot_block = block_inputs
        out_block, kept_state = forward_pass(tok_block, cond_block, weights)
        grad_block, flat_grads = backward_pass(kept_state, weights, cot_block)
        return (total + flat_grads, (out_block, grad_block))
    total, (out_blocks, grad_blocks) = lax.scan(scan_step, jnp.zeros((P_SIZE,), jnp.float32), (tokens.reshape(block_count, per_block, SEQ, D), cond_rows.reshape(block_count, per_block, D), cotangent.reshape(block_count, per_block, SEQ, D)))
    blended = out_blocks.reshape(LATENTS, SEQ, D)
    grad_tokens = grad_blocks.reshape(LATENTS, SEQ, D)
    new_momentum = MOMENTUM_RATE * momentum + total
    updates = []
    offset = 0
    for rows_count, cols_count in matrix_shapes():
        length = rows_count * cols_count
        piece = new_momentum[offset:offset + length].reshape(rows_count, cols_count)
        updates.append((update_scale(rows_count, cols_count) * orthogonalize(piece)).reshape(-1))
        offset += length
    new_params = params - jnp.concatenate(updates)
    return (blended, grad_tokens, total, new_params, new_momentum)
```

```python
import functools
import math

import jax
import jax.numpy as jnp
from jax import lax
from jax.experimental import pallas as pl
from jax.experimental.pallas import tpu as pltpu
from jax.sharding import PartitionSpec as P

D = 384
HEADS = 6
HD = 64
FF = 1536
SEQ = 256
NS_ITERS = 3

LN_EPSILON = 1e-06
MOMENTUM_RATE = 0.95
LEARN_RATE = 0.2
COEFF_A = 3.4445
COEFF_B = -4.775
COEFF_C = 2.0315

F32 = jnp.float32
BF16 = jnp.bfloat16
ANY = pl.ANY
VMEM_LIMIT = 60 * 1024 * 1024

MATS = ((D, 6 * D, 0, True), (D, 3 * D, 6, True), (D, D, 9, True), (D, FF, 10, True), (FF, D, 14, False))
NBLOCKS = 18
ADALN, QKV, OUTW, UP, DOWN = range(5)
P_SIZE = sum(m[0] * m[1] for m in MATS)
GRAD_ROWS = 3584
KEPT_ROWS = 16


def update_scale(mat):
    return LEARN_RATE * 0.2 * math.sqrt(max(MATS[mat][0], MATS[mat][1]))


def shard_pieces(shard, count):
    size = P_SIZE // count
    begin, end = shard * size, (shard + 1) * size
    pieces, crow, offset = [], 0, 0
    for mat, (rows, cols, first, by_cols) in enumerate(MATS):
        lo, hi = max(begin, offset), min(end, offset + rows * cols)
        if lo < hi:
            r0, r1 = (lo - offset) // cols, (hi - offset) // cols
            stride = cols // 128
            base = (offset - begin) // 128
            if by_cols:
                for b in range(cols // D):
                    pieces.append((mat, first + b, r0, r1 - r0, crow, base + r0 * stride + 3 * b, stride))
                    crow += r1 - r0
            else:
                r = r0
                while r < r1:
                    n = min(r1, (r // D + 1) * D) - r
                    pieces.append((mat, first + r // D, r % D, n, crow, base + r * stride, stride))
                    crow += n
                    r += n
        offset += rows * cols
    return pieces


def mm(a, b, ca=1, cb=0):
    return lax.dot_general(a, b, (((ca,), (cb,)), ((), ())), preferred_element_type=F32)


def vspec():
    return pl.BlockSpec(memory_space=pltpu.VMEM)


def aspec():
    return pl.BlockSpec(memory_space=ANY)


def sspec():
    return pl.BlockSpec(memory_space=pltpu.SMEM)


def params_of(**kw):
    return pltpu.CompilerParams(vmem_limit_bytes=VMEM_LIMIT, **kw)


def prep_kernel(count, s_ref, p_ref, m_ref, w_ref, mo_ref):
    for shard in range(count):

        @pl.when(s_ref[0] == shard)
        def _(shard=shard):
            for _, _, _, n, crow, frow, stride in shard_pieces(shard, count):
                for j in range(3):
                    src = pl.ds(frow + j, n, stride=stride)
                    w_ref[crow : crow + n, 128 * j : 128 * j + 128] = p_ref[src, :].astype(BF16)
                    mo_ref[crow : crow + n, 128 * j : 128 * j + 128] = m_ref[src, :].astype(BF16)


def prep(sidx, params, momentum, count):
    rows = P_SIZE // count // D
    out = jax.ShapeDtypeStruct((rows, D), BF16)
    return pl.pallas_call(
        functools.partial(prep_kernel, count),
        out_shape=(out, out),
        in_specs=[sspec(), vspec(), vspec()],
        out_specs=(vspec(), vspec()),
        compiler_params=params_of(),
        name="prep",
    )(sidx, params, momentum)


def layer_norm(h):
    center = jnp.mean(h, axis=-1, keepdims=True)
    cent = h - center
    spread = jnp.mean(jnp.square(cent), axis=-1, keepdims=True)
    rstd = lax.rsqrt(spread + LN_EPSILON)
    return cent * rstd, rstd


def layer_norm_grad(xhat, rstd, gx):
    m1 = jnp.mean(gx, axis=-1, keepdims=True)
    m2 = jnp.mean(gx * xhat, axis=-1, keepdims=True)
    return rstd * (gx - m1 - xhat * m2)


def gather_plan(count):
    plan = []
    half = P_SIZE // count // D // 2
    for shard in range(count):
        for _, block, r0, n, crow, _, _ in shard_pieces(shard, count):
            cuts = sorted({crow, crow + n} | {c for c in range(0, 2 * half + 1, half // 2) if crow < c < crow + n})
            for a, b in zip(cuts[:-1], cuts[1:]):
                plan.append((shard, a // half, a % half, b - a, block, r0 + a - crow))
    return plan


def load_weights_fast(s_ref, bufs, wts, sems, start):
    own, rx, ry, rda, rdb, px, py, pda, pdb = bufs
    me, core = s_ref[0], s_ref[1]
    half = own.shape[0] // 2
    quarter = half // 2
    for q, (shard, h, r, n, block, br) in enumerate(gather_plan(4)):
        dst = wts.at[block, br : br + n]
        if not start:
            pltpu.make_async_copy(own.at[0:n], dst, sems.at[q]).wait()
            continue
        for m in range(4):
            for mine in (True, False):
                if m == 0 and not mine:
                    continue
                cond = me == (shard ^ m)
                if m > 0:
                    cond = jnp.logical_and(cond, (core == h) if mine else (core != h))
                if m == 0:
                    src = own.at[h * half + r : h * half + r + n]
                elif m < 3:
                    src = ((rx, ry) if mine else (px, py))[m - 1].at[r : r + n]
                else:
                    pair = (rda, rdb) if mine else (pda, pdb)
                    k = r // quarter
                    src = pair[k].at[r - k * quarter : r - k * quarter + n]

                @pl.when(cond)
                def _(src=src, dst=dst, q=q):
                    pltpu.make_async_copy(src, dst, sems.at[q]).start()


def main_kernel(nbuf, fast, rows, s_ref, table, tok, cot, *refs):
    bufs = refs[:nbuf]
    (blend, qkv, probs, amix_in, gafter, gmx, mods, gmod, silu, wqkv, grads) = refs[nbuf : nbuf + 11]
    wts, ao_s, aa_s, amix, minp, gmi, mo, sems = refs[nbuf + 11 :]
    lat = rows // SEQ
    if fast:
        load_weights_fast(s_ref, bufs, wts, sems, True)
    else:
        whole = pltpu.make_async_copy(bufs[0], wts, sems.at[0])
        whole.start()
    nt = table.shape[0]
    lanes = lax.broadcasted_iota(jnp.int32, (16, nt), 1)
    rws = lax.broadcasted_iota(jnp.int32, (16, nt), 0)
    pick = jnp.zeros((16, nt), jnp.bool_)
    for l in range(lat):
        pick = pick | ((rws == l) & (lanes == s_ref[2 + l]))
    cond = mm(pick.astype(F32).astype(BF16), table[...])
    sc = (cond * (1.0 / (1.0 + jnp.exp(-cond)))).astype(BF16)
    silu[...] = sc.astype(F32)
    if fast:
        load_weights_fast(s_ref, bufs, wts, sems, False)
    else:
        whole.wait()
    for b in range(6):
        mods[b] = mm(sc, wts[b])[:8]
    for j in range(3):
        wqkv[j] = wts[6 + j]
    grads[9 * D :, :] = jnp.zeros((GRAD_ROWS - 9 * D, D), F32)

    def mod(b, l):
        return mods[b, l : l + 1, :]

    for l in range(lat):
        rs = slice(l * SEQ, (l + 1) * SEQ)
        xhat, _ = layer_norm(tok[rs, :].astype(F32))
        amix_in[rs, :] = (xhat * (1.0 + mod(1, l)) + mod(0, l)).astype(BF16)
    ai = amix_in[...]
    for j in range(3):
        qkv[j] = mm(ai, wts[6 + j]).astype(BF16)

    low = lax.broadcasted_iota(jnp.int32, (SEQ, 128), 1) < HD
    zero = jnp.zeros((SEQ, 128), BF16)

    def attend(l, carry):
        rs = pl.ds(pl.multiple_of(l * SEQ, SEQ), SEQ)
        for hp in range(HEADS // 2):
            cs = slice(hp * 128, hp * 128 + 128)
            q, k, v = qkv[0, rs, cs], qkv[1, rs, cs], qkv[2, rs, cs]
            outs = []
            for h in range(2):
                qm = jnp.where(low if h == 0 else jnp.logical_not(low), q, zero)
                s = mm(qm, k, 1, 1) * HD ** (-0.5)
                top = jnp.max(s, axis=-1, keepdims=True)
                e = jnp.exp(s - top)
                pr = e * (1.0 / jnp.sum(e, axis=-1, keepdims=True))
                probs[l * HEADS + hp * 2 + h] = pr
                outs.append(mm(pr.astype(BF16), v))
            amix[rs, cs] = jnp.where(low, outs[0], outs[1]).astype(BF16)
        return carry

    lax.fori_loop(0, lat, attend, 0)

    ao = mm(amix[...], wts[9])
    ao_s[...] = ao
    for l in range(lat):
        rs = slice(l * SEQ, (l + 1) * SEQ)
        aa = tok[rs, :].astype(F32) + mod(2, l) * ao_s[rs, :]
        aa_s[rs, :] = aa
        xhat, _ = layer_norm(aa)
        minp[rs, :] = (xhat * (1.0 + mod(4, l)) + mod(3, l)).astype(BF16)
        gmx[rs, :] = (cot[rs, :].astype(F32) * mod(5, l)).astype(BF16)
    gmi[...] = jnp.zeros_like(gmi)
    mo[...] = jnp.zeros_like(mo)

    def mlp(j, carry):
        wu, wd = wts[10 + j], wts[14 + j]
        u = mm(minp[...], wu)
        c = math.sqrt(2.0 / math.pi)
        u2 = u * u
        t = jnp.tanh(c * (u + 0.044715 * (u2 * u)))
        half = 0.5 * (1.0 + t)
        act = (u * half).astype(BF16)
        slope = half + 0.5 * u * (1.0 - t * t) * (c * (1.0 + 3.0 * 0.044715 * u2))
        mo[...] += mm(act, wd)
        gmo = gmx[...]
        gp = (mm(gmo, wd, 1, 1) * slope).astype(BF16)
        grads[pl.ds(pl.multiple_of((5 + j) * D, D), D), :] = mm(act, gmo, 0, 0)
        grads[pl.ds(pl.multiple_of((1 + j) * D, D), D), :] = mm(minp[...], gp, 0, 0)
        gmi[...] += mm(gp, wu, 1, 1)
        return carry

    lax.fori_loop(0, FF // D, mlp, 0)

    gmod[...] = jnp.zeros_like(gmod)
    for l in range(lat):
        rs = slice(l * SEQ, (l + 1) * SEQ)
        up = cot[rs, :].astype(F32)
        blend[rs, :] = (aa_s[rs, :] + mod(5, l) * mo[rs, :]).astype(BF16)
        gmod[5, l : l + 1, :] = jnp.sum(up * mo[rs, :], axis=0, keepdims=True)
        xhat, rstd = layer_norm(aa_s[rs, :])
        g = gmi[rs, :]
        gmod[3, l : l + 1, :] = jnp.sum(g, axis=0, keepdims=True)
        gmod[4, l : l + 1, :] = jnp.sum(g * xhat, axis=0, keepdims=True)
        ga = up + layer_norm_grad(xhat, rstd, g * (1.0 + mod(4, l)))
        gafter[rs, :] = ga
        gmod[2, l : l + 1, :] = jnp.sum(ga * ao_s[rs, :], axis=0, keepdims=True)
        minp[rs, :] = (ga * mod(2, l)).astype(BF16)
    gao = minp[...]
    grads[0:D, :] = mm(amix[...], gao, 0, 0)
    gmx[...] = mm(gao, wts[9], 1, 1).astype(BF16)


def main_call(sidx, table, tokens, cotangent, bufs, fast):
    rows = tokens.shape[0]
    lat = rows // SEQ
    sd = jax.ShapeDtypeStruct
    outs = (
        sd((rows, D), BF16),
        sd((3, rows, D), BF16),
        sd((lat * HEADS, SEQ, SEQ), F32),
        sd((rows, D), BF16),
        sd((rows, D), F32),
        sd((rows, D), BF16),
        sd((6, 8, D), F32),
        sd((6, 8, D), F32),
        sd((16, D), F32),
        sd((3, D, D), BF16),
        sd((GRAD_ROWS, D), F32),
    )
    nsem = len(gather_plan(4)) if fast else 1
    return pl.pallas_call(
        functools.partial(main_kernel, len(bufs), fast, rows),
        out_shape=outs,
        in_specs=[sspec(), vspec(), vspec(), vspec()] + [aspec()] * len(bufs),
        out_specs=(vspec(),) * len(outs),
        scratch_shapes=[
            pltpu.VMEM((NBLOCKS, D, D), BF16),
            pltpu.VMEM((rows, D), F32),
            pltpu.VMEM((rows, D), F32),
            pltpu.VMEM((rows, D), BF16),
            pltpu.VMEM((rows, D), BF16),
            pltpu.VMEM((rows, D), F32),
            pltpu.VMEM((rows, D), F32),
            pltpu.SemaphoreType.DMA((nsem,)),
        ],
        compiler_params=params_of(),
        cost_estimate=pl.CostEstimate(flops=20_000_000_000, bytes_accessed=30_000_000, transcendentals=0),
        name="main",
    )(sidx, table, tokens, cotangent, *bufs)


def heads_kernel(rows, tok, qkv, probs, ai, gafter, gmx, mods, gmod1, silu, wqkv, gtok, gq, keep, gqkv, srow):
    lat = rows // SEQ
    low = lax.broadcasted_iota(jnp.int32, (SEQ, 128), 1) < HD
    zero = jnp.zeros((SEQ, 128), BF16)

    def back(l, carry):
        rs = pl.ds(pl.multiple_of(l * SEQ, SEQ), SEQ)
        for hp in range(HEADS // 2):
            cs = slice(hp * 128, hp * 128 + 128)
            q, k, v = qkv[0, rs, cs], qkv[1, rs, cs], qkv[2, rs, cs]
            g = gmx[rs, cs]
            res = []
            for h in range(2):
                p = probs[l * HEADS + hp * 2 + h]
                gm = jnp.where(low if h == 0 else jnp.logical_not(low), g, zero)
                gv = mm(p.astype(BF16), g, 0, 0)
                gpr = mm(gm, v, 1, 1)
                dots = jnp.sum(p * gpr, axis=-1, keepdims=True)
                gs = (p * (gpr - dots) * HD ** (-0.5)).astype(BF16)
                res.append((mm(gs, k), mm(gs, q, 0, 0), gv))
            for j in range(3):
                gqkv[j, rs, cs] = jnp.where(low, res[0][j], res[1][j]).astype(BF16)
        return carry

    lax.fori_loop(0, lat, back, 0)
    gai = None
    for j in range(3):
        part = mm(gqkv[j], wqkv[j], 1, 1)
        gai = part if gai is None else gai + part
        gq[j * D : (j + 1) * D, :] = mm(ai[...], gqkv[j], 0, 0)
    srow[...] = jnp.zeros_like(srow)
    for l in range(lat):
        rs = slice(l * SEQ, (l + 1) * SEQ)
        xhat, rstd = layer_norm(tok[rs, :].astype(F32))
        g = gai[rs, :]
        srow[l : l + 1, :] = jnp.sum(g, axis=0, keepdims=True)
        srow[lat + l : lat + l + 1, :] = jnp.sum(g * xhat, axis=0, keepdims=True)
        gtok[rs, :] = gafter[rs, :] + layer_norm_grad(xhat, rstd, g * (1.0 + mods[1, l : l + 1, :]))
        for b in range(2, 6):
            srow[lat * b + l : lat * b + l + 1, :] = gmod1[b, l : l + 1, :]
        srow[lat * 6 + l : lat * 6 + l + 1, :] = silu[l : l + 1, :]
    keep[...] = srow[...].astype(BF16)


def heads_call(tokens, qkv, probs, ai, gafter, gmx, mods, gmod1, silu, wqkv):
    rows = tokens.shape[0]
    sd = jax.ShapeDtypeStruct
    outs = (sd((rows, D), F32), sd((3 * D, D), F32), sd((KEPT_ROWS, D), BF16))
    return pl.pallas_call(
        functools.partial(heads_kernel, rows),
        out_shape=outs,
        in_specs=[vspec()] * 10,
        out_specs=(vspec(),) * 3,
        scratch_shapes=[pltpu.VMEM((3, rows, D), BF16), pltpu.VMEM((KEPT_ROWS, D), F32)],
        compiler_params=params_of(),
        cost_estimate=pl.CostEstimate(flops=12_000_000_000, bytes_accessed=12_000_000, transcendentals=0),
        name="heads",
    )(tokens, qkv, probs, ai, gafter, gmx, mods, gmod1, silu, wqkv)


def split(x):
    hi = x.astype(BF16)
    return hi, (x - hi.astype(F32)).astype(BF16)


def mm3(a, b, ca=1, cb=0):
    return mm(a[0], b[0], ca, cb) + (mm(a[0], b[1], ca, cb) + mm(a[1], b[0], ca, cb))


def newton_schulz(mat_ref, upd_ref, pow_s, nblk, flipped, factor):
    pow_s[...] = jnp.zeros_like(pow_s)

    def gram(b, carry):
        x = split(mat_ref[b])

        @pl.when(flipped)
        def _():
            pow_s[...] += mm3(x, x, 0, 0)

        @pl.when(jnp.logical_not(flipped))
        def _():
            pow_s[...] += mm3(x, x, 1, 1)

        return carry

    lax.fori_loop(0, nblk, gram, 0)
    g = pow_s[...]
    ri = lax.broadcasted_iota(jnp.int32, (D, D), 0)
    ci = lax.broadcasted_iota(jnp.int32, (D, D), 1)
    eye = ri == ci
    diag = jnp.sum(jnp.where(eye, g, 0.0), axis=1, keepdims=True)
    total = jnp.sum(diag, axis=0, keepdims=True)
    inv = 1.0 / (jnp.sqrt(total) + 1e-07)
    a = g * (inv * inv)
    q = None
    for it in range(NS_ITERS):
        sa = split(a)
        poly = COEFF_B * a + COEFF_C * mm3(sa, sa)
        poly = jnp.where(eye, poly + COEFF_A, poly)
        sp = split(poly)
        if it < NS_ITERS - 1:
            a = mm3(split(mm3(sp, sa)), sp)
        q = poly if q is None else mm3(sp, split(q))
    pow_s[...] = q * (inv * factor)

    def apply(b, carry):
        x = split(mat_ref[b])
        w = split(pow_s[...])

        @pl.when(flipped)
        def _():
            upd_ref[b] = mm3(x, w)

        @pl.when(jnp.logical_not(flipped))
        def _():
            upd_ref[b] = mm3(w, x)

        return carry

    lax.fori_loop(0, nblk, apply, 0)


def ns_a_kernel(s_ref, mom, fx0, fx1, kept, gup, upd, grd, mat, pow_s, kf):
    me, core = s_ref[0], s_ref[1]
    count = 4
    half = fx0.shape[0]
    ndev = kept.shape[0] // KEPT_ROWS
    for j in range(3):
        kf[j] = kept[:, 128 * j : 128 * j + 128].astype(F32)

    def kept_rows(first):
        part = [kf[j, pl.ds(first, ndev, stride=KEPT_ROWS), :] for j in range(3)]
        return jnp.concatenate(part, axis=1).astype(BF16)

    for pair, target in (((0, 1), ADALN), ((2, 3), UP)):
        nb = MATS[target][1] // D
        first = MATS[target][2]

        @pl.when((me // 2) == pair[0] // 2)
        def _(target=target, nb=nb):
            if target == ADALN:
                sil = [kept_rows(12 + l) for l in range(2)]
                for b in range(nb):
                    acc = None
                    for l in range(2):
                        part = mm(sil[l], kept_rows(2 * b + l), 0, 0)
                        acc = part if acc is None else acc + part
                    grd[b] = acc
            else:
                for b in range(nb):
                    grd[b] = gup[b * D : (b + 1) * D, :].astype(F32)

        for t in pair:
            for _, block, r0, n, crow, frow, stride in [p for p in shard_pieces(t, count) if p[0] == target]:
                b = block - first

                @pl.when(me == t)
                def _(b=b, r0=r0, n=n, frow=frow, stride=stride):
                    for j in range(3):
                        cs = slice(128 * j, 128 * j + 128)
                        m = mom[pl.ds(frow + j, n, stride=stride), :]
                        mat[b, r0 : r0 + n, cs] = MOMENTUM_RATE * m + grd[b, r0 : r0 + n, cs]

                cuts = sorted({crow, crow + n} | {c for c in (half,) if crow < c < crow + n})
                for lo, hi in zip(cuts[:-1], cuts[1:]):
                    h = lo // half
                    for mine in (True, False):

                        @pl.when(jnp.logical_and(me == (t ^ 1), (core == h) if mine else (core != h)))
                        def _(b=b, r0=r0, lo=lo, hi=hi, h=h, crow=crow, mine=mine):
                            src = fx0 if mine else fx1
                            dst = slice(r0 + lo - crow, r0 + hi - crow)
                            m = src[lo - h * half : hi - h * half, :].astype(F32)
                            mat[b, dst, :] = MOMENTUM_RATE * m + grd[b, dst, :]

    low = me < 2
    nblk = jnp.where(low, 6, 4)
    factor = jnp.where(low, update_scale(ADALN), update_scale(UP))
    newton_schulz(mat, upd, pow_s, nblk, jnp.bool_(False), factor)


def ns_a(sidx, mom, fx0, fx1, kept, gup):
    sd = jax.ShapeDtypeStruct((6, D, D), F32)
    return pl.pallas_call(
        ns_a_kernel,
        out_shape=(sd, sd),
        in_specs=[sspec()] + [vspec()] * 5,
        out_specs=(vspec(), vspec()),
        scratch_shapes=[
            pltpu.VMEM((6, D, D), F32),
            pltpu.VMEM((D, D), F32),
            pltpu.VMEM((3, kept.shape[0], 128), F32),
        ],
        compiler_params=params_of(),
        cost_estimate=pl.CostEstimate(flops=12_000_000_000, bytes_accessed=12_000_000, transcendentals=0),
        name="ns_a",
    )(sidx, mom, fx0, fx1, kept, gup)


def final_kernel(s_ref, par, mom, g1, g2, upa, grda, ograd, onew, omom, upb, mat, pow_s):
    me = s_ref[0]
    count = 4
    grad_of = {QKV: (g2, 0), OUTW: (g1, 0), DOWN: (g1, 5 * D)}
    owner = {QKV: 1, OUTW: 2, DOWN: 3}
    for target, t in owner.items():
        first = MATS[target][2]
        ref, base = grad_of[target]
        for _, block, r0, n, crow, frow, stride in [p for p in shard_pieces(t, count) if p[0] == target]:
            b = block - first

            @pl.when(me == t)
            def _(b=b, r0=r0, n=n, frow=frow, stride=stride, ref=ref, base=base):
                for j in range(3):
                    cs = slice(128 * j, 128 * j + 128)
                    m = mom[pl.ds(frow + j, n, stride=stride), :]
                    g = ref[base + b * D + r0 : base + b * D + r0 + n, cs].astype(F32)
                    mat[b, r0 : r0 + n, cs] = MOMENTUM_RATE * m + g

    @pl.when(me > 0)
    def _():
        nblk = jnp.where(me == 1, 3, jnp.where(me == 2, 1, 4))
        factor = jnp.where(
            me == 1, update_scale(QKV), jnp.where(me == 2, update_scale(OUTW), update_scale(DOWN))
        )
        newton_schulz(mat, upb, pow_s, nblk, me == 3, factor)

    for t in range(count):

        @pl.when(me == t)
        def _(t=t):
            for mat_id, block, r0, n, crow, frow, stride in shard_pieces(t, count):
                b = block - MATS[mat_id][2]
                for j in range(3):
                    cs = slice(128 * j, 128 * j + 128)
                    fl = pl.ds(frow + j, n, stride=stride)
                    if mat_id in (ADALN, UP):
                        g = grda[b, r0 : r0 + n, cs]
                        u = upa[b, r0 : r0 + n, cs]
                    else:
                        ref, base = grad_of[mat_id]
                        g = ref[base + b * D + r0 : base + b * D + r0 + n, cs].astype(F32)
                        u = upb[b, r0 : r0 + n, cs]
                    ograd[fl, :] = g
                    omom[fl, :] = MOMENTUM_RATE * mom[fl, :] + g
                    onew[fl, :] = par[fl, :] - u


def final_call(sidx, par, mom, g1, g2, upa, grda):
    sd = jax.ShapeDtypeStruct(par.shape, F32)
    return pl.pallas_call(
        final_kernel,
        out_shape=(sd, sd, sd),
        in_specs=[sspec()] + [vspec()] * 6,
        out_specs=(vspec(),) * 3,
        scratch_shapes=[pltpu.VMEM((4, D, D), F32), pltpu.VMEM((4, D, D), F32), pltpu.VMEM((D, D), F32)],
        compiler_params=params_of(),
        cost_estimate=pl.CostEstimate(flops=12_000_000_000, bytes_accessed=24_000_000, transcendentals=0),
        name="finish",
    )(sidx, par, mom, g1, g2, upa, grda)


def swap(x, axis, mask):
    count = lax.axis_size(axis)
    return lax.ppermute(x, axis, [(i, i ^ mask) for i in range(count)])


def rows_at(x, start, n):
    return lax.dynamic_slice_in_dim(x, start, n, 0)


def all_rows(x):
    for axis, mask in (("rep", 1), ("rep", 2), ("rep", 4), ("fsdp", 1), ("fsdp", 2)):
        x = jnp.concatenate([x, swap(x, axis, mask)], axis=0)
    return x


def wide_sum(parts):
    total = None
    for p in parts:
        total = p.astype(F32) if total is None else total + p.astype(F32)
    return total


def plane_scatter(x, me):
    mine = lax.dynamic_index_in_dim(x, me, 0, keepdims=False)
    got = [swap(lax.dynamic_index_in_dim(x, me ^ m, 0, keepdims=False), "fsdp", m) for m in (1, 2, 3)]
    return wide_sum([mine] + got)


def core_sum(g, core):
    half = g.shape[0] // 2
    mine = rows_at(g, core * half, half)
    return mine + swap(rows_at(g, (1 - core) * half, half), "rep", 1)


def fast_device(tokens, conditions, assignment, params, momentum, cotangent):
    me = lax.axis_index("fsdp")
    rep = lax.axis_index("rep")
    core, zed = rep % 2, rep // 2
    lat = tokens.shape[0]
    rows = lat * SEQ
    par = params.reshape(-1, 128)
    mom = momentum.reshape(-1, 128)
    dev = me * lax.axis_size("rep") + rep
    pick = ((assignment // lat) ^ dev) * lat + assignment % lat
    sidx = jnp.concatenate([jnp.stack([me, core]), pick]).astype(jnp.int32)

    wc, mc = prep(sidx, par, mom, 4)
    half = wc.shape[0] // 2
    quarter = half // 2
    wh = rows_at(wc, core * half, half)
    rx, ry = swap(wh, "fsdp", 1), swap(wh, "fsdp", 2)
    table = all_rows(conditions)
    rda, rdb = swap(rx[:quarter], "fsdp", 2), swap(ry[quarter:], "fsdp", 1)
    px, py = swap(rx, "rep", 1), swap(ry, "rep", 1)
    pda, pdb = swap(rda, "rep", 1), swap(rdb, "rep", 1)
    bufs = (wc, rx, ry, rda, rdb, px, py, pda, pdb)

    tok2, cot2 = tokens.reshape(rows, D), cotangent.reshape(rows, D)
    (blend, qkv, probs, ai, gafter, gmx, mods, gmod1, silu, wqkv, g1) = main_call(
        sidx, table, tok2, cot2, bufs, True
    )
    fx0 = swap(rows_at(mc, core * half, half), "fsdp", 1)
    fx1 = swap(fx0, "rep", 1)

    h1 = core_sum(g1, core).astype(BF16)
    s1 = plane_scatter(h1.reshape(4, GRAD_ROWS // 8, D), me).astype(BF16)
    piece = s1.shape[0] // 4
    s1 = s1.reshape(4, piece, D)
    mine = lax.dynamic_index_in_dim(s1, zed, 0, keepdims=False)
    got = [
        swap(lax.dynamic_index_in_dim(s1, zed ^ m, 0, keepdims=False), "rep", 2 * m) for m in (1, 2, 3)
    ]
    zsum = wide_sum([mine] + got).astype(BF16)
    col = jnp.stack([zsum] + [swap(zsum, "rep", 2 * m) for m in (1, 2, 3)])
    plane = jnp.stack([col] + [swap(col, "fsdp", m) for m in (1, 2, 3)])
    both = jnp.stack([plane, swap(plane, "rep", 1)])

    gtok, g2, keep = heads_call(tok2, qkv, probs, ai, gafter, gmx, mods, gmod1, silu, wqkv)

    h2 = core_sum(g2, core).astype(BF16).reshape(4, 3 * D // 8, D)
    s2 = plane_scatter(h2, me).astype(BF16)
    k2 = jnp.concatenate([keep] + [swap(keep, "fsdp", m) for m in (1, 2, 3)], axis=0)
    msg = jnp.concatenate([s2, k2], axis=0)
    z1, z2, z3 = (swap(msg, "rep", 2 * m) for m in (1, 2, 3))
    ns = s2.shape[0]
    q2 = (wide_sum([s2, z1[:ns]]) + wide_sum([z2[:ns], z3[:ns]])).astype(BF16)
    kz = jnp.concatenate([k2, z1[ns:], z2[ns:], z3[ns:]], axis=0)
    kept = jnp.concatenate([kz, swap(kz, "rep", 1)], axis=0)
    p2 = jnp.stack([q2] + [swap(q2, "fsdp", m) for m in (1, 2, 3)])
    both2 = jnp.stack([p2, swap(p2, "rep", 1)])

    bits = jnp.arange(2)
    quad = jnp.arange(4)
    g1full = both[bits ^ core][:, quad ^ me][:, :, quad ^ zed].reshape(GRAD_ROWS, D)
    g2full = both2[bits ^ core][:, quad ^ me].reshape(3 * D, D)
    upa, grda = ns_a(sidx, mom, fx0, fx1, kept, g1full[D : 5 * D])
    ograd, onew, omom = final_call(sidx, par, mom, g1full, g2full, upa, grda)
    shape = tokens.shape
    return (
        blend.reshape(shape),
        gtok.reshape(shape),
        ograd.reshape(-1),
        onew.reshape(-1),
        omom.reshape(-1),
    )


def unpack(flat):
    pieces, offset = [], 0
    for rows_count, cols_count, _, _ in MATS:
        pieces.append(flat[offset : offset + rows_count * cols_count].reshape(rows_count, cols_count))
        offset += rows_count * cols_count
    return pieces


def to_blocks(mats):
    out = []
    for matrix, (rows_count, cols_count, _, by_cols) in zip(mats, MATS):
        if by_cols:
            out.append(matrix.reshape(D, cols_count // D, D).transpose(1, 0, 2))
        else:
            out.append(matrix.reshape(rows_count // D, D, D))
    return jnp.concatenate(out, axis=0)


def from_blocks(blocks, by_cols):
    if by_cols:
        return blocks.transpose(1, 0, 2).reshape(-1)
    return blocks.reshape(-1)


def orthogonalize(matrix):
    flipped = matrix.shape[0] > matrix.shape[1]
    current = matrix.T if flipped else matrix
    current = current / (jnp.sqrt(jnp.sum(current * current)) + 1e-07)
    for _ in range(NS_ITERS):
        square = jnp.dot(current, current.T, precision=lax.Precision.HIGHEST)
        polynomial = COEFF_B * square + COEFF_C * jnp.dot(square, square, precision=lax.Precision.HIGHEST)
        current = COEFF_A * current + jnp.dot(polynomial, current, precision=lax.Precision.HIGHEST)
    return current.T if flipped else current


def scaled_update(matrix, factor):
    return (factor * orthogonalize(matrix)).reshape(-1)


def empty_update(matrix, factor):
    return jnp.zeros((matrix.shape[0] * matrix.shape[1],), F32)


def any_device(tokens, conditions, assignment, params, momentum, cotangent):
    lat = tokens.shape[0]
    rows = lat * SEQ
    table = lax.all_gather(conditions, ("fsdp", "rep"), axis=0, tiled=True)
    gathered = lax.all_gather(params.astype(BF16), "fsdp", axis=0, tiled=True)
    blocks = to_blocks(unpack(gathered))
    me = lax.axis_index("fsdp")
    sidx = jnp.concatenate([jnp.stack([me, me]), assignment]).astype(jnp.int32)
    tok2, cot2 = tokens.reshape(rows, D), cotangent.reshape(rows, D)
    (blend, qkv, probs, ai, gafter, gmx, mods, gmod1, silu, wqkv, g1) = main_call(
        sidx, table, tok2, cot2, (blocks,), False
    )
    gtok, g2, keep = heads_call(tok2, qkv, probs, ai, gafter, gmx, mods, gmod1, silu, wqkv)
    rest = jnp.concatenate(
        [
            from_blocks(g2.reshape(3, D, D), True),
            g1[:D].reshape(-1),
            from_blocks(g1[D : 5 * D].reshape(4, D, D), True),
            g1[5 * D : 9 * D].reshape(-1),
        ]
    )
    kept = lax.all_gather(keep, ("fsdp", "rep"), axis=0, tiled=True).reshape(-1, KEPT_ROWS, D)
    silu_all = kept[:, 6 * lat : 7 * lat].reshape(-1, D)
    mod_all = kept[:, : 6 * lat].reshape(-1, 6, lat, D).transpose(0, 2, 1, 3).reshape(-1, 6 * D)
    adaln = lax.dot_general(silu_all, mod_all, (((0,), (0,)), ((), ())), preferred_element_type=F32)
    shard_len = params.shape[0]
    head = jnp.concatenate([adaln.reshape(-1), jnp.zeros_like(rest)])
    flat = jnp.concatenate([jnp.zeros((D * 6 * D,), F32), rest])
    part = lax.psum_scatter(flat, "fsdp", scatter_dimension=0, tiled=True)
    full_grad = lax.psum(part, "rep") + lax.dynamic_slice_in_dim(head, me * shard_len, shard_len, 0)
    new_momentum = MOMENTUM_RATE * momentum + full_grad
    whole_mom = lax.all_gather(new_momentum, "fsdp", axis=0, tiled=True)
    group_size = lax.axis_size("fsdp")
    updates, offset = [], 0
    for mat, piece in enumerate(unpack(whole_mom)):
        factor = F32(update_scale(mat))
        owner = (offset // shard_len + group_size // 2) % group_size
        updates.append(lax.cond(me == owner, scaled_update, empty_update, piece, factor))
        offset += piece.size
    update = lax.psum_scatter(jnp.concatenate(updates), "fsdp", scatter_dimension=0, tiled=True)
    shape = tokens.shape
    return (blend.reshape(shape), gtok.reshape(shape), full_grad, params - update, new_momentum)


def solution(mesh):
    both = ("fsdp", "rep")
    in_specs = (P(both, None, None), P(both, None), P(both), P("fsdp"), P("fsdp"), P(both, None, None))
    out_specs = (P(both, None, None), P(both, None, None), P("fsdp"), P("fsdp"), P("fsdp"))
    small = dict(mesh.shape) == {"fsdp": 4, "rep": 8}
    return jax.shard_map(
        fast_device if small else any_device,
        mesh=mesh,
        in_specs=in_specs,
        out_specs=out_specs,
        check_vma=False,
    )
```

```python
import functools
import math

import jax
import jax.numpy as jnp
from jax import lax
from jax.experimental import pallas as pl
from jax.experimental.pallas import tpu as pltpu
from jax.sharding import PartitionSpec as P

D = 384
HEADS = 6
HD = 64
FF = 1536
SEQ = 256
NS_ITERS = 3

LN_EPSILON = 1e-06
MOMENTUM_RATE = 0.95
LEARN_RATE = 0.2
COEFF_A = 3.4445
COEFF_B = -4.775
COEFF_C = 2.0315

F32 = jnp.float32
BF16 = jnp.bfloat16
ANY = pl.ANY
VMEM_LIMIT = 60 * 1024 * 1024

MATS = ((D, 6 * D, 0, True), (D, 3 * D, 6, True), (D, D, 9, True), (D, FF, 10, True), (FF, D, 14, False))
NBLOCKS = 18
ADALN, QKV, OUTW, UP, DOWN = range(5)
P_SIZE = sum(m[0] * m[1] for m in MATS)
GRAD_ROWS = 3584
KEPT_ROWS = 16


def update_scale(mat):
    return LEARN_RATE * 0.2 * math.sqrt(max(MATS[mat][0], MATS[mat][1]))


def shard_pieces(shard, count):
    size = P_SIZE // count
    begin, end = shard * size, (shard + 1) * size
    pieces, crow, offset = [], 0, 0
    for mat, (rows, cols, first, by_cols) in enumerate(MATS):
        lo, hi = max(begin, offset), min(end, offset + rows * cols)
        if lo < hi:
            r0, r1 = (lo - offset) // cols, (hi - offset) // cols
            stride = cols // 128
            base = (offset - begin) // 128
            if by_cols:
                for b in range(cols // D):
                    pieces.append((mat, first + b, r0, r1 - r0, crow, base + r0 * stride + 3 * b, stride))
                    crow += r1 - r0
            else:
                r = r0
                while r < r1:
                    n = min(r1, (r // D + 1) * D) - r
                    pieces.append((mat, first + r // D, r % D, n, crow, base + r * stride, stride))
                    crow += n
                    r += n
        offset += rows * cols
    return pieces


def mm(a, b, ca=1, cb=0):
    return lax.dot_general(a, b, (((ca,), (cb,)), ((), ())), preferred_element_type=F32)


def vspec():
    return pl.BlockSpec(memory_space=pltpu.VMEM)


def aspec():
    return pl.BlockSpec(memory_space=ANY)


def sspec():
    return pl.BlockSpec(memory_space=pltpu.SMEM)


def params_of(**kw):
    return pltpu.CompilerParams(vmem_limit_bytes=VMEM_LIMIT, **kw)


def prep_kernel(count, s_ref, p_ref, m_ref, w_ref, mo_ref):
    for shard in range(count):

        @pl.when(s_ref[0] == shard)
        def _(shard=shard):
            for _, _, _, n, crow, frow, stride in shard_pieces(shard, count):
                for j in range(3):
                    src = pl.ds(frow + j, n, stride=stride)
                    w_ref[crow : crow + n, 128 * j : 128 * j + 128] = p_ref[src, :].astype(BF16)
                    mo_ref[crow : crow + n, 128 * j : 128 * j + 128] = m_ref[src, :].astype(BF16)


def prep(sidx, params, momentum, count):
    rows = P_SIZE // count // D
    out = jax.ShapeDtypeStruct((rows, D), BF16)
    return pl.pallas_call(
        functools.partial(prep_kernel, count),
        out_shape=(out, out),
        in_specs=[sspec(), vspec(), vspec()],
        out_specs=(vspec(), vspec()),
        compiler_params=params_of(),
        name="prep",
    )(sidx, params, momentum)


def layer_norm(h):
    center = jnp.mean(h, axis=-1, keepdims=True)
    cent = h - center
    spread = jnp.mean(jnp.square(cent), axis=-1, keepdims=True)
    rstd = lax.rsqrt(spread + LN_EPSILON)
    return cent * rstd, rstd


def layer_norm_grad(xhat, rstd, gx):
    m1 = jnp.mean(gx, axis=-1, keepdims=True)
    m2 = jnp.mean(gx * xhat, axis=-1, keepdims=True)
    return rstd * (gx - m1 - xhat * m2)


def gather_plan(count):
    plan = []
    half = P_SIZE // count // D // 2
    for shard in range(count):
        for _, block, r0, n, crow, _, _ in shard_pieces(shard, count):
            cuts = sorted({crow, crow + n} | {c for c in range(0, 2 * half + 1, half // 2) if crow < c < crow + n})
            for a, b in zip(cuts[:-1], cuts[1:]):
                plan.append((shard, a // half, a % half, b - a, block, r0 + a - crow))
    return plan


def load_weights_fast(s_ref, bufs, wts, sems, start):
    own, rx, ry, rda, rdb, px, py, pda, pdb = bufs
    me, core = s_ref[0], s_ref[1]
    half = own.shape[0] // 2
    quarter = half // 2
    for q, (shard, h, r, n, block, br) in enumerate(gather_plan(4)):
        dst = wts.at[block, br : br + n]
        if not start:
            pltpu.make_async_copy(own.at[0:n], dst, sems.at[q]).wait()
            continue
        for m in range(4):
            for mine in (True, False):
                if m == 0 and not mine:
                    continue
                cond = me == (shard ^ m)
                if m > 0:
                    cond = jnp.logical_and(cond, (core == h) if mine else (core != h))
                if m == 0:
                    src = own.at[h * half + r : h * half + r + n]
                elif m < 3:
                    src = ((rx, ry) if mine else (px, py))[m - 1].at[r : r + n]
                else:
                    pair = (rda, rdb) if mine else (pda, pdb)
                    k = r // quarter
                    src = pair[k].at[r - k * quarter : r - k * quarter + n]

                @pl.when(cond)
                def _(src=src, dst=dst, q=q):
                    pltpu.make_async_copy(src, dst, sems.at[q]).start()


def main_kernel(nbuf, fast, rows, s_ref, table, tok, cot, *refs):
    bufs = refs[:nbuf]
    (blend, qkv, probs, amix_in, gafter, gmx, mods, gmod, silu, wqkv, grads) = refs[nbuf : nbuf + 11]
    wts, ao_s, aa_s, amix, minp, gmi, mo, sems = refs[nbuf + 11 :]
    lat = rows // SEQ
    if fast:
        load_weights_fast(s_ref, bufs, wts, sems, True)
    else:
        whole = pltpu.make_async_copy(bufs[0], wts, sems.at[0])
        whole.start()
    nt = table.shape[0]
    lanes = lax.broadcasted_iota(jnp.int32, (16, nt), 1)
    rws = lax.broadcasted_iota(jnp.int32, (16, nt), 0)
    pick = jnp.zeros((16, nt), jnp.bool_)
    for l in range(lat):
        pick = pick | ((rws == l) & (lanes == s_ref[3 + l]))
    cond = mm(pick.astype(F32).astype(BF16), table[...])
    sc = (cond * (1.0 / (1.0 + jnp.exp(-cond)))).astype(BF16)
    silu[...] = sc.astype(F32)
    if fast:
        load_weights_fast(s_ref, bufs, wts, sems, False)
    else:
        whole.wait()
    for b in range(6):
        mods[b] = mm(sc, wts[b])[:8]
    for j in range(3):
        wqkv[j] = wts[6 + j]
    grads[9 * D :, :] = jnp.zeros((GRAD_ROWS - 9 * D, D), F32)

    def mod(b, l):
        return mods[b, l : l + 1, :]

    for l in range(lat):
        rs = slice(l * SEQ, (l + 1) * SEQ)
        xhat, _ = layer_norm(tok[rs, :].astype(F32))
        amix_in[rs, :] = (xhat * (1.0 + mod(1, l)) + mod(0, l)).astype(BF16)
    ai = amix_in[...]
    for j in range(3):
        qkv[j] = mm(ai, wts[6 + j]).astype(BF16)

    low = lax.broadcasted_iota(jnp.int32, (SEQ, 128), 1) < HD
    zero = jnp.zeros((SEQ, 128), BF16)

    def attend(l, carry):
        rs = pl.ds(pl.multiple_of(l * SEQ, SEQ), SEQ)
        for hp in range(HEADS // 2):
            cs = slice(hp * 128, hp * 128 + 128)
            q, k, v = qkv[0, rs, cs], qkv[1, rs, cs], qkv[2, rs, cs]
            outs = []
            for h in range(2):
                qm = jnp.where(low if h == 0 else jnp.logical_not(low), q, zero)
                s = mm(qm, k, 1, 1) * HD ** (-0.5)
                top = jnp.max(s, axis=-1, keepdims=True)
                e = jnp.exp(s - top)
                pr = e * (1.0 / jnp.sum(e, axis=-1, keepdims=True))
                probs[l * HEADS + hp * 2 + h] = pr
                outs.append(mm(pr.astype(BF16), v))
            amix[rs, cs] = jnp.where(low, outs[0], outs[1]).astype(BF16)
        return carry

    lax.fori_loop(0, lat, attend, 0)

    ao = mm(amix[...], wts[9])
    ao_s[...] = ao
    for l in range(lat):
        rs = slice(l * SEQ, (l + 1) * SEQ)
        aa = tok[rs, :].astype(F32) + mod(2, l) * ao_s[rs, :]
        aa_s[rs, :] = aa
        xhat, _ = layer_norm(aa)
        minp[rs, :] = (xhat * (1.0 + mod(4, l)) + mod(3, l)).astype(BF16)
        gmx[rs, :] = (cot[rs, :].astype(F32) * mod(5, l)).astype(BF16)
    gmi[...] = jnp.zeros_like(gmi)
    mo[...] = jnp.zeros_like(mo)

    def mlp(j, carry):
        wu, wd = wts[10 + j], wts[14 + j]
        u = mm(minp[...], wu)
        c = math.sqrt(2.0 / math.pi)
        u2 = u * u
        t = jnp.tanh(c * (u + 0.044715 * (u2 * u)))
        half = 0.5 * (1.0 + t)
        act = (u * half).astype(BF16)
        slope = half + 0.5 * u * (1.0 - t * t) * (c * (1.0 + 3.0 * 0.044715 * u2))
        mo[...] += mm(act, wd)
        gmo = gmx[...]
        gp = (mm(gmo, wd, 1, 1) * slope).astype(BF16)
        grads[pl.ds(pl.multiple_of((5 + j) * D, D), D), :] = mm(act, gmo, 0, 0)
        grads[pl.ds(pl.multiple_of((1 + j) * D, D), D), :] = mm(minp[...], gp, 0, 0)
        gmi[...] += mm(gp, wu, 1, 1)
        return carry

    lax.fori_loop(0, FF // D, mlp, 0)

    gmod[...] = jnp.zeros_like(gmod)
    for l in range(lat):
        rs = slice(l * SEQ, (l + 1) * SEQ)
        up = cot[rs, :].astype(F32)
        blend[rs, :] = (aa_s[rs, :] + mod(5, l) * mo[rs, :]).astype(BF16)
        gmod[5, l : l + 1, :] = jnp.sum(up * mo[rs, :], axis=0, keepdims=True)
        xhat, rstd = layer_norm(aa_s[rs, :])
        g = gmi[rs, :]
        gmod[3, l : l + 1, :] = jnp.sum(g, axis=0, keepdims=True)
        gmod[4, l : l + 1, :] = jnp.sum(g * xhat, axis=0, keepdims=True)
        ga = up + layer_norm_grad(xhat, rstd, g * (1.0 + mod(4, l)))
        gafter[rs, :] = ga
        gmod[2, l : l + 1, :] = jnp.sum(ga * ao_s[rs, :], axis=0, keepdims=True)
        minp[rs, :] = (ga * mod(2, l)).astype(BF16)
    gao = minp[...]
    grads[0:D, :] = mm(amix[...], gao, 0, 0)
    gmx[...] = mm(gao, wts[9], 1, 1).astype(BF16)


def main_call(sidx, table, tokens, cotangent, bufs, fast):
    rows = tokens.shape[0]
    lat = rows // SEQ
    sd = jax.ShapeDtypeStruct
    outs = (
        sd((rows, D), BF16),
        sd((3, rows, D), BF16),
        sd((lat * HEADS, SEQ, SEQ), F32),
        sd((rows, D), BF16),
        sd((rows, D), F32),
        sd((rows, D), BF16),
        sd((6, 8, D), F32),
        sd((6, 8, D), F32),
        sd((16, D), F32),
        sd((3, D, D), BF16),
        sd((GRAD_ROWS, D), F32),
    )
    nsem = len(gather_plan(4)) if fast else 1
    return pl.pallas_call(
        functools.partial(main_kernel, len(bufs), fast, rows),
        out_shape=outs,
        in_specs=[sspec(), vspec(), vspec(), vspec()] + [aspec()] * len(bufs),
        out_specs=(vspec(),) * len(outs),
        scratch_shapes=[
            pltpu.VMEM((NBLOCKS, D, D), BF16),
            pltpu.VMEM((rows, D), F32),
            pltpu.VMEM((rows, D), F32),
            pltpu.VMEM((rows, D), BF16),
            pltpu.VMEM((rows, D), BF16),
            pltpu.VMEM((rows, D), F32),
            pltpu.VMEM((rows, D), F32),
            pltpu.SemaphoreType.DMA((nsem,)),
        ],
        compiler_params=params_of(),
        cost_estimate=pl.CostEstimate(flops=20_000_000_000, bytes_accessed=30_000_000, transcendentals=0),
        name="main",
    )(sidx, table, tokens, cotangent, *bufs)


def heads_kernel(rows, tok, qkv, probs, ai, gafter, gmx, mods, gmod1, silu, wqkv, gtok, gq, keep, gqkv, srow):
    lat = rows // SEQ
    low = lax.broadcasted_iota(jnp.int32, (SEQ, 128), 1) < HD
    zero = jnp.zeros((SEQ, 128), BF16)

    def back(l, carry):
        rs = pl.ds(pl.multiple_of(l * SEQ, SEQ), SEQ)
        for hp in range(HEADS // 2):
            cs = slice(hp * 128, hp * 128 + 128)
            q, k, v = qkv[0, rs, cs], qkv[1, rs, cs], qkv[2, rs, cs]
            g = gmx[rs, cs]
            res = []
            for h in range(2):
                p = probs[l * HEADS + hp * 2 + h]
                gm = jnp.where(low if h == 0 else jnp.logical_not(low), g, zero)
                gv = mm(p.astype(BF16), g, 0, 0)
                gpr = mm(gm, v, 1, 1)
                dots = jnp.sum(p * gpr, axis=-1, keepdims=True)
                gs = (p * (gpr - dots) * HD ** (-0.5)).astype(BF16)
                res.append((mm(gs, k), mm(gs, q, 0, 0), gv))
            for j in range(3):
                gqkv[j, rs, cs] = jnp.where(low, res[0][j], res[1][j]).astype(BF16)
        return carry

    lax.fori_loop(0, lat, back, 0)
    gai = None
    for j in range(3):
        part = mm(gqkv[j], wqkv[j], 1, 1)
        gai = part if gai is None else gai + part
        gq[j * D : (j + 1) * D, :] = mm(ai[...], gqkv[j], 0, 0)
    srow[...] = jnp.zeros_like(srow)
    for l in range(lat):
        rs = slice(l * SEQ, (l + 1) * SEQ)
        xhat, rstd = layer_norm(tok[rs, :].astype(F32))
        g = gai[rs, :]
        srow[l : l + 1, :] = jnp.sum(g, axis=0, keepdims=True)
        srow[lat + l : lat + l + 1, :] = jnp.sum(g * xhat, axis=0, keepdims=True)
        gtok[rs, :] = gafter[rs, :] + layer_norm_grad(xhat, rstd, g * (1.0 + mods[1, l : l + 1, :]))
        for b in range(2, 6):
            srow[lat * b + l : lat * b + l + 1, :] = gmod1[b, l : l + 1, :]
        srow[lat * 6 + l : lat * 6 + l + 1, :] = silu[l : l + 1, :]
    keep[...] = srow[...].astype(BF16)


def heads_call(tokens, qkv, probs, ai, gafter, gmx, mods, gmod1, silu, wqkv):
    rows = tokens.shape[0]
    sd = jax.ShapeDtypeStruct
    outs = (sd((rows, D), F32), sd((3 * D, D), F32), sd((KEPT_ROWS, D), BF16))
    return pl.pallas_call(
        functools.partial(heads_kernel, rows),
        out_shape=outs,
        in_specs=[vspec()] * 10,
        out_specs=(vspec(),) * 3,
        scratch_shapes=[pltpu.VMEM((3, rows, D), BF16), pltpu.VMEM((KEPT_ROWS, D), F32)],
        compiler_params=params_of(),
        cost_estimate=pl.CostEstimate(flops=12_000_000_000, bytes_accessed=12_000_000, transcendentals=0),
        name="heads",
    )(tokens, qkv, probs, ai, gafter, gmx, mods, gmod1, silu, wqkv)


def split(x):
    hi = x.astype(BF16)
    return hi, (x - hi.astype(F32)).astype(BF16)


POLY = (COEFF_C, COEFF_B, COEFF_A)
PLAIN = (1.0, 0.0, 0.0)
STEPS = (
    (0, 0, 2, POLY),
    (2, 0, 3, PLAIN),
    (3, 2, 0, PLAIN),
    (0, 0, 1, POLY),
    (1, 2, 2, PLAIN),
    (1, 0, 3, PLAIN),
    (3, 1, 0, PLAIN),
    (0, 0, 1, POLY),
    (1, 2, 2, PLAIN),
)


def step_tables():
    ints = jnp.array([x for st in STEPS for x in st[:3]], jnp.int32)
    coeffs = jnp.array([x for st in STEPS for x in st[3]], F32)
    return ints, coeffs


def newton_schulz(ints, coeffs, mat_ref, upd_ref, bufs, npairs, flipped, factor):
    bufs[0] = jnp.zeros((D, D), F32)

    def gram(b, carry):
        x0, x1 = mat_ref[2 * b].astype(BF16), mat_ref[2 * b + 1].astype(BF16)

        @pl.when(flipped)
        def _():
            x = jnp.concatenate([x0, x1], axis=0)
            bufs[0] += mm(x, x, 0, 0)

        @pl.when(jnp.logical_not(flipped))
        def _():
            x = jnp.concatenate([x0, x1], axis=1)
            bufs[0] += mm(x, x, 1, 1)

        return carry

    lax.fori_loop(0, npairs, gram, 0)
    g = bufs[0]
    ri = lax.broadcasted_iota(jnp.int32, (D, D), 0)
    ci = lax.broadcasted_iota(jnp.int32, (D, D), 1)
    eye = jnp.where(ri == ci, 1.0, 0.0)
    diag = jnp.sum(g * eye, axis=1, keepdims=True)
    total = jnp.sum(diag, axis=0, keepdims=True)
    inv = 1.0 / (jnp.sqrt(total) + 1e-07)
    bufs[0] = g * (inv * inv)

    def step(k, carry):
        i, j, d = ints[3 * k], ints[3 * k + 1], ints[3 * k + 2]
        x = bufs[i]
        xh, xl = split(x)
        yh, yl = split(bufs[j])
        prod = mm(jnp.concatenate([xh, xl, xh], axis=1), jnp.concatenate([yh, yh, yl], axis=0))
        r0 = lax.broadcasted_iota(jnp.int32, (D, D), 0)
        r1 = lax.broadcasted_iota(jnp.int32, (D, D), 1)
        ident = jnp.where(r0 == r1, coeffs[3 * k + 2], 0.0)
        bufs[d] = coeffs[3 * k] * prod + (coeffs[3 * k + 1] * x + ident)
        return carry

    lax.fori_loop(0, len(STEPS), step, 0)
    bufs[0] = bufs[2] * (inv * factor)

    def apply(b, carry):
        wh, wl = split(bufs[0])
        xs = [mat_ref[2 * b + i] for i in range(2)]

        @pl.when(flipped)
        def _():
            for i in range(2):
                xh, xl = split(xs[i])
                upd_ref[2 * b + i] = mm(
                    jnp.concatenate([xh, xl, xh], axis=1), jnp.concatenate([wh, wh, wl], axis=0)
                )

        @pl.when(jnp.logical_not(flipped))
        def _():
            (h0, l0), (h1, l1) = split(xs[0]), split(xs[1])
            xh = jnp.concatenate([h0, h1], axis=1)
            xl = jnp.concatenate([l0, l1], axis=1)
            out = mm(jnp.concatenate([wh, wl, wh], axis=1), jnp.concatenate([xh, xh, xl], axis=0))
            upd_ref[2 * b] = out[:, :D]
            upd_ref[2 * b + 1] = out[:, D:]

        return carry

    lax.fori_loop(0, npairs, apply, 0)


def first_chunks():
    for q in range(32):
        size = GRAD_ROWS // 32
        row = q * size
        while row < min((q + 1) * size, 9 * D):
            n = min((q + 1) * size, (row // D + 1) * D) - row
            yield (q // 16, q // 4 % 4, q % 4), row // D, row % D, n, row - q * size
            row += n


def take_first(s_ref, chunks, dst, first, count):
    me, core, zed = s_ref[0], s_ref[1], s_ref[2]
    for (c, m, z), block, row, n, crow in first_chunks():
        if first <= block < first + count:
            piece = chunks[core ^ c, me ^ m, zed ^ z, crow : crow + n, :]
            dst[block - first, row : row + n, :] = piece.astype(F32)


def take_second(s_ref, chunks, dst):
    me, core = s_ref[0], s_ref[1]
    size = 3 * D // 8
    for q in range(8):
        row = q * size
        while row < (q + 1) * size:
            n = min((q + 1) * size, (row // D + 1) * D) - row
            piece = chunks[core ^ (q // 4), me ^ (q % 4), row - q * size : row - q * size + n, :]
            dst[row // D, row % D : row % D + n, :] = piece.astype(F32)
            row += n


def ns_a_kernel(s_ref, ints, coeffs, mom, fx0, fx1, kept, chunks, upd, grd, mat, bufs, kf):
    me, core = s_ref[0], s_ref[1]
    half = fx0.shape[0]
    ndev = kept.shape[0] // KEPT_ROWS

    def kept_rows(first):
        part = [kf[j, pl.ds(first, ndev, stride=KEPT_ROWS), :] for j in range(3)]
        return jnp.concatenate(part, axis=1).astype(BF16)

    for pair, target in (((0, 1), ADALN), ((2, 3), UP)):
        nb = MATS[target][1] // D
        first = MATS[target][2]

        @pl.when((me // 2) == pair[0] // 2)
        def _(target=target, nb=nb):
            if target == ADALN:
                for j in range(3):
                    kf[j] = kept[:, 128 * j : 128 * j + 128].astype(F32)
                sil = jnp.concatenate([kept_rows(12), kept_rows(13)], axis=0)
                for b in range(nb):
                    gm = jnp.concatenate([kept_rows(2 * b), kept_rows(2 * b + 1)], axis=0)
                    grd[b] = mm(sil, gm, 0, 0)
            else:
                take_first(s_ref, chunks, grd, 1, nb)

        for t in pair:
            for _, block, r0, n, crow, frow, stride in [p for p in shard_pieces(t, 4) if p[0] == target]:
                b = block - first

                @pl.when(me == t)
                def _(b=b, r0=r0, n=n, frow=frow, stride=stride):
                    for j in range(3):
                        cs = slice(128 * j, 128 * j + 128)
                        m = mom[pl.ds(frow + j, n, stride=stride), :]
                        mat[b, r0 : r0 + n, cs] = MOMENTUM_RATE * m + grd[b, r0 : r0 + n, cs]

                cuts = sorted({crow, crow + n} | {c for c in (half,) if crow < c < crow + n})
                for lo, hi in zip(cuts[:-1], cuts[1:]):
                    h = lo // half
                    for mine in (True, False):

                        @pl.when(jnp.logical_and(me == (t ^ 1), (core == h) if mine else (core != h)))
                        def _(b=b, r0=r0, lo=lo, hi=hi, h=h, crow=crow, mine=mine):
                            src = fx0 if mine else fx1
                            dst = slice(r0 + lo - crow, r0 + hi - crow)
                            m = src[lo - h * half : hi - h * half, :].astype(F32)
                            mat[b, dst, :] = MOMENTUM_RATE * m + grd[b, dst, :]

    low = me < 2
    npairs = jnp.where(low, 3, 2)
    factor = jnp.where(low, update_scale(ADALN), update_scale(UP))
    newton_schulz(ints, coeffs, mat, upd, bufs, npairs, jnp.bool_(False), factor)


def ns_a(sidx, tables, mom, fx0, fx1, kept, chunks):
    sd = jax.ShapeDtypeStruct((6, D, D), F32)
    return pl.pallas_call(
        ns_a_kernel,
        out_shape=(sd, sd),
        in_specs=[sspec()] * 3 + [vspec()] * 5,
        out_specs=(vspec(), vspec()),
        scratch_shapes=[
            pltpu.VMEM((6, D, D), F32),
            pltpu.VMEM((4, D, D), F32),
            pltpu.VMEM((3, kept.shape[0], 128), F32),
        ],
        compiler_params=params_of(),
        cost_estimate=pl.CostEstimate(flops=8_000_000_000, bytes_accessed=12_000_000, transcendentals=0),
        name="ns_a",
    )(sidx, *tables, mom, fx0, fx1, kept, chunks)


OWNER = ((QKV, 1, 2), (OUTW, 2, 1), (DOWN, 3, 2))


def final_kernel(
    s_ref, ints, coeffs, par, mom, chunks, chunks2, upa, grda, ograd, onew, omom, upb, gb, mat, bufs
):
    me = s_ref[0]
    for target, t, npairs in OWNER:

        @pl.when(me == t)
        def _(target=target, t=t, npairs=npairs):
            first = MATS[target][2]
            count = MATS[target][0] * MATS[target][1] // (D * D)
            if target == QKV:
                take_second(s_ref, chunks2, gb)
            else:
                take_first(s_ref, chunks, gb, first - 9 if target == OUTW else 5, count)
            for b in range(count, 2 * npairs):
                mat[b] = jnp.zeros((D, D), F32)
            for _, block, r0, n, crow, frow, stride in [p for p in shard_pieces(t, 4) if p[0] == target]:
                b = block - first
                for j in range(3):
                    cs = slice(128 * j, 128 * j + 128)
                    m = mom[pl.ds(frow + j, n, stride=stride), :]
                    mat[b, r0 : r0 + n, cs] = MOMENTUM_RATE * m + gb[b, r0 : r0 + n, cs]

    @pl.when(me > 0)
    def _():
        npairs = jnp.where(me == 2, 1, 2)
        factor = jnp.where(
            me == 1, update_scale(QKV), jnp.where(me == 2, update_scale(OUTW), update_scale(DOWN))
        )
        newton_schulz(ints, coeffs, mat, upb, bufs, npairs, me == 3, factor)

    for t in range(4):

        @pl.when(me == t)
        def _(t=t):
            for mat_id, block, r0, n, crow, frow, stride in shard_pieces(t, 4):
                b = block - MATS[mat_id][2]
                gref, uref = (grda, upa) if mat_id in (ADALN, UP) else (gb, upb)
                for j in range(3):
                    cs = slice(128 * j, 128 * j + 128)
                    fl = pl.ds(frow + j, n, stride=stride)
                    g = gref[b, r0 : r0 + n, cs]
                    ograd[fl, :] = g
                    omom[fl, :] = MOMENTUM_RATE * mom[fl, :] + g
                    onew[fl, :] = par[fl, :] - uref[b, r0 : r0 + n, cs]


def final_call(sidx, tables, par, mom, chunks, chunks2, upa, grda):
    sd = jax.ShapeDtypeStruct(par.shape, F32)
    block4 = pltpu.VMEM((4, D, D), F32)
    return pl.pallas_call(
        final_kernel,
        out_shape=(sd, sd, sd),
        in_specs=[sspec()] * 3 + [vspec()] * 6,
        out_specs=(vspec(),) * 3,
        scratch_shapes=[block4, block4, block4, block4],
        compiler_params=params_of(),
        cost_estimate=pl.CostEstimate(flops=8_000_000_000, bytes_accessed=24_000_000, transcendentals=0),
        name="finish",
    )(sidx, *tables, par, mom, chunks, chunks2, upa, grda)


def swap(x, axis, mask):
    count = lax.axis_size(axis)
    return lax.ppermute(x, axis, [(i, i ^ mask) for i in range(count)])


def rows_at(x, start, n):
    return lax.dynamic_slice_in_dim(x, start, n, 0)


def more_rows(x, hops):
    for axis, mask in hops:
        x = jnp.concatenate([x, swap(x, axis, mask)], axis=0)
    return x


def wide_sum(parts):
    total = None
    for p in parts:
        total = p.astype(F32) if total is None else total + p.astype(F32)
    return total


def plane_scatter(x, me):
    mine = lax.dynamic_index_in_dim(x, me, 0, keepdims=False)
    got = [swap(lax.dynamic_index_in_dim(x, me ^ m, 0, keepdims=False), "fsdp", m) for m in (1, 2, 3)]
    return wide_sum([mine] + got)


def core_sum(g, core):
    half = g.shape[0] // 2
    mine = rows_at(g, core * half, half)
    return mine + swap(rows_at(g, (1 - core) * half, half), "rep", 1)


def fast_device(tokens, conditions, assignment, params, momentum, cotangent):
    me = lax.axis_index("fsdp")
    rep = lax.axis_index("rep")
    core, zed = rep % 2, rep // 2
    lat = tokens.shape[0]
    rows = lat * SEQ
    par = params.reshape(-1, 128)
    mom = momentum.reshape(-1, 128)
    dev = me * lax.axis_size("rep") + rep
    pick = ((assignment // lat) ^ dev) * lat + assignment % lat
    sidx = jnp.concatenate([jnp.stack([me, core, zed]), pick]).astype(jnp.int32)

    wc, mc = prep(sidx, par, mom, 4)
    half = wc.shape[0] // 2
    quarter = half // 2
    wh = rows_at(wc, core * half, half)
    conditions, wh = lax.optimization_barrier((conditions, wh))
    rx, ry = swap(wh, "fsdp", 1), swap(wh, "fsdp", 2)
    table = more_rows(conditions, (("rep", 1), ("rep", 2), ("rep", 4)))
    rx, ry, table = lax.optimization_barrier((rx, ry, table))
    table = more_rows(table, (("fsdp", 1), ("fsdp", 2)))
    rda, rdb = swap(rx[:quarter], "fsdp", 2), swap(ry[quarter:], "fsdp", 1)
    px, py = swap(rx, "rep", 1), swap(ry, "rep", 1)
    pda, pdb = swap(rda, "rep", 1), swap(rdb, "rep", 1)
    bufs = (wc, rx, ry, rda, rdb, px, py, pda, pdb)

    tok2, cot2 = tokens.reshape(rows, D), cotangent.reshape(rows, D)
    (blend, qkv, probs, ai, gafter, gmx, mods, gmod1, silu, wqkv, g1) = main_call(
        sidx, table, tok2, cot2, bufs, True
    )
    fx0 = swap(rows_at(mc, core * half, half), "fsdp", 1)
    fx1 = swap(fx0, "rep", 1)

    h1 = core_sum(g1, core).astype(BF16)
    s1 = plane_scatter(h1.reshape(4, GRAD_ROWS // 8, D), me).astype(BF16)
    piece = s1.shape[0] // 4
    s1 = s1.reshape(4, piece, D)
    mine = lax.dynamic_index_in_dim(s1, zed, 0, keepdims=False)
    got = [
        swap(lax.dynamic_index_in_dim(s1, zed ^ m, 0, keepdims=False), "rep", 2 * m) for m in (1, 2, 3)
    ]
    zsum = wide_sum([mine] + got).astype(BF16)
    col = jnp.stack([zsum] + [swap(zsum, "rep", 2 * m) for m in (1, 2, 3)])
    plane = jnp.stack([col] + [swap(col, "fsdp", m) for m in (1, 2, 3)])
    both = jnp.stack([plane, swap(plane, "rep", 1)])

    gtok, g2, keep = heads_call(tok2, qkv, probs, ai, gafter, gmx, mods, gmod1, silu, wqkv)

    h2 = core_sum(g2, core).astype(BF16).reshape(4, 3 * D // 8, D)
    s2 = plane_scatter(h2, me).astype(BF16)
    k2 = jnp.concatenate([keep] + [swap(keep, "fsdp", m) for m in (1, 2, 3)], axis=0)
    msg = jnp.concatenate([s2, k2], axis=0)
    z1, z2, z3 = (swap(msg, "rep", 2 * m) for m in (1, 2, 3))
    ns = s2.shape[0]
    q2 = (wide_sum([s2, z1[:ns]]) + wide_sum([z2[:ns], z3[:ns]])).astype(BF16)
    kz = jnp.concatenate([k2, z1[ns:], z2[ns:], z3[ns:]], axis=0)
    kept = jnp.concatenate([kz, swap(kz, "rep", 1)], axis=0)
    p2 = jnp.stack([q2] + [swap(q2, "fsdp", m) for m in (1, 2, 3)])
    both2 = jnp.stack([p2, swap(p2, "rep", 1)])

    tables = step_tables()
    upa, grda = ns_a(sidx, tables, mom, fx0, fx1, kept, both)
    ograd, onew, omom = final_call(sidx, tables, par, mom, both, both2, upa, grda)
    shape = tokens.shape
    return (
        blend.reshape(shape),
        gtok.reshape(shape),
        ograd.reshape(-1),
        onew.reshape(-1),
        omom.reshape(-1),
    )


def unpack(flat):
    pieces, offset = [], 0
    for rows_count, cols_count, _, _ in MATS:
        pieces.append(flat[offset : offset + rows_count * cols_count].reshape(rows_count, cols_count))
        offset += rows_count * cols_count
    return pieces


def to_blocks(mats):
    out = []
    for matrix, (rows_count, cols_count, _, by_cols) in zip(mats, MATS):
        if by_cols:
            out.append(matrix.reshape(D, cols_count // D, D).transpose(1, 0, 2))
        else:
            out.append(matrix.reshape(rows_count // D, D, D))
    return jnp.concatenate(out, axis=0)


def from_blocks(blocks, by_cols):
    if by_cols:
        return blocks.transpose(1, 0, 2).reshape(-1)
    return blocks.reshape(-1)


def orthogonalize(matrix):
    flipped = matrix.shape[0] > matrix.shape[1]
    current = matrix.T if flipped else matrix
    current = current / (jnp.sqrt(jnp.sum(current * current)) + 1e-07)
    for _ in range(NS_ITERS):
        square = jnp.dot(current, current.T, precision=lax.Precision.HIGHEST)
        polynomial = COEFF_B * square + COEFF_C * jnp.dot(square, square, precision=lax.Precision.HIGHEST)
        current = COEFF_A * current + jnp.dot(polynomial, current, precision=lax.Precision.HIGHEST)
    return current.T if flipped else current


def scaled_update(matrix, factor):
    return (factor * orthogonalize(matrix)).reshape(-1)


def empty_update(matrix, factor):
    return jnp.zeros((matrix.shape[0] * matrix.shape[1],), F32)


def any_device(tokens, conditions, assignment, params, momentum, cotangent):
    lat = tokens.shape[0]
    rows = lat * SEQ
    table = lax.all_gather(conditions, ("fsdp", "rep"), axis=0, tiled=True)
    gathered = lax.all_gather(params.astype(BF16), "fsdp", axis=0, tiled=True)
    blocks = to_blocks(unpack(gathered))
    me = lax.axis_index("fsdp")
    sidx = jnp.concatenate([jnp.stack([me, me, me]), assignment]).astype(jnp.int32)
    tok2, cot2 = tokens.reshape(rows, D), cotangent.reshape(rows, D)
    (blend, qkv, probs, ai, gafter, gmx, mods, gmod1, silu, wqkv, g1) = main_call(
        sidx, table, tok2, cot2, (blocks,), False
    )
    gtok, g2, keep = heads_call(tok2, qkv, probs, ai, gafter, gmx, mods, gmod1, silu, wqkv)
    rest = jnp.concatenate(
        [
            from_blocks(g2.reshape(3, D, D), True),
            g1[:D].reshape(-1),
            from_blocks(g1[D : 5 * D].reshape(4, D, D), True),
            g1[5 * D : 9 * D].reshape(-1),
        ]
    )
    kept = lax.all_gather(keep, ("fsdp", "rep"), axis=0, tiled=True).reshape(-1, KEPT_ROWS, D)
    silu_all = kept[:, 6 * lat : 7 * lat].reshape(-1, D)
    mod_all = kept[:, : 6 * lat].reshape(-1, 6, lat, D).transpose(0, 2, 1, 3).reshape(-1, 6 * D)
    adaln = lax.dot_general(silu_all, mod_all, (((0,), (0,)), ((), ())), preferred_element_type=F32)
    shard_len = params.shape[0]
    head = jnp.concatenate([adaln.reshape(-1), jnp.zeros_like(rest)])
    flat = jnp.concatenate([jnp.zeros((D * 6 * D,), F32), rest])
    part = lax.psum_scatter(flat, "fsdp", scatter_dimension=0, tiled=True)
    full_grad = lax.psum(part, "rep") + lax.dynamic_slice_in_dim(head, me * shard_len, shard_len, 0)
    new_momentum = MOMENTUM_RATE * momentum + full_grad
    whole_mom = lax.all_gather(new_momentum, "fsdp", axis=0, tiled=True)
    group_size = lax.axis_size("fsdp")
    updates, offset = [], 0
    for mat, piece in enumerate(unpack(whole_mom)):
        factor = F32(update_scale(mat))
        owner = (offset // shard_len + group_size // 2) % group_size
        updates.append(lax.cond(me == owner, scaled_update, empty_update, piece, factor))
        offset += piece.size
    update = lax.psum_scatter(jnp.concatenate(updates), "fsdp", scatter_dimension=0, tiled=True)
    shape = tokens.shape
    return (blend.reshape(shape), gtok.reshape(shape), full_grad, params - update, new_momentum)


def solution(mesh):
    both = ("fsdp", "rep")
    in_specs = (P(both, None, None), P(both, None), P(both), P("fsdp"), P("fsdp"), P(both, None, None))
    out_specs = (P(both, None, None), P(both, None, None), P("fsdp"), P("fsdp"), P("fsdp"))
    small = dict(mesh.shape) == {"fsdp": 4, "rep": 8}
    return jax.shard_map(
        fast_device if small else any_device,
        mesh=mesh,
        in_specs=in_specs,
        out_specs=out_specs,
        check_vma=False,
    )
```

```python
import functools
import math

import jax
import jax.numpy as jnp
from jax import lax
from jax.experimental import pallas as pl
from jax.experimental.pallas import tpu as pltpu
from jax.sharding import PartitionSpec as P


D = 384
HEADS = 6
HD = 64
FF = 1536
SEQ = 256
NS_ITERS = 3

LN_EPSILON = 1e-06
MOMENTUM_RATE = 0.95
LEARN_RATE = 0.2
COEFF_A = 3.4445
COEFF_B = -4.775
COEFF_C = 2.0315

F32 = jnp.float32
BF16 = jnp.bfloat16
ANY = pl.ANY
VMEM_LIMIT = 60 * 1024 * 1024

MATS = ((D, 6 * D, 0, True), (D, 3 * D, 6, True), (D, D, 9, True), (D, FF, 10, True), (FF, D, 14, False))
NBLOCKS = 18
ADALN, QKV, OUTW, UP, DOWN = range(5)
P_SIZE = sum(m[0] * m[1] for m in MATS)
KEPT_ROWS = 16


def update_scale(mat):
    return LEARN_RATE * 0.2 * math.sqrt(max(MATS[mat][0], MATS[mat][1]))


def shard_pieces(shard, count):
    size = P_SIZE // count
    begin, end = shard * size, (shard + 1) * size
    pieces, crow, offset = [], 0, 0
    for mat, (rows, cols, first, by_cols) in enumerate(MATS):
        lo, hi = max(begin, offset), min(end, offset + rows * cols)
        if lo < hi:
            r0, r1 = (lo - offset) // cols, (hi - offset) // cols
            stride = cols // 128
            base = (offset - begin) // 128
            if by_cols:
                for b in range(cols // D):
                    pieces.append((mat, first + b, r0, r1 - r0, crow, base + r0 * stride + 3 * b, stride))
                    crow += r1 - r0
            else:
                r = r0
                while r < r1:
                    n = min(r1, (r // D + 1) * D) - r
                    pieces.append((mat, first + r // D, r % D, n, crow, base + r * stride, stride))
                    crow += n
                    r += n
        offset += rows * cols
    return pieces


def mm(a, b, ca=1, cb=0):
    return lax.dot_general(a, b, (((ca,), (cb,)), ((), ())), preferred_element_type=F32)


def vspec():
    return pl.BlockSpec(memory_space=pltpu.VMEM)


def aspec():
    return pl.BlockSpec(memory_space=ANY)


def sspec():
    return pl.BlockSpec(memory_space=pltpu.SMEM)


def params_of(**kw):
    return pltpu.CompilerParams(vmem_limit_bytes=VMEM_LIMIT, **kw)


def prep_kernel(count, s_ref, p_ref, m_ref, w_ref, wh_ref, mh_ref, mo_ref):
    for shard in range(count):

        @pl.when(s_ref[0] == shard)
        def _(shard=shard):
            for _, _, _, n, crow, frow, stride in shard_pieces(shard, count):
                for j in range(3):
                    src = pl.ds(frow + j, n, stride=stride)
                    w_ref[crow : crow + n, 128 * j : 128 * j + 128] = p_ref[src, :].astype(BF16)
                    mo_ref[crow : crow + n, 128 * j : 128 * j + 128] = m_ref[src, :].astype(BF16)

    half = wh_ref.shape[0]
    mine = pl.ds(pl.multiple_of(s_ref[1] * half, half), half)
    wh_ref[...] = w_ref[mine, :]
    mh_ref[...] = mo_ref[mine, :]


def prep(sidx, params, momentum, count):
    rows = P_SIZE // count // D
    out = jax.ShapeDtypeStruct((rows, D), BF16)
    part = jax.ShapeDtypeStruct((rows // 2, D), BF16)
    return pl.pallas_call(
        functools.partial(prep_kernel, count),
        out_shape=(out, part, part),
        in_specs=[sspec(), vspec(), vspec()],
        out_specs=(vspec(),) * 3,
        scratch_shapes=[pltpu.VMEM((rows, D), BF16)],
        compiler_params=params_of(),
        name="prep",
    )(sidx, params, momentum)


def layer_norm(h):
    center = jnp.mean(h, axis=-1, keepdims=True)
    cent = h - center
    spread = jnp.mean(jnp.square(cent), axis=-1, keepdims=True)
    rstd = lax.rsqrt(spread + LN_EPSILON)
    return cent * rstd, rstd


def layer_norm_grad(xhat, rstd, gx):
    m1 = jnp.mean(gx, axis=-1, keepdims=True)
    m2 = jnp.mean(gx * xhat, axis=-1, keepdims=True)
    return rstd * (gx - m1 - xhat * m2)


def gather_plan(count):
    plan = []
    half = P_SIZE // count // D // 2
    for shard in range(count):
        for _, block, r0, n, crow, _, _ in shard_pieces(shard, count):
            cuts = sorted({crow, crow + n} | {c for c in range(0, 2 * half + 1, half // 2) if crow < c < crow + n})
            for a, b in zip(cuts[:-1], cuts[1:]):
                plan.append((shard, a // half, a % half, b - a, block, r0 + a - crow))
    return plan


def load_weights_fast(s_ref, bufs, wts, sems, start):
    own, rx, ry, rda, rdb, px, py, pda, pdb = bufs
    me, core = s_ref[0], s_ref[1]
    half = own.shape[0] // 2
    quarter = half // 2
    for q, (shard, h, r, n, block, br) in enumerate(gather_plan(4)):
        dst = wts.at[block, br : br + n]
        if not start:
            pltpu.make_async_copy(own.at[0:n], dst, sems.at[q]).wait()
            continue
        for m in range(4):
            for mine in (True, False):
                if m == 0 and not mine:
                    continue
                cond = me == (shard ^ m)
                if m > 0:
                    cond = jnp.logical_and(cond, (core == h) if mine else (core != h))
                if m == 0:
                    src = own.at[h * half + r : h * half + r + n]
                elif m < 3:
                    src = ((rx, ry) if mine else (px, py))[m - 1].at[r : r + n]
                else:
                    pair = (rda, rdb) if mine else (pda, pdb)
                    k = r // quarter
                    src = pair[k].at[r - k * quarter : r - k * quarter + n]

                @pl.when(cond)
                def _(src=src, dst=dst, q=q):
                    pltpu.make_async_copy(src, dst, sems.at[q]).start()


def by_core(value, core):
    half = value.shape[0] // 2
    top, bottom = value[:half], value[half:]
    return jnp.where(core == 0, top, bottom), jnp.where(core == 0, bottom, top)


def main_kernel(nbuf, fast, rows, s_ref, table, tok, cot, *refs):
    bufs = refs[:nbuf]
    (blend, qkv, probs, amix_in, gafter, gmx, mods, gmod, silu, wqkv, gout, keep1, send1) = refs[nbuf : nbuf + 13]
    wts, ao_s, aa_s, amix, minp, gmi, mo, sems = refs[nbuf + 13 :]
    lat = rows // SEQ
    if fast:
        load_weights_fast(s_ref, bufs, wts, sems, True)
    else:
        whole = pltpu.make_async_copy(bufs[0], wts, sems.at[0])
        whole.start()
    nt = table.shape[0]
    lanes = lax.broadcasted_iota(jnp.int32, (16, nt), 1)
    rws = lax.broadcasted_iota(jnp.int32, (16, nt), 0)
    pick = jnp.zeros((16, nt), jnp.bool_)
    for l in range(lat):
        pick = pick | ((rws == l) & (lanes == s_ref[3 + l]))
    cond = mm(pick.astype(F32).astype(BF16), table[...])
    sc = (cond * (1.0 / (1.0 + jnp.exp(-cond)))).astype(BF16)
    silu[...] = sc.astype(F32)
    if fast:
        load_weights_fast(s_ref, bufs, wts, sems, False)
    else:
        whole.wait()
    for b in range(6):
        mods[b] = mm(sc, wts[b])[:8]
    for j in range(3):
        wqkv[j] = wts[6 + j]

    def mod(b, l):
        return mods[b, l : l + 1, :]

    for l in range(lat):
        rs = slice(l * SEQ, (l + 1) * SEQ)
        xhat, _ = layer_norm(tok[rs, :].astype(F32))
        amix_in[rs, :] = (xhat * (1.0 + mod(1, l)) + mod(0, l)).astype(BF16)
    ai = amix_in[...]
    for j in range(3):
        qkv[j] = mm(ai, wts[6 + j]).astype(BF16)

    low = lax.broadcasted_iota(jnp.int32, (SEQ, 128), 1) < HD
    zero = jnp.zeros((SEQ, 128), BF16)

    def attend(l, carry):
        rs = pl.ds(pl.multiple_of(l * SEQ, SEQ), SEQ)
        for hp in range(HEADS // 2):
            cs = slice(hp * 128, hp * 128 + 128)
            q, k, v = qkv[0, rs, cs], qkv[1, rs, cs], qkv[2, rs, cs]
            outs = []
            for h in range(2):
                qm = jnp.where(low if h == 0 else jnp.logical_not(low), q, zero)
                s = mm(qm, k, 1, 1) * HD ** (-0.5)
                top = jnp.max(s, axis=-1, keepdims=True)
                e = jnp.exp(s - top)
                pr = e * (1.0 / jnp.sum(e, axis=-1, keepdims=True))
                probs[l * HEADS + hp * 2 + h] = pr
                outs.append(mm(pr.astype(BF16), v))
            amix[rs, cs] = jnp.where(low, outs[0], outs[1]).astype(BF16)
        return carry

    lax.fori_loop(0, lat, attend, 0)

    ao = mm(amix[...], wts[9])
    ao_s[...] = ao
    for l in range(lat):
        rs = slice(l * SEQ, (l + 1) * SEQ)
        aa = tok[rs, :].astype(F32) + mod(2, l) * ao_s[rs, :]
        aa_s[rs, :] = aa
        xhat, _ = layer_norm(aa)
        minp[rs, :] = (xhat * (1.0 + mod(4, l)) + mod(3, l)).astype(BF16)
        gmx[rs, :] = (cot[rs, :].astype(F32) * mod(5, l)).astype(BF16)
    gmi[...] = jnp.zeros_like(gmi)
    mo[...] = jnp.zeros_like(mo)

    me, core = s_ref[0], s_ref[1]

    def put(value, members, j):
        mine, other = by_core(value, core)
        for i, member in enumerate(members):
            rs = pl.ds(pl.multiple_of(j * 96, 96), 96)
            keep1[member ^ me, rs, :] = mine[96 * i : 96 * i + 96]
            send1[member ^ me, rs, :] = other[96 * i : 96 * i + 96].astype(BF16)

    def mlp(j, carry):
        wu, wd = wts[10 + j], wts[14 + j]
        u = mm(minp[...], wu)
        c = math.sqrt(2.0 / math.pi)
        u2 = u * u
        t = jnp.tanh(c * (u + 0.044715 * (u2 * u)))
        half = 0.5 * (1.0 + t)
        act = (u * half).astype(BF16)
        slope = half + 0.5 * u * (1.0 - t * t) * (c * (1.0 + 3.0 * 0.044715 * u2))
        mo[...] += mm(act, wd)
        gmo = gmx[...]
        gp = (mm(gmo, wd, 1, 1) * slope).astype(BF16)
        put(mm(act, gmo, 0, 0), (3, 1), j)
        put(mm(minp[...], gp, 0, 0), (2, 0), j)
        gmi[...] += mm(gp, wu, 1, 1)
        return carry

    lax.fori_loop(0, FF // D, mlp, 0)

    gmod[...] = jnp.zeros_like(gmod)
    for l in range(lat):
        rs = slice(l * SEQ, (l + 1) * SEQ)
        up = cot[rs, :].astype(F32)
        blend[rs, :] = (aa_s[rs, :] + mod(5, l) * mo[rs, :]).astype(BF16)
        gmod[5, l : l + 1, :] = jnp.sum(up * mo[rs, :], axis=0, keepdims=True)
        xhat, rstd = layer_norm(aa_s[rs, :])
        g = gmi[rs, :]
        gmod[3, l : l + 1, :] = jnp.sum(g, axis=0, keepdims=True)
        gmod[4, l : l + 1, :] = jnp.sum(g * xhat, axis=0, keepdims=True)
        ga = up + layer_norm_grad(xhat, rstd, g * (1.0 + mod(4, l)))
        gafter[rs, :] = ga
        gmod[2, l : l + 1, :] = jnp.sum(ga * ao_s[rs, :], axis=0, keepdims=True)
        minp[rs, :] = (ga * mod(2, l)).astype(BF16)
    gao = minp[...]
    gout[...] = mm(amix[...], gao, 0, 0)
    gmx[...] = mm(gao, wts[9], 1, 1).astype(BF16)


def main_call(sidx, table, tokens, cotangent, bufs, fast):
    rows = tokens.shape[0]
    lat = rows // SEQ
    sd = jax.ShapeDtypeStruct
    outs = (
        sd((rows, D), BF16),
        sd((3, rows, D), BF16),
        sd((lat * HEADS, SEQ, SEQ), F32),
        sd((rows, D), BF16),
        sd((rows, D), F32),
        sd((rows, D), BF16),
        sd((6, 8, D), F32),
        sd((6, 8, D), F32),
        sd((16, D), F32),
        sd((3, D, D), BF16),
        sd((D, D), F32),
        sd((4, D, D), F32),
        sd((4, D, D), BF16),
    )
    nsem = len(gather_plan(4)) if fast else 1
    return pl.pallas_call(
        functools.partial(main_kernel, len(bufs), fast, rows),
        out_shape=outs,
        in_specs=[sspec(), vspec(), vspec(), vspec()] + [aspec()] * len(bufs),
        out_specs=(vspec(),) * len(outs),
        scratch_shapes=[
            pltpu.VMEM((NBLOCKS, D, D), BF16),
            pltpu.VMEM((rows, D), F32),
            pltpu.VMEM((rows, D), F32),
            pltpu.VMEM((rows, D), BF16),
            pltpu.VMEM((rows, D), BF16),
            pltpu.VMEM((rows, D), F32),
            pltpu.VMEM((rows, D), F32),
            pltpu.SemaphoreType.DMA((nsem,)),
        ],
        compiler_params=params_of(),
        cost_estimate=pl.CostEstimate(flops=20_000_000_000, bytes_accessed=30_000_000, transcendentals=0),
        name="main",
    )(sidx, table, tokens, cotangent, *bufs)


def heads_kernel(rows, qkv, probs, gmx, gqkv):
    lat = rows // SEQ
    low = lax.broadcasted_iota(jnp.int32, (SEQ, 128), 1) < HD
    zero = jnp.zeros((SEQ, 128), BF16)

    def back(l, carry):
        rs = pl.ds(pl.multiple_of(l * SEQ, SEQ), SEQ)
        for hp in range(HEADS // 2):
            cs = slice(hp * 128, hp * 128 + 128)
            q, k, v = qkv[0, rs, cs], qkv[1, rs, cs], qkv[2, rs, cs]
            g = gmx[rs, cs]
            res = []
            for h in range(2):
                p = probs[l * HEADS + hp * 2 + h]
                gm = jnp.where(low if h == 0 else jnp.logical_not(low), g, zero)
                gv = mm(p.astype(BF16), g, 0, 0)
                gpr = mm(gm, v, 1, 1)
                dots = jnp.sum(p * gpr, axis=-1, keepdims=True)
                gs = (p * (gpr - dots) * HD ** (-0.5)).astype(BF16)
                res.append((mm(gs, k), mm(gs, q, 0, 0), gv))
            for j in range(3):
                gqkv[j, rs, cs] = jnp.where(low, res[0][j], res[1][j]).astype(BF16)
        return carry

    lax.fori_loop(0, lat, back, 0)


def heads_call(qkv, probs, gmx):
    rows = gmx.shape[0]
    return pl.pallas_call(
        functools.partial(heads_kernel, rows),
        out_shape=jax.ShapeDtypeStruct((3, rows, D), BF16),
        in_specs=[vspec()] * 3,
        out_specs=vspec(),
        compiler_params=params_of(),
        cost_estimate=pl.CostEstimate(flops=6_000_000_000, bytes_accessed=6_000_000, transcendentals=0),
        name="heads",
    )(qkv, probs, gmx)


def input_kernel(rows, s_ref, tok, gqkv, ai, gafter, mods, gmod1, silu, wqkv, gout, gtok, keep2, send2, keep, srow):
    me, core = s_ref[0], s_ref[1]
    lat = rows // SEQ
    gai = None
    for j in range(4):
        if j < 3:
            part = mm(gqkv[j], wqkv[j], 1, 1)
            gai = part if gai is None else gai + part
            value = mm(ai[...], gqkv[j], 0, 0)
        else:
            value = gout[...]
        mine, other = by_core(value, core)
        for m in range(4):
            rs = slice(48 * j, 48 * j + 48)
            keep2[m ^ me, rs, :] = mine[48 * m : 48 * m + 48]
            send2[m ^ me, rs, :] = other[48 * m : 48 * m + 48].astype(BF16)
    srow[...] = jnp.zeros_like(srow)
    for l in range(lat):
        rs = slice(l * SEQ, (l + 1) * SEQ)
        xhat, rstd = layer_norm(tok[rs, :].astype(F32))
        g = gai[rs, :]
        srow[l : l + 1, :] = jnp.sum(g, axis=0, keepdims=True)
        srow[lat + l : lat + l + 1, :] = jnp.sum(g * xhat, axis=0, keepdims=True)
        gtok[rs, :] = gafter[rs, :] + layer_norm_grad(xhat, rstd, g * (1.0 + mods[1, l : l + 1, :]))
        for b in range(2, 6):
            srow[lat * b + l : lat * b + l + 1, :] = gmod1[b, l : l + 1, :]
        srow[lat * 6 + l : lat * 6 + l + 1, :] = silu[l : l + 1, :]
    keep[...] = srow[...].astype(BF16)


def input_call(sidx, tokens, gqkv, ai, gafter, mods, gmod1, silu, wqkv, gout):
    rows = tokens.shape[0]
    sd = jax.ShapeDtypeStruct
    outs = (sd((rows, D), F32), sd((4, D // 2, D), F32), sd((4, D // 2, D), BF16), sd((KEPT_ROWS, D), BF16))
    return pl.pallas_call(
        functools.partial(input_kernel, rows),
        out_shape=outs,
        in_specs=[sspec()] + [vspec()] * 9,
        out_specs=(vspec(),) * 4,
        scratch_shapes=[pltpu.VMEM((KEPT_ROWS, D), F32)],
        compiler_params=params_of(),
        cost_estimate=pl.CostEstimate(flops=6_000_000_000, bytes_accessed=6_000_000, transcendentals=0),
        name="input",
    )(sidx, tokens, gqkv, ai, gafter, mods, gmod1, silu, wqkv, gout)


def split(x):
    hi = x.astype(BF16)
    return hi, (x - hi.astype(F32)).astype(BF16)


POLY = (COEFF_C, COEFF_B, COEFF_A)
PLAIN = (1.0, 0.0, 0.0)
STEPS = (
    (0, 0, 2, POLY),
    (2, 0, 3, PLAIN),
    (3, 2, 0, PLAIN),
    (0, 0, 1, POLY),
    (1, 2, 2, PLAIN),
    (1, 0, 3, PLAIN),
    (3, 1, 0, PLAIN),
    (0, 0, 1, POLY),
    (1, 2, 2, PLAIN),
)


def step_tables():
    ints = jnp.array([x for st in STEPS for x in st[:3]], jnp.int32)
    coeffs = jnp.array([x for st in STEPS for x in st[3]], F32)
    return ints, coeffs


def either(flipped, tall, wide):
    if flipped is None:
        wide()
    else:
        pl.when(flipped)(tall)
        pl.when(jnp.logical_not(flipped))(wide)


def newton_schulz(ints, coeffs, mat_ref, upd_ref, bufs, npairs, flipped, factor):
    bufs[0] = jnp.zeros((D, D), F32)

    def gram(b, carry):
        x0, x1 = mat_ref[2 * b].astype(BF16), mat_ref[2 * b + 1].astype(BF16)

        def tall():
            x = jnp.concatenate([x0, x1], axis=0)
            bufs[0] += mm(x, x, 0, 0)

        def wide():
            x = jnp.concatenate([x0, x1], axis=1)
            bufs[0] += mm(x, x, 1, 1)

        either(flipped, tall, wide)

        return carry

    lax.fori_loop(0, npairs, gram, 0)
    g = bufs[0]
    ri = lax.broadcasted_iota(jnp.int32, (D, D), 0)
    ci = lax.broadcasted_iota(jnp.int32, (D, D), 1)
    eye = jnp.where(ri == ci, 1.0, 0.0)
    diag = jnp.sum(g * eye, axis=1, keepdims=True)
    total = jnp.sum(diag, axis=0, keepdims=True)
    inv = 1.0 / (jnp.sqrt(total) + 1e-07)
    bufs[0] = g * (inv * inv)

    def step(k, carry):
        i, j, d = ints[3 * k], ints[3 * k + 1], ints[3 * k + 2]
        x = bufs[i]
        xh, xl = split(x)
        yh, yl = split(bufs[j])
        prod = mm(jnp.concatenate([xh, xl, xh], axis=1), jnp.concatenate([yh, yh, yl], axis=0))
        r0 = lax.broadcasted_iota(jnp.int32, (D, D), 0)
        r1 = lax.broadcasted_iota(jnp.int32, (D, D), 1)
        ident = jnp.where(r0 == r1, coeffs[3 * k + 2], 0.0)
        bufs[d] = coeffs[3 * k] * prod + (coeffs[3 * k + 1] * x + ident)
        return carry

    lax.fori_loop(0, len(STEPS), step, 0)
    bufs[0] = bufs[2] * (inv * factor)

    def apply(b, carry):
        wh, wl = split(bufs[0])
        xs = [mat_ref[2 * b + i] for i in range(2)]

        def tall():
            for i in range(2):
                xh, xl = split(xs[i])
                upd_ref[2 * b + i] = mm(
                    jnp.concatenate([xh, xl, xh], axis=1), jnp.concatenate([wh, wh, wl], axis=0)
                )

        def wide():
            (h0, l0), (h1, l1) = split(xs[0]), split(xs[1])
            xh = jnp.concatenate([h0, h1], axis=1)
            xl = jnp.concatenate([l0, l1], axis=1)
            out = mm(jnp.concatenate([wh, wl, wh], axis=1), jnp.concatenate([xh, xh, xl], axis=0))
            upd_ref[2 * b] = out[:, :D]
            upd_ref[2 * b + 1] = out[:, D:]

        either(flipped, tall, wide)
        return carry

    lax.fori_loop(0, npairs, apply, 0)


def take_first(s_ref, chunks, dst):
    me, core, zed = s_ref[0], s_ref[1], s_ref[2]
    for c, ref in enumerate(chunks):
        for y in range(2):
            part = ((me // 2) ^ 1) ^ y
            rs = pl.ds(pl.multiple_of((core ^ c) * 192 + part * 96, 96), 96)
            for z in range(4):
                dst[zed ^ z, rs, :] = ref[y, z].astype(F32)


def take_second(s_ref, chunks, dst):
    me, core, zed = s_ref[0], s_ref[1], s_ref[2]
    for c, ref in enumerate(chunks):
        for m in range(4):
            rs = pl.ds(pl.multiple_of((core ^ c) * 192 + (me ^ m) * 48, 48), 48)
            for z in range(4):
                dst[zed ^ z, rs, :] = ref[m, z].astype(F32)


def adaln_grads(kept, grd, kf):
    ndev = 2 * kept[0].shape[0] // KEPT_ROWS
    for i, ref in enumerate(kept):
        n = ref.shape[0]
        for j in range(3):
            kf[j, i * n : (i + 1) * n, :] = ref[:, 128 * j : 128 * j + 128].astype(F32)

    def rows(first):
        part = [kf[j, pl.ds(first, ndev, stride=KEPT_ROWS), :] for j in range(3)]
        return jnp.concatenate(part, axis=1).astype(BF16)

    sil = jnp.concatenate([rows(12), rows(13)], axis=0)
    for b in range(6):
        gm = jnp.concatenate([rows(2 * b), rows(2 * b + 1)], axis=0)
        grd[b] = mm(sil, gm, 0, 0)


def add_momentum(t, target, mom, grd, mat, base=0):
    first = MATS[target][2]
    for _, block, r0, n, _, frow, stride in [p for p in shard_pieces(t, 4) if p[0] == target]:
        b = block - first
        for j in range(3):
            cs = slice(128 * j, 128 * j + 128)
            m = mom[pl.ds(frow + j, n, stride=stride), :]
            mat[b, r0 : r0 + n, cs] = MOMENTUM_RATE * m + grd[base + b, r0 : r0 + n, cs]


def add_foreign(s_ref, t, target, foreign, grd, mat):
    core = s_ref[1]
    half = foreign[0].shape[0]
    for _, block, r0, n, crow, _, _ in [p for p in shard_pieces(t ^ 1, 4) if p[0] == target]:
        b = block - MATS[target][2]
        cuts = sorted({crow, crow + n} | {c for c in (half,) if crow < c < crow + n})
        for lo, hi in zip(cuts[:-1], cuts[1:]):
            h = lo // half
            for mine, src in enumerate(foreign):

                @pl.when(core == (h ^ mine))
                def _(b=b, r0=r0, lo=lo, hi=hi, h=h, crow=crow, src=src):
                    dst = slice(r0 + lo - crow, r0 + hi - crow)
                    m = src[lo - h * half : hi - h * half, :].astype(F32)
                    mat[b, dst, :] = MOMENTUM_RATE * m + grd[b, dst, :]


TAIL = 48


def ns_a_kernel(s_ref, ints, coeffs, mom, fx0, fx1, kz0, kz1, ch0, ch1, upd, grd, tail, mat, bufs, kf):
    me = s_ref[0]

    @pl.when(me < 2)
    def _():
        adaln_grads((kz0, kz1), grd, kf)

    @pl.when(me >= 2)
    def _():
        take_first(s_ref, (ch0, ch1), grd)

    for t, target in enumerate((ADALN, ADALN, UP, DOWN)):

        @pl.when(me == t)
        def _(t=t, target=target):
            add_momentum(t, target, mom, grd, mat)
            if target != DOWN:
                add_foreign(s_ref, t, target, (fx0, fx1), grd, mat)

    npairs = jnp.where(me < 2, 3, 2)
    factor = jnp.where(me < 2, update_scale(ADALN), update_scale(UP))
    newton_schulz(ints, coeffs, mat, upd, bufs, npairs, me == 3, factor)

    for b in range(4):
        rs = slice(TAIL * b, TAIL * b + TAIL)
        tail[0, rs, :] = grd[b, D - TAIL :, :].astype(BF16)
        tail[1, rs, :] = upd[b, D - TAIL :, :].astype(BF16)


def ns_a(sidx, tables, mom, foreign, kept, chunks):
    sd = jax.ShapeDtypeStruct((6, D, D), F32)
    return pl.pallas_call(
        ns_a_kernel,
        out_shape=(sd, sd, jax.ShapeDtypeStruct((2, 4 * TAIL, D), BF16)),
        in_specs=[sspec()] * 3 + [vspec()] * 7,
        out_specs=(vspec(),) * 3,
        scratch_shapes=[
            pltpu.VMEM((6, D, D), F32),
            pltpu.VMEM((4, D, D), F32),
            pltpu.VMEM((3, 2 * kept[0].shape[0], 128), F32),
        ],
        compiler_params=params_of(),
        cost_estimate=pl.CostEstimate(flops=8_000_000_000, bytes_accessed=12_000_000, transcendentals=0),
        name="ns_a",
    )(sidx, *tables, mom, *foreign, *kept, *chunks)


def final_kernel(
    s_ref, ints, coeffs, par, mom, ch0, ch1, upa, grda, tail, ograd, onew, omom, upb, gb, mat, bufs
):
    me = s_ref[0]
    inner = jnp.logical_or(me == 1, me == 2)

    @pl.when(inner)
    def _():
        take_second(s_ref, (ch0, ch1), gb)
        for b in range(1, 4):
            mat[b] = jnp.zeros((D, D), F32)

    @pl.when(me == 1)
    def _():
        add_momentum(1, QKV, mom, gb, mat)

    @pl.when(me == 2)
    def _():
        add_momentum(2, OUTW, mom, gb, mat, 3)

    @pl.when(inner)
    def _():
        npairs = jnp.where(me == 1, 2, 1)
        factor = jnp.where(me == 1, update_scale(QKV), update_scale(OUTW))
        newton_schulz(ints, coeffs, mat, upb, bufs, npairs, None, factor)

    for t in range(4):

        @pl.when(me == t)
        def _(t=t):
            for mat_id, block, r0, n, crow, frow, stride in shard_pieces(t, 4):
                b = block - MATS[mat_id][2]
                for j in range(3):
                    cs = slice(128 * j, 128 * j + 128)
                    fl = pl.ds(frow + j, n, stride=stride)
                    if mat_id == UP and t == 3:
                        assert r0 == D - TAIL and n == TAIL
                        g = tail[0, TAIL * b : TAIL * b + TAIL, cs].astype(F32)
                        u = tail[1, TAIL * b : TAIL * b + TAIL, cs].astype(F32)
                    elif mat_id in (QKV, OUTW):
                        g = gb[b + 3 * (mat_id == OUTW), r0 : r0 + n, cs]
                        u = upb[b, r0 : r0 + n, cs]
                    else:
                        g = grda[b, r0 : r0 + n, cs]
                        u = upa[b, r0 : r0 + n, cs]
                    ograd[fl, :] = g
                    omom[fl, :] = MOMENTUM_RATE * mom[fl, :] + g
                    onew[fl, :] = par[fl, :] - u


def final_call(sidx, tables, par, mom, chunks, upa, grda, tail):
    sd = jax.ShapeDtypeStruct(par.shape, F32)
    block4 = pltpu.VMEM((4, D, D), F32)
    return pl.pallas_call(
        final_kernel,
        out_shape=(sd, sd, sd),
        in_specs=[sspec()] * 3 + [vspec()] * 7,
        out_specs=(vspec(),) * 3,
        scratch_shapes=[block4, block4, block4, block4],
        compiler_params=params_of(),
        cost_estimate=pl.CostEstimate(flops=8_000_000_000, bytes_accessed=24_000_000, transcendentals=0),
        name="finish",
    )(sidx, *tables, par, mom, *chunks, upa, grda, tail)


def swap(x, axis, mask):
    count = lax.axis_size(axis)
    return lax.ppermute(x, axis, [(i, i ^ mask) for i in range(count)])


def more_rows(x, hops):
    for axis, mask in hops:
        x = jnp.concatenate([x, swap(x, axis, mask)], axis=0)
    return x


def wide_sum(parts):
    total = None
    for p in parts:
        total = p.astype(F32) if total is None else total + p.astype(F32)
    return total


def at(x, i):
    return lax.dynamic_index_in_dim(x, i, 0, keepdims=False)


def z_scatter(s, zed, extra=None):
    size = s.shape[0] // 4
    blocks = s.reshape(4, size, D)
    got = []
    for m in (1, 2, 3):
        piece = at(blocks, zed ^ m).astype(BF16)
        if extra is not None:
            piece = jnp.concatenate([piece, extra], axis=0)
        got.append(swap(piece, "rep", 2 * m))
    total = wide_sum([at(blocks, zed)] + [g[:size] for g in got]).astype(BF16)
    if extra is None:
        return total
    return total, jnp.concatenate([extra] + [g[size:] for g in got], axis=0)


def fan(x, axis, masks):
    got = [x]
    for m in masks:
        got.append(swap(x, axis, m))
    return jnp.stack(got)


def fast_device(tokens, conditions, assignment, params, momentum, cotangent):
    return fast_body(tokens, conditions, assignment, params, momentum, cotangent)


def fast_body(tokens, conditions, assignment, params, momentum, cotangent):
    me = lax.axis_index("fsdp")
    rep = lax.axis_index("rep")
    core, zed = rep % 2, rep // 2
    lat = tokens.shape[0]
    rows = lat * SEQ
    par = params.reshape(-1, 128)
    mom = momentum.reshape(-1, 128)
    source = assignment // lat
    apart = ((source // 8) ^ me) + 4 * ((source % 8) ^ rep)
    pick = apart * lat + assignment % lat
    sidx = jnp.concatenate([jnp.stack([me, core, zed]), pick]).astype(jnp.int32)

    hop = swap(conditions, "fsdp", 1)
    wc, wh, mh = prep(sidx, par, mom, 4)
    table = jnp.concatenate([conditions, hop], axis=0)
    table, wh = lax.optimization_barrier((table, wh))
    hop = swap(table, "fsdp", 2)
    rx = swap(wh, "fsdp", 1)
    ry = swap(wh, "fsdp", 2)
    table = jnp.concatenate([table, hop], axis=0)
    table = more_rows(table, (("rep", 1), ("rep", 2), ("rep", 4)))
    rx, ry, table = lax.optimization_barrier((rx, ry, table))
    quarter = wh.shape[0] // 2
    rda, rdb = swap(rx[:quarter], "fsdp", 2), swap(ry[quarter:], "fsdp", 1)
    px, py = swap(rx, "rep", 1), swap(ry, "rep", 1)
    pda, pdb = swap(rda, "rep", 1), swap(rdb, "rep", 1)
    bufs = (wc, rx, ry, rda, rdb, px, py, pda, pdb)
    fx0 = swap(mh, "fsdp", 1)

    tok2, cot2 = tokens.reshape(rows, D), cotangent.reshape(rows, D)
    (blend, qkv, probs, ai, gafter, gmx, mods, gmod1, silu, wqkv, gout, keep1, send1) = main_call(
        sidx, table, tok2, cot2, bufs, True
    )
    fx1 = swap(fx0, "rep", 1)

    other = swap(send1, "rep", 1)
    gqkv = heads_call(qkv, probs, gmx)
    got = []
    for m in (1, 2, 3):
        got.append(swap((keep1[m] + other[m].astype(F32)).astype(BF16), "fsdp", m))
    gtok, keep2, send2, keep = input_call(sidx, tok2, gqkv, ai, gafter, mods, gmod1, silu, wqkv, gout)
    s1 = wide_sum([keep1[0] + other[0].astype(F32)] + got)
    col = fan(z_scatter(s1, zed), "rep", (2, 4, 6))
    pair = fan(col, "fsdp", (2,))
    pairs = (pair, swap(pair, "rep", 1))

    other = swap(send2, "rep", 1)
    got = []
    for m in (1, 2, 3):
        part = (keep2[m] + other[m].astype(F32)).astype(BF16)
        got.append(swap(jnp.concatenate([part, keep], axis=0), "fsdp", m))
    size = keep2.shape[1]
    s2 = wide_sum([keep2[0] + other[0].astype(F32)] + [g[:size] for g in got])
    q2, kz = z_scatter(s2, zed, jnp.concatenate([keep] + [g[size:] for g in got], axis=0))
    kept = (kz, swap(kz, "rep", 1))
    quad = fan(fan(q2, "rep", (2, 4, 6)), "fsdp", (1, 2, 3))
    quads = (quad, swap(quad, "rep", 1))

    tables = step_tables()
    upa, grda, tail = ns_a(sidx, tables, mom, (fx0, fx1), kept, pairs)
    tail = swap(tail, "fsdp", 1)
    ograd, onew, omom = final_call(sidx, tables, par, mom, quads, upa, grda, tail)
    shape = tokens.shape
    return (
        blend.reshape(shape),
        gtok.reshape(shape),
        ograd.reshape(-1),
        onew.reshape(-1),
        omom.reshape(-1),
    )


def unpack(flat):
    pieces, offset = [], 0
    for rows_count, cols_count, _, _ in MATS:
        pieces.append(flat[offset : offset + rows_count * cols_count].reshape(rows_count, cols_count))
        offset += rows_count * cols_count
    return pieces


def to_blocks(mats):
    out = []
    for matrix, (rows_count, cols_count, _, by_cols) in zip(mats, MATS):
        if by_cols:
            out.append(matrix.reshape(D, cols_count // D, D).transpose(1, 0, 2))
        else:
            out.append(matrix.reshape(rows_count // D, D, D))
    return jnp.concatenate(out, axis=0)


def from_blocks(blocks, by_cols):
    if by_cols:
        return blocks.transpose(1, 0, 2).reshape(-1)
    return blocks.reshape(-1)


def orthogonalize(matrix):
    flipped = matrix.shape[0] > matrix.shape[1]
    current = matrix.T if flipped else matrix
    current = current / (jnp.sqrt(jnp.sum(current * current)) + 1e-07)
    for _ in range(NS_ITERS):
        square = jnp.dot(current, current.T, precision=lax.Precision.HIGHEST)
        polynomial = COEFF_B * square + COEFF_C * jnp.dot(square, square, precision=lax.Precision.HIGHEST)
        current = COEFF_A * current + jnp.dot(polynomial, current, precision=lax.Precision.HIGHEST)
    return current.T if flipped else current


def scaled_update(matrix, factor):
    return (factor * orthogonalize(matrix)).reshape(-1)


def empty_update(matrix, factor):
    return jnp.zeros((matrix.shape[0] * matrix.shape[1],), F32)


def any_device(tokens, conditions, assignment, params, momentum, cotangent):
    lat = tokens.shape[0]
    rows = lat * SEQ
    table = lax.all_gather(conditions, ("fsdp", "rep"), axis=0, tiled=True)
    gathered = lax.all_gather(params.astype(BF16), "fsdp", axis=0, tiled=True)
    blocks = to_blocks(unpack(gathered))
    me = lax.axis_index("fsdp")
    sidx = jnp.concatenate([jnp.zeros((3,), jnp.int32), assignment.astype(jnp.int32)])
    tok2, cot2 = tokens.reshape(rows, D), cotangent.reshape(rows, D)
    (blend, qkv, probs, ai, gafter, gmx, mods, gmod1, silu, wqkv, gout, keep1, send1) = main_call(
        sidx, table, tok2, cot2, (blocks,), False
    )
    gqkv = heads_call(qkv, probs, gmx)
    gtok, keep2, send2, keep = input_call(sidx, tok2, gqkv, ai, gafter, mods, gmod1, silu, wqkv, gout)
    halves1 = jnp.stack([keep1, send1.astype(F32)]).reshape(2, 4, 4, 96, D)
    up = halves1[:, jnp.array([2, 0])].transpose(2, 0, 1, 3, 4).reshape(4, D, D)
    down = halves1[:, jnp.array([3, 1])].transpose(2, 0, 1, 3, 4).reshape(4, D, D)
    halves2 = jnp.stack([keep2, send2.astype(F32)]).reshape(2, 4, 4, 48, D)
    last = halves2.transpose(2, 0, 1, 3, 4).reshape(4, D, D)
    rest = jnp.concatenate(
        [from_blocks(last[:3], True), last[3].reshape(-1), from_blocks(up, True), down.reshape(-1)]
    )
    kept = lax.all_gather(keep, ("fsdp", "rep"), axis=0, tiled=True).reshape(-1, KEPT_ROWS, D)
    silu_all = kept[:, 6 * lat : 7 * lat].reshape(-1, D)
    mod_all = kept[:, : 6 * lat].reshape(-1, 6, lat, D).transpose(0, 2, 1, 3).reshape(-1, 6 * D)
    adaln = lax.dot_general(silu_all, mod_all, (((0,), (0,)), ((), ())), preferred_element_type=F32)
    shard_len = params.shape[0]
    head = jnp.concatenate([adaln.reshape(-1), jnp.zeros_like(rest)])
    flat = jnp.concatenate([jnp.zeros((D * 6 * D,), F32), rest])
    part = lax.psum_scatter(flat, "fsdp", scatter_dimension=0, tiled=True)
    full_grad = lax.psum(part, "rep") + lax.dynamic_slice_in_dim(head, me * shard_len, shard_len, 0)
    new_momentum = MOMENTUM_RATE * momentum + full_grad
    whole_mom = lax.all_gather(new_momentum, "fsdp", axis=0, tiled=True)
    group_size = lax.axis_size("fsdp")
    updates, offset = [], 0
    for mat, piece in enumerate(unpack(whole_mom)):
        factor = F32(update_scale(mat))
        owner = (offset // shard_len + group_size // 2) % group_size
        updates.append(lax.cond(me == owner, scaled_update, empty_update, piece, factor))
        offset += piece.size
    update = lax.psum_scatter(jnp.concatenate(updates), "fsdp", scatter_dimension=0, tiled=True)
    shape = tokens.shape
    return (blend.reshape(shape), gtok.reshape(shape), full_grad, params - update, new_momentum)


def solution(mesh):
    both = ("fsdp", "rep")
    in_specs = (P(both, None, None), P(both, None), P(both), P("fsdp"), P("fsdp"), P(both, None, None))
    out_specs = (P(both, None, None), P(both, None, None), P("fsdp"), P("fsdp"), P("fsdp"))
    small = dict(mesh.shape) == {"fsdp": 4, "rep": 8}
    return jax.shard_map(
        fast_device if small else any_device,
        mesh=mesh,
        in_specs=in_specs,
        out_specs=out_specs,
        check_vma=False,
    )
```

```python
import functools
import math

import jax
import jax.numpy as jnp
from jax import lax
from jax.experimental import pallas as pl
from jax.experimental.pallas import tpu as pltpu
from jax.sharding import PartitionSpec as P


D = 384
HEADS = 6
HD = 64
FF = 1536
SEQ = 256
NS_ITERS = 3

LN_EPSILON = 1e-06
MOMENTUM_RATE = 0.95
LEARN_RATE = 0.2
COEFF_A = 3.4445
COEFF_B = -4.775
COEFF_C = 2.0315

F32 = jnp.float32
BF16 = jnp.bfloat16
ANY = pl.ANY

MATS = ((D, 6 * D, 0, True), (D, 3 * D, 6, True), (D, D, 9, True), (D, FF, 10, True), (FF, D, 14, False))
NBLOCKS = 18
ADALN, QKV, OUTW, UP, DOWN = range(5)
P_SIZE = sum(m[0] * m[1] for m in MATS)
KEPT_ROWS = 16


def update_scale(mat):
    return LEARN_RATE * 0.2 * math.sqrt(max(MATS[mat][0], MATS[mat][1]))


def shard_pieces(shard, count):
    size = P_SIZE // count
    begin, end = shard * size, (shard + 1) * size
    pieces, crow, offset = [], 0, 0
    for mat, (rows, cols, first, by_cols) in enumerate(MATS):
        lo, hi = max(begin, offset), min(end, offset + rows * cols)
        if lo < hi:
            r0, r1 = (lo - offset) // cols, (hi - offset) // cols
            stride = cols // 128
            base = (offset - begin) // 128
            if by_cols:
                for b in range(cols // D):
                    pieces.append((mat, first + b, r0, r1 - r0, crow, base + r0 * stride + 3 * b, stride))
                    crow += r1 - r0
            else:
                r = r0
                while r < r1:
                    n = min(r1, (r // D + 1) * D) - r
                    pieces.append((mat, first + r // D, r % D, n, crow, base + r * stride, stride))
                    crow += n
                    r += n
        offset += rows * cols
    return pieces


def mm(a, b, ca=1, cb=0):
    return lax.dot_general(a, b, (((ca,), (cb,)), ((), ())), preferred_element_type=F32)


def vspec():
    return pl.BlockSpec(memory_space=pltpu.VMEM)


def aspec():
    return pl.BlockSpec(memory_space=ANY)


def sspec():
    return pl.BlockSpec(memory_space=pltpu.SMEM)


def params_of(mib):
    return pltpu.CompilerParams(vmem_limit_bytes=mib * 1024 * 1024)


def prep_kernel(count, s_ref, p_ref, m_ref, w_ref, wh_ref, mh_ref, mo_ref):
    for shard in range(count):

        @pl.when(s_ref[0] == shard)
        def _(shard=shard):
            for _, _, _, n, crow, frow, stride in shard_pieces(shard, count):
                for j in range(3):
                    src = pl.ds(frow + j, n, stride=stride)
                    w_ref[crow : crow + n, 128 * j : 128 * j + 128] = p_ref[src, :].astype(BF16)
                    mo_ref[crow : crow + n, 128 * j : 128 * j + 128] = m_ref[src, :].astype(BF16)

    half = wh_ref.shape[0]
    mine = pl.ds(pl.multiple_of(s_ref[1] * half, half), half)
    wh_ref[...] = w_ref[mine, :]
    mh_ref[...] = mo_ref[mine, :]


def prep(sidx, params, momentum, count):
    rows = P_SIZE // count // D
    out = jax.ShapeDtypeStruct((rows, D), BF16)
    part = jax.ShapeDtypeStruct((rows // 2, D), BF16)
    return pl.pallas_call(
        functools.partial(prep_kernel, count),
        out_shape=(out, part, part),
        in_specs=[sspec(), vspec(), vspec()],
        out_specs=(vspec(),) * 3,
        scratch_shapes=[pltpu.VMEM((rows, D), BF16)],
        compiler_params=params_of(12),
        name="prep",
    )(sidx, params, momentum)


def layer_norm(h):
    center = jnp.mean(h, axis=-1, keepdims=True)
    cent = h - center
    spread = jnp.mean(jnp.square(cent), axis=-1, keepdims=True)
    rstd = lax.rsqrt(spread + LN_EPSILON)
    return cent * rstd, rstd


def layer_norm_grad(xhat, rstd, gx):
    m1 = jnp.mean(gx, axis=-1, keepdims=True)
    m2 = jnp.mean(gx * xhat, axis=-1, keepdims=True)
    return rstd * (gx - m1 - xhat * m2)


def gather_plan(count):
    plan = []
    half = P_SIZE // count // D // 2
    for shard in range(count):
        for _, block, r0, n, crow, _, _ in shard_pieces(shard, count):
            cuts = sorted({crow, crow + n} | {c for c in range(0, 2 * half + 1, half // 2) if crow < c < crow + n})
            for a, b in zip(cuts[:-1], cuts[1:]):
                plan.append((shard, a // half, a % half, b - a, block, r0 + a - crow))
    return plan


def load_weights_fast(s_ref, bufs, wts, sems, start):
    own, rx, ry, rda, rdb, px, py, pda, pdb = bufs
    me, core = s_ref[0], s_ref[1]
    half = own.shape[0] // 2
    quarter = half // 2
    for q, (shard, h, r, n, block, br) in enumerate(gather_plan(4)):
        dst = wts.at[block, br : br + n]
        if not start:
            pltpu.make_async_copy(own.at[0:n], dst, sems.at[q]).wait()
            continue
        for m in range(4):
            for mine in (True, False):
                if m == 0 and not mine:
                    continue
                cond = me == (shard ^ m)
                if m > 0:
                    cond = jnp.logical_and(cond, (core == h) if mine else (core != h))
                if m == 0:
                    src = own.at[h * half + r : h * half + r + n]
                elif m < 3:
                    src = ((rx, ry) if mine else (px, py))[m - 1].at[r : r + n]
                else:
                    pair = (rda, rdb) if mine else (pda, pdb)
                    k = r // quarter
                    src = pair[k].at[r - k * quarter : r - k * quarter + n]

                @pl.when(cond)
                def _(src=src, dst=dst, q=q):
                    pltpu.make_async_copy(src, dst, sems.at[q]).start()


def by_core(value, core):
    half = value.shape[0] // 2
    top, bottom = value[:half], value[half:]
    return jnp.where(core == 0, top, bottom), jnp.where(core == 0, bottom, top)


def main_kernel(nbuf, fast, rows, s_ref, table, tok, cot, *refs):
    bufs = refs[:nbuf]
    (blend, qkv, probs, amix_in, gafter, gmx, mods, gmod, silu, wqkv, gout, keep1, send1) = refs[nbuf : nbuf + 13]
    wts, ao_s, aa_s, amix, minp, gmi, mo, sems = refs[nbuf + 13 :]
    lat = rows // SEQ
    if fast:
        load_weights_fast(s_ref, bufs, wts, sems, True)
    else:
        whole = pltpu.make_async_copy(bufs[0], wts, sems.at[0])
        whole.start()
    nt = table.shape[0]
    lanes = lax.broadcasted_iota(jnp.int32, (16, nt), 1)
    rws = lax.broadcasted_iota(jnp.int32, (16, nt), 0)
    pick = jnp.zeros((16, nt), jnp.bool_)
    for l in range(lat):
        pick = pick | ((rws == l) & (lanes == s_ref[3 + l]))
    cond = mm(pick.astype(F32).astype(BF16), table[...])
    sc = (cond * (1.0 / (1.0 + jnp.exp(-cond)))).astype(BF16)
    silu[...] = sc.astype(F32)
    if fast:
        load_weights_fast(s_ref, bufs, wts, sems, False)
    else:
        whole.wait()
    for b in range(6):
        mods[b] = mm(sc, wts[b])[:8]
    for j in range(3):
        wqkv[j] = wts[6 + j]

    def mod(b, l):
        return mods[b, l : l + 1, :]

    for l in range(lat):
        rs = slice(l * SEQ, (l + 1) * SEQ)
        xhat, _ = layer_norm(tok[rs, :].astype(F32))
        amix_in[rs, :] = (xhat * (1.0 + mod(1, l)) + mod(0, l)).astype(BF16)
    ai = amix_in[...]
    for j in range(3):
        qkv[j] = mm(ai, wts[6 + j]).astype(BF16)

    low = lax.broadcasted_iota(jnp.int32, (SEQ, 128), 1) < HD
    zero = jnp.zeros((SEQ, 128), BF16)

    def attend(l, carry):
        rs = pl.ds(pl.multiple_of(l * SEQ, SEQ), SEQ)
        for hp in range(HEADS // 2):
            cs = slice(hp * 128, hp * 128 + 128)
            q, k, v = qkv[0, rs, cs], qkv[1, rs, cs], qkv[2, rs, cs]
            outs = []
            for h in range(2):
                qm = jnp.where(low if h == 0 else jnp.logical_not(low), q, zero)
                s = mm(qm, k, 1, 1) * HD ** (-0.5)
                top = jnp.max(s, axis=-1, keepdims=True)
                e = jnp.exp(s - top)
                pr = e * (1.0 / jnp.sum(e, axis=-1, keepdims=True))
                probs[l * HEADS + hp * 2 + h] = pr
                outs.append(mm(pr.astype(BF16), v))
            amix[rs, cs] = jnp.where(low, outs[0], outs[1]).astype(BF16)
        return carry

    lax.fori_loop(0, lat, attend, 0)

    ao = mm(amix[...], wts[9])
    ao_s[...] = ao
    for l in range(lat):
        rs = slice(l * SEQ, (l + 1) * SEQ)
        aa = tok[rs, :].astype(F32) + mod(2, l) * ao_s[rs, :]
        aa_s[rs, :] = aa
        xhat, _ = layer_norm(aa)
        minp[rs, :] = (xhat * (1.0 + mod(4, l)) + mod(3, l)).astype(BF16)
        gmx[rs, :] = (cot[rs, :].astype(F32) * mod(5, l)).astype(BF16)
    gmi[...] = jnp.zeros_like(gmi)
    mo[...] = jnp.zeros_like(mo)

    me, core = s_ref[0], s_ref[1]

    def put(value, members, j):
        mine, other = by_core(value, core)
        for i, member in enumerate(members):
            rs = pl.ds(pl.multiple_of(j * 96, 96), 96)
            keep1[member ^ me, rs, :] = mine[96 * i : 96 * i + 96]
            send1[member ^ me, rs, :] = other[96 * i : 96 * i + 96].astype(BF16)

    def mlp(j, carry):
        wu, wd = wts[10 + j], wts[14 + j]
        u = mm(minp[...], wu)
        c = math.sqrt(2.0 / math.pi)
        u2 = u * u
        t = jnp.tanh(c * (u + 0.044715 * (u2 * u)))
        half = 0.5 * (1.0 + t)
        act = (u * half).astype(BF16)
        slope = half + 0.5 * u * (1.0 - t * t) * (c * (1.0 + 3.0 * 0.044715 * u2))
        mo[...] += mm(act, wd)
        gmo = gmx[...]
        gp = (mm(gmo, wd, 1, 1) * slope).astype(BF16)
        put(mm(act, gmo, 0, 0), (3, 1), j)
        put(mm(minp[...], gp, 0, 0), (2, 0), j)
        gmi[...] += mm(gp, wu, 1, 1)
        return carry

    lax.fori_loop(0, FF // D, mlp, 0)

    gmod[...] = jnp.zeros_like(gmod)
    for l in range(lat):
        rs = slice(l * SEQ, (l + 1) * SEQ)
        up = cot[rs, :].astype(F32)
        blend[rs, :] = (aa_s[rs, :] + mod(5, l) * mo[rs, :]).astype(BF16)
        gmod[5, l : l + 1, :] = jnp.sum(up * mo[rs, :], axis=0, keepdims=True)
        xhat, rstd = layer_norm(aa_s[rs, :])
        g = gmi[rs, :]
        gmod[3, l : l + 1, :] = jnp.sum(g, axis=0, keepdims=True)
        gmod[4, l : l + 1, :] = jnp.sum(g * xhat, axis=0, keepdims=True)
        ga = up + layer_norm_grad(xhat, rstd, g * (1.0 + mod(4, l)))
        gafter[rs, :] = ga
        gmod[2, l : l + 1, :] = jnp.sum(ga * ao_s[rs, :], axis=0, keepdims=True)
        minp[rs, :] = (ga * mod(2, l)).astype(BF16)
    gao = minp[...]
    gout[...] = mm(amix[...], gao, 0, 0)
    gmx[...] = mm(gao, wts[9], 1, 1).astype(BF16)


def main_call(sidx, table, tokens, cotangent, bufs, fast):
    rows = tokens.shape[0]
    lat = rows // SEQ
    sd = jax.ShapeDtypeStruct
    outs = (
        sd((rows, D), BF16),
        sd((3, rows, D), BF16),
        sd((lat * HEADS, SEQ, SEQ), F32),
        sd((rows, D), BF16),
        sd((rows, D), F32),
        sd((rows, D), BF16),
        sd((6, 8, D), F32),
        sd((6, 8, D), F32),
        sd((16, D), F32),
        sd((3, D, D), BF16),
        sd((D, D), F32),
        sd((4, D, D), F32),
        sd((4, D, D), BF16),
    )
    nsem = len(gather_plan(4)) if fast else 1
    return pl.pallas_call(
        functools.partial(main_kernel, len(bufs), fast, rows),
        out_shape=outs,
        in_specs=[sspec(), vspec(), vspec(), vspec()] + [aspec()] * len(bufs),
        out_specs=(vspec(),) * len(outs),
        scratch_shapes=[
            pltpu.VMEM((NBLOCKS, D, D), BF16),
            pltpu.VMEM((rows, D), F32),
            pltpu.VMEM((rows, D), F32),
            pltpu.VMEM((rows, D), BF16),
            pltpu.VMEM((rows, D), BF16),
            pltpu.VMEM((rows, D), F32),
            pltpu.VMEM((rows, D), F32),
            pltpu.SemaphoreType.DMA((nsem,)),
        ],
        compiler_params=params_of(34),
        cost_estimate=pl.CostEstimate(flops=20_000_000_000, bytes_accessed=30_000_000, transcendentals=0),
        name="main",
    )(sidx, table, tokens, cotangent, *bufs)


def heads_kernel(rows, qkv, probs, gmx, gqkv):
    lat = rows // SEQ
    low = lax.broadcasted_iota(jnp.int32, (SEQ, 128), 1) < HD
    zero = jnp.zeros((SEQ, 128), BF16)

    def back(l, carry):
        rs = pl.ds(pl.multiple_of(l * SEQ, SEQ), SEQ)
        for hp in range(HEADS // 2):
            cs = slice(hp * 128, hp * 128 + 128)
            q, k, v = qkv[0, rs, cs], qkv[1, rs, cs], qkv[2, rs, cs]
            g = gmx[rs, cs]
            res = []
            for h in range(2):
                p = probs[l * HEADS + hp * 2 + h]
                gm = jnp.where(low if h == 0 else jnp.logical_not(low), g, zero)
                gv = mm(p.astype(BF16), g, 0, 0)
                gpr = mm(gm, v, 1, 1)
                dots = jnp.sum(p * gpr, axis=-1, keepdims=True)
                gs = (p * (gpr - dots) * HD ** (-0.5)).astype(BF16)
                res.append((mm(gs, k), mm(gs, q, 0, 0), gv))
            for j in range(3):
                gqkv[j, rs, cs] = jnp.where(low, res[0][j], res[1][j]).astype(BF16)
        return carry

    lax.fori_loop(0, lat, back, 0)


def heads_call(qkv, probs, gmx):
    rows = gmx.shape[0]
    return pl.pallas_call(
        functools.partial(heads_kernel, rows),
        out_shape=jax.ShapeDtypeStruct((3, rows, D), BF16),
        in_specs=[vspec()] * 3,
        out_specs=vspec(),
        compiler_params=params_of(12),
        cost_estimate=pl.CostEstimate(flops=6_000_000_000, bytes_accessed=6_000_000, transcendentals=0),
        name="heads",
    )(qkv, probs, gmx)


def input_kernel(rows, s_ref, tok, gqkv, ai, gafter, mods, gmod1, silu, wqkv, gout, gtok, keep2, send2, keep, srow):
    me, core = s_ref[0], s_ref[1]
    lat = rows // SEQ
    gai = None
    for j in range(4):
        if j < 3:
            part = mm(gqkv[j], wqkv[j], 1, 1)
            gai = part if gai is None else gai + part
            value = mm(ai[...], gqkv[j], 0, 0)
        else:
            value = gout[...]
        mine, other = by_core(value, core)
        for m in range(4):
            rs = slice(48 * j, 48 * j + 48)
            keep2[m ^ me, rs, :] = mine[48 * m : 48 * m + 48]
            send2[m ^ me, rs, :] = other[48 * m : 48 * m + 48].astype(BF16)
    srow[...] = jnp.zeros_like(srow)
    for l in range(lat):
        rs = slice(l * SEQ, (l + 1) * SEQ)
        xhat, rstd = layer_norm(tok[rs, :].astype(F32))
        g = gai[rs, :]
        srow[l : l + 1, :] = jnp.sum(g, axis=0, keepdims=True)
        srow[lat + l : lat + l + 1, :] = jnp.sum(g * xhat, axis=0, keepdims=True)
        gtok[rs, :] = gafter[rs, :] + layer_norm_grad(xhat, rstd, g * (1.0 + mods[1, l : l + 1, :]))
        for b in range(2, 6):
            srow[lat * b + l : lat * b + l + 1, :] = gmod1[b, l : l + 1, :]
        srow[lat * 6 + l : lat * 6 + l + 1, :] = silu[l : l + 1, :]
    keep[...] = srow[...].astype(BF16)


def input_call(sidx, tokens, gqkv, ai, gafter, mods, gmod1, silu, wqkv, gout):
    rows = tokens.shape[0]
    sd = jax.ShapeDtypeStruct
    outs = (sd((rows, D), F32), sd((4, D // 2, D), F32), sd((4, D // 2, D), BF16), sd((KEPT_ROWS, D), BF16))
    return pl.pallas_call(
        functools.partial(input_kernel, rows),
        out_shape=outs,
        in_specs=[sspec()] + [vspec()] * 9,
        out_specs=(vspec(),) * 4,
        scratch_shapes=[pltpu.VMEM((KEPT_ROWS, D), F32)],
        compiler_params=params_of(12),
        cost_estimate=pl.CostEstimate(flops=6_000_000_000, bytes_accessed=6_000_000, transcendentals=0),
        name="input",
    )(sidx, tokens, gqkv, ai, gafter, mods, gmod1, silu, wqkv, gout)


def split(x):
    hi = x.astype(BF16)
    return hi, (x - hi.astype(F32)).astype(BF16)


POLY = (COEFF_C, COEFF_B, COEFF_A)
PLAIN = (1.0, 0.0, 0.0)
STEPS = (
    (0, 0, 2, 1, POLY),
    (2, 0, 3, 2, PLAIN),
    (3, 2, 0, 2, PLAIN),
    (0, 0, 1, 1, POLY),
    (1, 2, 2, 3, PLAIN),
    (1, 0, 3, 2, PLAIN),
    (3, 1, 0, 2, PLAIN),
    (0, 0, 1, 3, POLY),
    (1, 2, 2, 3, PLAIN),
)


def step_tables():
    ints = jnp.array([x for st in STEPS for x in st[:4]], jnp.int32)
    coeffs = jnp.array([x for st in STEPS for x in st[4]], F32)
    return ints, coeffs


def either(flipped, tall, wide):
    if flipped is None:
        wide()
    else:
        pl.when(flipped)(tall)
        pl.when(jnp.logical_not(flipped))(wide)


def newton_schulz(ints, coeffs, mat_ref, upd_ref, bufs, npairs, flipped, factor):
    bufs[0] = jnp.zeros((D, D), F32)

    def gram(b, carry):
        x0, x1 = mat_ref[2 * b].astype(BF16), mat_ref[2 * b + 1].astype(BF16)

        def tall():
            x = jnp.concatenate([x0, x1], axis=0)
            bufs[0] += mm(x, x, 0, 0)

        def wide():
            x = jnp.concatenate([x0, x1], axis=1)
            bufs[0] += mm(x, x, 1, 1)

        either(flipped, tall, wide)

        return carry

    lax.fori_loop(0, npairs, gram, 0)
    g = bufs[0]
    ri = lax.broadcasted_iota(jnp.int32, (D, D), 0)
    ci = lax.broadcasted_iota(jnp.int32, (D, D), 1)
    eye = jnp.where(ri == ci, 1.0, 0.0)
    diag = jnp.sum(g * eye, axis=1, keepdims=True)
    total = jnp.sum(diag, axis=0, keepdims=True)
    inv = 1.0 / (jnp.sqrt(total) + 1e-07)
    bufs[0] = g * (inv * inv)

    def step(k, carry):
        i, j, d, passes = (ints[4 * k + n] for n in range(4))

        def product(count):
            x = bufs[i]
            xh, xl = split(x)
            yh, yl = split(bufs[j])
            lhs = (xh, xl, xh)[:count]
            rhs = (yh, yh, yl)[:count]
            prod = mm(jnp.concatenate(lhs, axis=1), jnp.concatenate(rhs, axis=0))
            r0 = lax.broadcasted_iota(jnp.int32, (D, D), 0)
            r1 = lax.broadcasted_iota(jnp.int32, (D, D), 1)
            ident = jnp.where(r0 == r1, coeffs[3 * k + 2], 0.0)
            bufs[d] = coeffs[3 * k] * prod + (coeffs[3 * k + 1] * x + ident)

        for count in (1, 2, 3):
            pl.when(passes == count)(functools.partial(product, count))
        return carry

    lax.fori_loop(0, len(STEPS), step, 0)
    bufs[0] = bufs[2] * (inv * factor)

    def apply(b, carry):
        wh, wl = split(bufs[0])
        xs = [mat_ref[2 * b + i] for i in range(2)]

        def tall():
            for i in range(2):
                x = xs[i].astype(BF16)
                upd_ref[2 * b + i] = mm(
                    jnp.concatenate([x, x], axis=1), jnp.concatenate([wh, wl], axis=0)
                )

        def wide():
            x = jnp.concatenate([xs[0].astype(BF16), xs[1].astype(BF16)], axis=1)
            out = mm(jnp.concatenate([wh, wl], axis=1), jnp.concatenate([x, x], axis=0))
            upd_ref[2 * b] = out[:, :D]
            upd_ref[2 * b + 1] = out[:, D:]

        either(flipped, tall, wide)
        return carry

    lax.fori_loop(0, npairs, apply, 0)


def take_first(s_ref, chunks, dst):
    me, core, zed = s_ref[0], s_ref[1], s_ref[2]
    for c, ref in enumerate(chunks):
        for y in range(2):
            part = ((me // 2) ^ 1) ^ y
            rs = pl.ds(pl.multiple_of((core ^ c) * 192 + part * 96, 96), 96)
            for z in range(4):
                dst[zed ^ z, rs, :] = ref[y, z].astype(F32)


def take_second(s_ref, chunks, dst):
    me, core, zed = s_ref[0], s_ref[1], s_ref[2]
    for c, ref in enumerate(chunks):
        for m in range(4):
            rs = pl.ds(pl.multiple_of((core ^ c) * 192 + (me ^ m) * 48, 48), 48)
            for z in range(4):
                dst[zed ^ z, rs, :] = ref[m, z].astype(F32)


def adaln_grads(kept, grd, kf):
    ndev = 2 * kept[0].shape[0] // KEPT_ROWS
    for i, ref in enumerate(kept):
        n = ref.shape[0]
        for j in range(3):
            kf[j, i * n : (i + 1) * n, :] = ref[:, 128 * j : 128 * j + 128].astype(F32)

    def rows(first):
        part = [kf[j, pl.ds(first, ndev, stride=KEPT_ROWS), :] for j in range(3)]
        return jnp.concatenate(part, axis=1).astype(BF16)

    sil = jnp.concatenate([rows(12), rows(13)], axis=0)
    for b in range(6):
        gm = jnp.concatenate([rows(2 * b), rows(2 * b + 1)], axis=0)
        grd[b] = mm(sil, gm, 0, 0)


def add_momentum(t, target, mom, grd, mat, base=0):
    first = MATS[target][2]
    for _, block, r0, n, _, frow, stride in [p for p in shard_pieces(t, 4) if p[0] == target]:
        b = block - first
        for j in range(3):
            cs = slice(128 * j, 128 * j + 128)
            m = mom[pl.ds(frow + j, n, stride=stride), :]
            mat[b, r0 : r0 + n, cs] = MOMENTUM_RATE * m + grd[base + b, r0 : r0 + n, cs]


def add_foreign(s_ref, t, target, foreign, grd, mat):
    core = s_ref[1]
    half = foreign[0].shape[0]
    for _, block, r0, n, crow, _, _ in [p for p in shard_pieces(t ^ 1, 4) if p[0] == target]:
        b = block - MATS[target][2]
        cuts = sorted({crow, crow + n} | {c for c in (half,) if crow < c < crow + n})
        for lo, hi in zip(cuts[:-1], cuts[1:]):
            h = lo // half
            for mine, src in enumerate(foreign):

                @pl.when(core == (h ^ mine))
                def _(b=b, r0=r0, lo=lo, hi=hi, h=h, crow=crow, src=src):
                    dst = slice(r0 + lo - crow, r0 + hi - crow)
                    m = src[lo - h * half : hi - h * half, :].astype(F32)
                    mat[b, dst, :] = MOMENTUM_RATE * m + grd[b, dst, :]


TAIL = 48


def ns_a_kernel(s_ref, ints, coeffs, mom, fx0, fx1, kz0, kz1, ch0, ch1, upd, grd, tail, mat, bufs, kf):
    me = s_ref[0]

    @pl.when(me < 2)
    def _():
        adaln_grads((kz0, kz1), grd, kf)

    @pl.when(me >= 2)
    def _():
        take_first(s_ref, (ch0, ch1), grd)

    for t, target in enumerate((ADALN, ADALN, UP, DOWN)):

        @pl.when(me == t)
        def _(t=t, target=target):
            add_momentum(t, target, mom, grd, mat)
            if target != DOWN:
                add_foreign(s_ref, t, target, (fx0, fx1), grd, mat)

    npairs = jnp.where(me < 2, 3, 2)
    factor = jnp.where(me < 2, update_scale(ADALN), update_scale(UP))
    newton_schulz(ints, coeffs, mat, upd, bufs, npairs, me == 3, factor)

    for b in range(4):
        rs = slice(TAIL * b, TAIL * b + TAIL)
        tail[0, rs, :] = grd[b, D - TAIL :, :].astype(BF16)
        tail[1, rs, :] = upd[b, D - TAIL :, :].astype(BF16)


def ns_a(sidx, tables, mom, foreign, kept, chunks):
    sd = jax.ShapeDtypeStruct((6, D, D), F32)
    return pl.pallas_call(
        ns_a_kernel,
        out_shape=(sd, sd, jax.ShapeDtypeStruct((2, 4 * TAIL, D), BF16)),
        in_specs=[sspec()] * 3 + [vspec()] * 7,
        out_specs=(vspec(),) * 3,
        scratch_shapes=[
            pltpu.VMEM((6, D, D), F32),
            pltpu.VMEM((4, D, D), F32),
            pltpu.VMEM((3, 2 * kept[0].shape[0], 128), F32),
        ],
        compiler_params=params_of(26),
        cost_estimate=pl.CostEstimate(flops=8_000_000_000, bytes_accessed=12_000_000, transcendentals=0),
        name="ns_a",
    )(sidx, *tables, mom, *foreign, *kept, *chunks)


def final_kernel(
    s_ref, ints, coeffs, par, mom, ch0, ch1, upa, grda, tail, ograd, onew, omom, upb, gb, mat, bufs
):
    me = s_ref[0]
    inner = jnp.logical_or(me == 1, me == 2)

    @pl.when(inner)
    def _():
        take_second(s_ref, (ch0, ch1), gb)
        for b in range(1, 4):
            mat[b] = jnp.zeros((D, D), F32)

    @pl.when(me == 1)
    def _():
        add_momentum(1, QKV, mom, gb, mat)

    @pl.when(me == 2)
    def _():
        add_momentum(2, OUTW, mom, gb, mat, 3)

    @pl.when(inner)
    def _():
        npairs = jnp.where(me == 1, 2, 1)
        factor = jnp.where(me == 1, update_scale(QKV), update_scale(OUTW))
        newton_schulz(ints, coeffs, mat, upb, bufs, npairs, None, factor)

    for t in range(4):

        @pl.when(me == t)
        def _(t=t):
            for mat_id, block, r0, n, crow, frow, stride in shard_pieces(t, 4):
                b = block - MATS[mat_id][2]
                for j in range(3):
                    cs = slice(128 * j, 128 * j + 128)
                    fl = pl.ds(frow + j, n, stride=stride)
                    if mat_id == UP and t == 3:
                        assert r0 == D - TAIL and n == TAIL
                        g = tail[0, TAIL * b : TAIL * b + TAIL, cs].astype(F32)
                        u = tail[1, TAIL * b : TAIL * b + TAIL, cs].astype(F32)
                    elif mat_id in (QKV, OUTW):
                        g = gb[b + 3 * (mat_id == OUTW), r0 : r0 + n, cs]
                        u = upb[b, r0 : r0 + n, cs]
                    else:
                        g = grda[b, r0 : r0 + n, cs]
                        u = upa[b, r0 : r0 + n, cs]
                    ograd[fl, :] = g
                    omom[fl, :] = MOMENTUM_RATE * mom[fl, :] + g
                    onew[fl, :] = par[fl, :] - u


def final_call(sidx, tables, par, mom, chunks, upa, grda, tail):
    sd = jax.ShapeDtypeStruct(par.shape, F32)
    block4 = pltpu.VMEM((4, D, D), F32)
    return pl.pallas_call(
        final_kernel,
        out_shape=(sd, sd, sd),
        in_specs=[sspec()] * 3 + [vspec()] * 7,
        out_specs=(vspec(),) * 3,
        scratch_shapes=[block4, block4, block4, block4],
        compiler_params=params_of(38),
        cost_estimate=pl.CostEstimate(flops=8_000_000_000, bytes_accessed=24_000_000, transcendentals=0),
        name="finish",
    )(sidx, *tables, par, mom, *chunks, upa, grda, tail)


def swap(x, axis, mask):
    count = lax.axis_size(axis)
    return lax.ppermute(x, axis, [(i, i ^ mask) for i in range(count)])


def more_rows(x, hops):
    for axis, mask in hops:
        x = jnp.concatenate([x, swap(x, axis, mask)], axis=0)
    return x


def wide_sum(parts):
    total = None
    for p in parts:
        total = p.astype(F32) if total is None else total + p.astype(F32)
    return total


def at(x, i):
    return lax.dynamic_index_in_dim(x, i, 0, keepdims=False)


def z_scatter(s, zed, extra=None):
    size = s.shape[0] // 4
    blocks = s.reshape(4, size, D)
    got = []
    for m in (1, 2, 3):
        piece = at(blocks, zed ^ m).astype(BF16)
        if extra is not None:
            piece = jnp.concatenate([piece, extra], axis=0)
        got.append(swap(piece, "rep", 2 * m))
    total = wide_sum([at(blocks, zed)] + [g[:size] for g in got]).astype(BF16)
    if extra is None:
        return total
    return total, jnp.concatenate([extra] + [g[size:] for g in got], axis=0)


def fan(x, axis, masks):
    got = [x]
    for m in masks:
        got.append(swap(x, axis, m))
    return jnp.stack(got)


def fast_device(tokens, conditions, assignment, params, momentum, cotangent):
    return fast_body(tokens, conditions, assignment, params, momentum, cotangent)


def fast_body(tokens, conditions, assignment, params, momentum, cotangent):
    me = lax.axis_index("fsdp")
    rep = lax.axis_index("rep")
    core, zed = rep % 2, rep // 2
    lat = tokens.shape[0]
    rows = lat * SEQ
    par = params.reshape(-1, 128)
    mom = momentum.reshape(-1, 128)
    source = assignment // lat
    apart = ((source // 8) ^ me) + 4 * ((source % 8) ^ rep)
    pick = apart * lat + assignment % lat
    sidx = jnp.concatenate([jnp.stack([me, core, zed]), pick]).astype(jnp.int32)

    hop = swap(conditions, "fsdp", 1)
    wc, wh, mh = prep(sidx, par, mom, 4)
    table = jnp.concatenate([conditions, hop], axis=0)
    table, wh = lax.optimization_barrier((table, wh))
    hop = swap(table, "fsdp", 2)
    rx = swap(wh, "fsdp", 1)
    ry = swap(wh, "fsdp", 2)
    table = jnp.concatenate([table, hop], axis=0)
    table = more_rows(table, (("rep", 1), ("rep", 2), ("rep", 4)))
    rx, ry, table = lax.optimization_barrier((rx, ry, table))
    quarter = wh.shape[0] // 2
    rda, rdb = swap(rx[:quarter], "fsdp", 2), swap(ry[quarter:], "fsdp", 1)
    px, py = swap(rx, "rep", 1), swap(ry, "rep", 1)
    pda, pdb = swap(rda, "rep", 1), swap(rdb, "rep", 1)
    bufs = (wc, rx, ry, rda, rdb, px, py, pda, pdb)
    fx0 = swap(mh, "fsdp", 1)

    tok2, cot2 = tokens.reshape(rows, D), cotangent.reshape(rows, D)
    (blend, qkv, probs, ai, gafter, gmx, mods, gmod1, silu, wqkv, gout, keep1, send1) = main_call(
        sidx, table, tok2, cot2, bufs, True
    )
    fx1 = swap(fx0, "rep", 1)

    other = swap(send1, "rep", 1)
    gqkv = heads_call(qkv, probs, gmx)
    got = []
    for m in (1, 2, 3):
        got.append(swap((keep1[m] + other[m].astype(F32)).astype(BF16), "fsdp", m))
    gtok, keep2, send2, keep = input_call(sidx, tok2, gqkv, ai, gafter, mods, gmod1, silu, wqkv, gout)
    s1 = wide_sum([keep1[0] + other[0].astype(F32)] + got)
    col = fan(z_scatter(s1, zed), "rep", (2, 4, 6))
    pair = fan(col, "fsdp", (2,))
    pairs = (pair, swap(pair, "rep", 1))

    other = swap(send2, "rep", 1)
    got = []
    for m in (1, 2, 3):
        part = (keep2[m] + other[m].astype(F32)).astype(BF16)
        got.append(swap(jnp.concatenate([part, keep], axis=0), "fsdp", m))
    size = keep2.shape[1]
    s2 = wide_sum([keep2[0] + other[0].astype(F32)] + [g[:size] for g in got])
    q2, kz = z_scatter(s2, zed, jnp.concatenate([keep] + [g[size:] for g in got], axis=0))
    kept = (kz, swap(kz, "rep", 1))
    quad = fan(fan(q2, "rep", (2, 4, 6)), "fsdp", (1, 2, 3))
    quads = (quad, swap(quad, "rep", 1))

    tables = step_tables()
    upa, grda, tail = ns_a(sidx, tables, mom, (fx0, fx1), kept, pairs)
    tail = lax.ppermute(tail, "fsdp", [(2, 3)])
    ograd, onew, omom = final_call(sidx, tables, par, mom, quads, upa, grda, tail)
    shape = tokens.shape
    return (
        blend.reshape(shape),
        gtok.reshape(shape),
        ograd.reshape(-1),
        onew.reshape(-1),
        omom.reshape(-1),
    )


def unpack(flat):
    pieces, offset = [], 0
    for rows_count, cols_count, _, _ in MATS:
        pieces.append(flat[offset : offset + rows_count * cols_count].reshape(rows_count, cols_count))
        offset += rows_count * cols_count
    return pieces


def to_blocks(mats):
    out = []
    for matrix, (rows_count, cols_count, _, by_cols) in zip(mats, MATS):
        if by_cols:
            out.append(matrix.reshape(D, cols_count // D, D).transpose(1, 0, 2))
        else:
            out.append(matrix.reshape(rows_count // D, D, D))
    return jnp.concatenate(out, axis=0)


def from_blocks(blocks, by_cols):
    if by_cols:
        return blocks.transpose(1, 0, 2).reshape(-1)
    return blocks.reshape(-1)


def orthogonalize(matrix):
    flipped = matrix.shape[0] > matrix.shape[1]
    current = matrix.T if flipped else matrix
    current = current / (jnp.sqrt(jnp.sum(current * current)) + 1e-07)
    for _ in range(NS_ITERS):
        square = jnp.dot(current, current.T, precision=lax.Precision.HIGHEST)
        polynomial = COEFF_B * square + COEFF_C * jnp.dot(square, square, precision=lax.Precision.HIGHEST)
        current = COEFF_A * current + jnp.dot(polynomial, current, precision=lax.Precision.HIGHEST)
    return current.T if flipped else current


def scaled_update(matrix, factor):
    return (factor * orthogonalize(matrix)).reshape(-1)


def empty_update(matrix, factor):
    return jnp.zeros((matrix.shape[0] * matrix.shape[1],), F32)


def any_device(tokens, conditions, assignment, params, momentum, cotangent):
    lat = tokens.shape[0]
    rows = lat * SEQ
    table = lax.all_gather(conditions, ("fsdp", "rep"), axis=0, tiled=True)
    gathered = lax.all_gather(params.astype(BF16), "fsdp", axis=0, tiled=True)
    blocks = to_blocks(unpack(gathered))
    me = lax.axis_index("fsdp")
    sidx = jnp.concatenate([jnp.zeros((3,), jnp.int32), assignment.astype(jnp.int32)])
    tok2, cot2 = tokens.reshape(rows, D), cotangent.reshape(rows, D)
    (blend, qkv, probs, ai, gafter, gmx, mods, gmod1, silu, wqkv, gout, keep1, send1) = main_call(
        sidx, table, tok2, cot2, (blocks,), False
    )
    gqkv = heads_call(qkv, probs, gmx)
    gtok, keep2, send2, keep = input_call(sidx, tok2, gqkv, ai, gafter, mods, gmod1, silu, wqkv, gout)
    halves1 = jnp.stack([keep1, send1.astype(F32)]).reshape(2, 4, 4, 96, D)
    up = halves1[:, jnp.array([2, 0])].transpose(2, 0, 1, 3, 4).reshape(4, D, D)
    down = halves1[:, jnp.array([3, 1])].transpose(2, 0, 1, 3, 4).reshape(4, D, D)
    halves2 = jnp.stack([keep2, send2.astype(F32)]).reshape(2, 4, 4, 48, D)
    last = halves2.transpose(2, 0, 1, 3, 4).reshape(4, D, D)
    rest = jnp.concatenate(
        [from_blocks(last[:3], True), last[3].reshape(-1), from_blocks(up, True), down.reshape(-1)]
    )
    kept = lax.all_gather(keep, ("fsdp", "rep"), axis=0, tiled=True).reshape(-1, KEPT_ROWS, D)
    silu_all = kept[:, 6 * lat : 7 * lat].reshape(-1, D)
    mod_all = kept[:, : 6 * lat].reshape(-1, 6, lat, D).transpose(0, 2, 1, 3).reshape(-1, 6 * D)
    adaln = lax.dot_general(silu_all, mod_all, (((0,), (0,)), ((), ())), preferred_element_type=F32)
    shard_len = params.shape[0]
    head = jnp.concatenate([adaln.reshape(-1), jnp.zeros_like(rest)])
    flat = jnp.concatenate([jnp.zeros((D * 6 * D,), F32), rest])
    part = lax.psum_scatter(flat, "fsdp", scatter_dimension=0, tiled=True)
    full_grad = lax.psum(part, "rep") + lax.dynamic_slice_in_dim(head, me * shard_len, shard_len, 0)
    new_momentum = MOMENTUM_RATE * momentum + full_grad
    whole_mom = lax.all_gather(new_momentum, "fsdp", axis=0, tiled=True)
    group_size = lax.axis_size("fsdp")
    updates, offset = [], 0
    for mat, piece in enumerate(unpack(whole_mom)):
        factor = F32(update_scale(mat))
        owner = (offset // shard_len + group_size // 2) % group_size
        updates.append(lax.cond(me == owner, scaled_update, empty_update, piece, factor))
        offset += piece.size
    update = lax.psum_scatter(jnp.concatenate(updates), "fsdp", scatter_dimension=0, tiled=True)
    shape = tokens.shape
    return (blend.reshape(shape), gtok.reshape(shape), full_grad, params - update, new_momentum)


def solution(mesh):
    both = ("fsdp", "rep")
    in_specs = (P(both, None, None), P(both, None), P(both), P("fsdp"), P("fsdp"), P(both, None, None))
    out_specs = (P(both, None, None), P(both, None, None), P("fsdp"), P("fsdp"), P("fsdp"))
    small = dict(mesh.shape) == {"fsdp": 4, "rep": 8}
    return jax.shard_map(
        fast_device if small else any_device,
        mesh=mesh,
        in_specs=in_specs,
        out_specs=out_specs,
        check_vma=False,
    )
```

```python
import functools
import math

import jax
import jax.numpy as jnp
from jax import lax
from jax.experimental import pallas as pl
from jax.experimental.pallas import tpu as pltpu
from jax.sharding import PartitionSpec as P


D = 384
HEADS = 6
HD = 64
FF = 1536
SEQ = 256
NS_ITERS = 3

LN_EPSILON = 1e-06
MOMENTUM_RATE = 0.95
LEARN_RATE = 0.2
COEFF_A = 3.4445
COEFF_B = -4.775
COEFF_C = 2.0315

F32 = jnp.float32
BF16 = jnp.bfloat16
ANY = pl.ANY

MATS = ((D, 6 * D, 0, True), (D, 3 * D, 6, True), (D, D, 9, True), (D, FF, 10, True), (FF, D, 14, False))
NBLOCKS = 18
ADALN, QKV, OUTW, UP, DOWN = range(5)
P_SIZE = sum(m[0] * m[1] for m in MATS)
KEPT_ROWS = 16


def update_scale(mat):
    return LEARN_RATE * 0.2 * math.sqrt(max(MATS[mat][0], MATS[mat][1]))


def shard_pieces(shard, count):
    size = P_SIZE // count
    begin, end = shard * size, (shard + 1) * size
    pieces, crow, offset = [], 0, 0
    for mat, (rows, cols, first, by_cols) in enumerate(MATS):
        lo, hi = max(begin, offset), min(end, offset + rows * cols)
        if lo < hi:
            r0, r1 = (lo - offset) // cols, (hi - offset) // cols
            stride = cols // 128
            base = (offset - begin) // 128
            if by_cols:
                for b in range(cols // D):
                    pieces.append((mat, first + b, r0, r1 - r0, crow, base + r0 * stride + 3 * b, stride))
                    crow += r1 - r0
            else:
                r = r0
                while r < r1:
                    n = min(r1, (r // D + 1) * D) - r
                    pieces.append((mat, first + r // D, r % D, n, crow, base + r * stride, stride))
                    crow += n
                    r += n
        offset += rows * cols
    return pieces


def mm(a, b, ca=1, cb=0):
    return lax.dot_general(a, b, (((ca,), (cb,)), ((), ())), preferred_element_type=F32)


def vspec():
    return pl.BlockSpec(memory_space=pltpu.VMEM)


def aspec():
    return pl.BlockSpec(memory_space=ANY)


def sspec():
    return pl.BlockSpec(memory_space=pltpu.SMEM)


def params_of(mib):
    return pltpu.CompilerParams(vmem_limit_bytes=mib * 1024 * 1024)


def prep_kernel(count, s_ref, p_ref, w_ref, half_ref):
    for shard in range(count):

        @pl.when(s_ref[0] == shard)
        def _(shard=shard):
            for _, _, _, n, crow, frow, stride in shard_pieces(shard, count):
                for j in range(3):
                    src = pl.ds(frow + j, n, stride=stride)
                    w_ref[crow : crow + n, 128 * j : 128 * j + 128] = p_ref[src, :].astype(BF16)

    half = half_ref.shape[0]
    half_ref[...] = w_ref[pl.ds(pl.multiple_of(s_ref[1] * half, half), half), :]


def prep(sidx, flat, count):
    rows = P_SIZE // count // D
    out = (jax.ShapeDtypeStruct((rows, D), BF16), jax.ShapeDtypeStruct((rows // 2, D), BF16))
    return pl.pallas_call(
        functools.partial(prep_kernel, count),
        out_shape=out,
        in_specs=[sspec(), vspec()],
        out_specs=(vspec(), vspec()),
        compiler_params=params_of(4),
        cost_estimate=pl.CostEstimate(flops=0, bytes_accessed=4_000_000, transcendentals=0),
        name="prep",
    )(sidx, flat)


def layer_norm(h):
    center = jnp.mean(h, axis=-1, keepdims=True)
    cent = h - center
    spread = jnp.mean(jnp.square(cent), axis=-1, keepdims=True)
    rstd = lax.rsqrt(spread + LN_EPSILON)
    return cent * rstd, rstd


def layer_norm_grad(xhat, rstd, gx):
    m1 = jnp.mean(gx, axis=-1, keepdims=True)
    m2 = jnp.mean(gx * xhat, axis=-1, keepdims=True)
    return rstd * (gx - m1 - xhat * m2)


def gather_plan(count):
    plan = []
    half = P_SIZE // count // D // 2
    for shard in range(count):
        for _, block, r0, n, crow, _, _ in shard_pieces(shard, count):
            cuts = sorted({crow, crow + n} | {c for c in range(0, 2 * half + 1, half // 2) if crow < c < crow + n})
            for a, b in zip(cuts[:-1], cuts[1:]):
                plan.append((shard, a // half, a % half, b - a, block, r0 + a - crow))
    return plan


def load_weights_fast(s_ref, bufs, wts, own_ready):
    own, rx, ry, rda, rdb, px, py, pda, pdb = bufs
    me, core = s_ref[0], s_ref[1]
    half = own.shape[0] // 2
    quarter = half // 2
    plan = gather_plan(4)

    def move(src, row, n, block, brow):
        size = 96 if n % 96 == 0 else 48

        def chunk(i, carry):
            a = pl.multiple_of(row + i * size, 16)
            b = pl.multiple_of(brow + i * size, 16)
            wts[block, pl.ds(b, size), :] = src[pl.ds(a, size), :]
            return carry

        lax.fori_loop(0, n // size, chunk, 0)

    for shard in range(4):
        for h in range(2):
            pieces = [p for p in plan if p[0] == shard and p[1] == h]
            for m in (1, 2, 3):
                for mine in (True, False):

                    @pl.when(jnp.logical_and(me == (shard ^ m), (core == h) if mine else (core != h)))
                    def _(pieces=pieces, m=m, mine=mine):
                        for _, _, r, n, block, br in pieces:
                            if m < 3:
                                move(((rx, ry) if mine else (px, py))[m - 1], r, n, block, br)
                            else:
                                k = r // quarter
                                pair = (rda, rdb) if mine else (pda, pdb)
                                move(pair[k], r - k * quarter, n, block, br)

    own_ready()
    for shard in range(4):

        @pl.when(me == shard)
        def _(shard=shard):
            for _, h, r, n, block, br in [p for p in plan if p[0] == shard]:
                move(own, h * half + r, n, block, br)


def by_core(value, core):
    half = value.shape[0] // 2
    top, bottom = value[:half], value[half:]
    return jnp.where(core == 0, top, bottom), jnp.where(core == 0, bottom, top)


def main_kernel(nbuf, fast, rows, s_ref, table, tok_hbm, cot_hbm, *refs):
    bufs = refs[:nbuf]
    (blend, qkv, probs, amix_in, gafter, gmx, mods, gmod, silu, wqkv, gout, keep1, send1) = refs[nbuf : nbuf + 13]
    wts, ao_s, aa_s, amix, minp, gmi, mo, tok, cot, own, sems = refs[nbuf + 13 :]
    lat = rows // SEQ
    get_tok = pltpu.make_async_copy(tok_hbm, tok, sems.at[1])
    get_cot = pltpu.make_async_copy(cot_hbm, cot, sems.at[2])
    first = pltpu.make_async_copy(bufs[0], own if fast else wts, sems.at[0])
    first.start()
    get_tok.start()
    get_cot.start()
    if fast:
        load_weights_fast(s_ref, (own,) + bufs[1:], wts, first.wait)
    else:
        first.wait()
    get_tok.wait()
    get_cot.wait()
    nt = table.shape[0]
    lanes = lax.broadcasted_iota(jnp.int32, (16, nt), 1)
    rws = lax.broadcasted_iota(jnp.int32, (16, nt), 0)
    pick = jnp.zeros((16, nt), jnp.bool_)
    for l in range(lat):
        pick = pick | ((rws == l) & (lanes == s_ref[3 + l]))
    cond = mm(pick.astype(F32).astype(BF16), table[...])
    sc = (cond * (1.0 / (1.0 + jnp.exp(-cond)))).astype(BF16)
    silu[...] = sc.astype(F32)
    for b in range(6):
        mods[b] = mm(sc, wts[b])[:8]
    for j in range(3):
        wqkv[j] = wts[6 + j]

    def mod(b, l):
        return mods[b, l : l + 1, :]

    for l in range(lat):
        rs = slice(l * SEQ, (l + 1) * SEQ)
        xhat, _ = layer_norm(tok[rs, :].astype(F32))
        amix_in[rs, :] = (xhat * (1.0 + mod(1, l)) + mod(0, l)).astype(BF16)
    ai = amix_in[...]
    for j in range(3):
        qkv[j] = mm(ai, wts[6 + j]).astype(BF16)

    low = lax.broadcasted_iota(jnp.int32, (SEQ, 128), 1) < HD
    zero = jnp.zeros((SEQ, 128), BF16)

    def attend(l, carry):
        rs = pl.ds(pl.multiple_of(l * SEQ, SEQ), SEQ)
        for hp in range(HEADS // 2):
            cs = slice(hp * 128, hp * 128 + 128)
            q, k, v = qkv[0, rs, cs], qkv[1, rs, cs], qkv[2, rs, cs]
            outs = []
            for h in range(2):
                qm = jnp.where(low if h == 0 else jnp.logical_not(low), q, zero)
                s = mm(qm, k, 1, 1) * HD ** (-0.5)
                top = jnp.max(s, axis=-1, keepdims=True)
                e = jnp.exp(s - top)
                pr = e * (1.0 / jnp.sum(e, axis=-1, keepdims=True))
                probs[l * HEADS + hp * 2 + h] = pr
                outs.append(mm(pr.astype(BF16), v))
            amix[rs, cs] = jnp.where(low, outs[0], outs[1]).astype(BF16)
        return carry

    lax.fori_loop(0, lat, attend, 0)

    ao = mm(amix[...], wts[9])
    ao_s[...] = ao
    for l in range(lat):
        rs = slice(l * SEQ, (l + 1) * SEQ)
        aa = tok[rs, :].astype(F32) + mod(2, l) * ao_s[rs, :]
        aa_s[rs, :] = aa
        xhat, _ = layer_norm(aa)
        minp[rs, :] = (xhat * (1.0 + mod(4, l)) + mod(3, l)).astype(BF16)
        gmx[rs, :] = (cot[rs, :].astype(F32) * mod(5, l)).astype(BF16)
    gmi[...] = jnp.zeros_like(gmi)
    mo[...] = jnp.zeros_like(mo)

    me, core = s_ref[0], s_ref[1]

    def put(value, members, j):
        mine, other = by_core(value, core)
        for i, member in enumerate(members):
            rs = pl.ds(pl.multiple_of(j * 96, 96), 96)
            keep1[member ^ me, rs, :] = mine[96 * i : 96 * i + 96]
            send1[member ^ me, rs, :] = other[96 * i : 96 * i + 96].astype(BF16)

    def mlp(j, carry):
        wu, wd = wts[10 + j], wts[14 + j]
        u = mm(minp[...], wu)
        c = math.sqrt(2.0 / math.pi)
        u2 = u * u
        t = jnp.tanh(c * (u + 0.044715 * (u2 * u)))
        half = 0.5 * (1.0 + t)
        act = (u * half).astype(BF16)
        slope = half + 0.5 * u * (1.0 - t * t) * (c * (1.0 + 3.0 * 0.044715 * u2))
        mo[...] += mm(act, wd)
        gmo = gmx[...]
        gp = (mm(gmo, wd, 1, 1) * slope).astype(BF16)
        put(mm(act, gmo, 0, 0), (3, 1), j)
        put(mm(minp[...], gp, 0, 0), (2, 0), j)
        gmi[...] += mm(gp, wu, 1, 1)
        return carry

    lax.fori_loop(0, FF // D, mlp, 0)

    gmod[...] = jnp.zeros_like(gmod)
    for l in range(lat):
        rs = slice(l * SEQ, (l + 1) * SEQ)
        up = cot[rs, :].astype(F32)
        blend[rs, :] = (aa_s[rs, :] + mod(5, l) * mo[rs, :]).astype(BF16)
        gmod[5, l : l + 1, :] = jnp.sum(up * mo[rs, :], axis=0, keepdims=True)
        xhat, rstd = layer_norm(aa_s[rs, :])
        g = gmi[rs, :]
        gmod[3, l : l + 1, :] = jnp.sum(g, axis=0, keepdims=True)
        gmod[4, l : l + 1, :] = jnp.sum(g * xhat, axis=0, keepdims=True)
        ga = up + layer_norm_grad(xhat, rstd, g * (1.0 + mod(4, l)))
        gafter[rs, :] = ga
        gmod[2, l : l + 1, :] = jnp.sum(ga * ao_s[rs, :], axis=0, keepdims=True)
        minp[rs, :] = (ga * mod(2, l)).astype(BF16)
    gao = minp[...]
    gout[...] = mm(amix[...], gao, 0, 0)
    gmx[...] = mm(gao, wts[9], 1, 1).astype(BF16)


def main_call(sidx, table, tokens, cotangent, bufs, fast):
    rows = tokens.shape[0]
    lat = rows // SEQ
    sd = jax.ShapeDtypeStruct
    outs = (
        sd((rows, D), BF16),
        sd((3, rows, D), BF16),
        sd((lat * HEADS, SEQ, SEQ), F32),
        sd((rows, D), BF16),
        sd((rows, D), F32),
        sd((rows, D), BF16),
        sd((6, 8, D), F32),
        sd((6, 8, D), F32),
        sd((16, D), F32),
        sd((3, D, D), BF16),
        sd((D, D), F32),
        sd((4, D, D), F32),
        sd((4, D, D), BF16),
    )
    return pl.pallas_call(
        functools.partial(main_kernel, len(bufs), fast, rows),
        out_shape=outs,
        in_specs=[sspec(), vspec(), aspec(), aspec(), aspec()] + [vspec()] * (len(bufs) - 1),
        out_specs=(vspec(),) * len(outs),
        scratch_shapes=[
            pltpu.VMEM((NBLOCKS, D, D), BF16),
            pltpu.VMEM((rows, D), F32),
            pltpu.VMEM((rows, D), F32),
            pltpu.VMEM((rows, D), BF16),
            pltpu.VMEM((rows, D), BF16),
            pltpu.VMEM((rows, D), F32),
            pltpu.VMEM((rows, D), F32),
            pltpu.VMEM((rows, D), BF16),
            pltpu.VMEM((rows, D), BF16),
            pltpu.VMEM(bufs[0].shape if fast else (16, D), BF16),
            pltpu.SemaphoreType.DMA((3,)),
        ],
        compiler_params=params_of(20),
        cost_estimate=pl.CostEstimate(flops=20_000_000_000, bytes_accessed=30_000_000, transcendentals=0),
        name="main",
    )(sidx, table, tokens, cotangent, *bufs)


def heads_kernel(rows, qkv, probs, gmx, gqkv):
    lat = rows // SEQ
    low = lax.broadcasted_iota(jnp.int32, (SEQ, 128), 1) < HD
    zero = jnp.zeros((SEQ, 128), BF16)

    def back(l, carry):
        rs = pl.ds(pl.multiple_of(l * SEQ, SEQ), SEQ)
        for hp in range(HEADS // 2):
            cs = slice(hp * 128, hp * 128 + 128)
            q, k, v = qkv[0, rs, cs], qkv[1, rs, cs], qkv[2, rs, cs]
            g = gmx[rs, cs]
            res = []
            for h in range(2):
                p = probs[l * HEADS + hp * 2 + h]
                gm = jnp.where(low if h == 0 else jnp.logical_not(low), g, zero)
                gv = mm(p.astype(BF16), g, 0, 0)
                gpr = mm(gm, v, 1, 1)
                dots = jnp.sum(p * gpr, axis=-1, keepdims=True)
                gs = (p * (gpr - dots) * HD ** (-0.5)).astype(BF16)
                res.append((mm(gs, k), mm(gs, q, 0, 0), gv))
            for j in range(3):
                gqkv[j, rs, cs] = jnp.where(low, res[0][j], res[1][j]).astype(BF16)
        return carry

    lax.fori_loop(0, lat, back, 0)


def heads_call(qkv, probs, gmx):
    rows = gmx.shape[0]
    return pl.pallas_call(
        functools.partial(heads_kernel, rows),
        out_shape=jax.ShapeDtypeStruct((3, rows, D), BF16),
        in_specs=[vspec()] * 3,
        out_specs=vspec(),
        compiler_params=params_of(4),
        cost_estimate=pl.CostEstimate(flops=6_000_000_000, bytes_accessed=6_000_000, transcendentals=0),
        name="heads",
    )(qkv, probs, gmx)


def input_kernel(rows, s_ref, tok, gqkv, ai, gafter, mods, gmod1, silu, wqkv, gout, gtok, keep2, send2, keep, srow):
    me, core = s_ref[0], s_ref[1]
    lat = rows // SEQ
    gai = None
    for j in range(4):
        if j < 3:
            part = mm(gqkv[j], wqkv[j], 1, 1)
            gai = part if gai is None else gai + part
            value = mm(ai[...], gqkv[j], 0, 0)
        else:
            value = gout[...]
        mine, other = by_core(value, core)
        for m in range(4):
            rs = slice(48 * j, 48 * j + 48)
            keep2[m ^ me, rs, :] = mine[48 * m : 48 * m + 48]
            send2[m ^ me, rs, :] = other[48 * m : 48 * m + 48].astype(BF16)
    srow[...] = jnp.zeros_like(srow)
    for l in range(lat):
        rs = slice(l * SEQ, (l + 1) * SEQ)
        xhat, rstd = layer_norm(tok[rs, :].astype(F32))
        g = gai[rs, :]
        srow[l : l + 1, :] = jnp.sum(g, axis=0, keepdims=True)
        srow[lat + l : lat + l + 1, :] = jnp.sum(g * xhat, axis=0, keepdims=True)
        gtok[rs, :] = gafter[rs, :] + layer_norm_grad(xhat, rstd, g * (1.0 + mods[1, l : l + 1, :]))
        for b in range(2, 6):
            srow[lat * b + l : lat * b + l + 1, :] = gmod1[b, l : l + 1, :]
        srow[lat * 6 + l : lat * 6 + l + 1, :] = silu[l : l + 1, :]
    keep[...] = srow[...].astype(BF16)


def input_call(sidx, tokens, gqkv, ai, gafter, mods, gmod1, silu, wqkv, gout):
    rows = tokens.shape[0]
    sd = jax.ShapeDtypeStruct
    outs = (sd((rows, D), F32), sd((4, D // 2, D), F32), sd((4, D // 2, D), BF16), sd((KEPT_ROWS, D), BF16))
    return pl.pallas_call(
        functools.partial(input_kernel, rows),
        out_shape=outs,
        in_specs=[sspec()] + [vspec()] * 9,
        out_specs=(vspec(),) * 4,
        scratch_shapes=[pltpu.VMEM((KEPT_ROWS, D), F32)],
        compiler_params=params_of(6),
        cost_estimate=pl.CostEstimate(flops=6_000_000_000, bytes_accessed=6_000_000, transcendentals=0),
        name="input",
    )(sidx, tokens, gqkv, ai, gafter, mods, gmod1, silu, wqkv, gout)


def split(x):
    hi = x.astype(BF16)
    return hi, (x - hi.astype(F32)).astype(BF16)


POLY = (COEFF_C, COEFF_B, COEFF_A)
PLAIN = (1.0, 0.0, 0.0)
STEPS = (
    (0, 0, 2, 1, POLY),
    (2, 0, 3, 2, PLAIN),
    (3, 2, 0, 2, PLAIN),
    (0, 0, 1, 1, POLY),
    (1, 2, 2, 3, PLAIN),
    (1, 0, 3, 2, PLAIN),
    (3, 1, 0, 2, PLAIN),
    (0, 0, 1, 3, POLY),
    (1, 2, 2, 3, PLAIN),
)


def step_tables():
    ints = jnp.array([x for st in STEPS for x in st[:4]], jnp.int32)
    coeffs = jnp.array([x for st in STEPS for x in st[4]], F32)
    return ints, coeffs


def either(flipped, tall, wide):
    if flipped is None:
        wide()
    else:
        pl.when(flipped)(tall)
        pl.when(jnp.logical_not(flipped))(wide)


def newton_schulz(ints, coeffs, mat_ref, upd_ref, bufs, npairs, flipped, factor):
    bufs[0] = jnp.zeros((D, D), F32)

    def gram(b, carry):
        x0, x1 = mat_ref[2 * b].astype(BF16), mat_ref[2 * b + 1].astype(BF16)

        def tall():
            x = jnp.concatenate([x0, x1], axis=0)
            bufs[0] += mm(x, x, 0, 0)

        def wide():
            x = jnp.concatenate([x0, x1], axis=1)
            bufs[0] += mm(x, x, 1, 1)

        either(flipped, tall, wide)

        return carry

    lax.fori_loop(0, npairs, gram, 0)
    g = bufs[0]
    ri = lax.broadcasted_iota(jnp.int32, (D, D), 0)
    ci = lax.broadcasted_iota(jnp.int32, (D, D), 1)
    eye = jnp.where(ri == ci, 1.0, 0.0)
    diag = jnp.sum(g * eye, axis=1, keepdims=True)
    total = jnp.sum(diag, axis=0, keepdims=True)
    inv = 1.0 / (jnp.sqrt(total) + 1e-07)
    bufs[0] = g * (inv * inv)

    def step(k, carry):
        i, j, d, passes = (ints[4 * k + n] for n in range(4))

        def product(count):
            x = bufs[i]
            xh, xl = split(x)
            yh, yl = split(bufs[j])
            lhs = (xh, xl, xh)[:count]
            rhs = (yh, yh, yl)[:count]
            prod = mm(jnp.concatenate(lhs, axis=1), jnp.concatenate(rhs, axis=0))
            r0 = lax.broadcasted_iota(jnp.int32, (D, D), 0)
            r1 = lax.broadcasted_iota(jnp.int32, (D, D), 1)
            ident = jnp.where(r0 == r1, coeffs[3 * k + 2], 0.0)
            bufs[d] = coeffs[3 * k] * prod + (coeffs[3 * k + 1] * x + ident)

        for count in (1, 2, 3):
            pl.when(passes == count)(functools.partial(product, count))
        return carry

    lax.fori_loop(0, len(STEPS), step, 0)
    bufs[0] = bufs[2] * (inv * factor)

    def apply(b, carry):
        wh, wl = split(bufs[0])
        xs = [mat_ref[2 * b + i] for i in range(2)]

        def tall():
            for i in range(2):
                x = xs[i].astype(BF16)
                upd_ref[2 * b + i] = mm(
                    jnp.concatenate([x, x], axis=1), jnp.concatenate([wh, wl], axis=0)
                )

        def wide():
            x = jnp.concatenate([xs[0].astype(BF16), xs[1].astype(BF16)], axis=1)
            out = mm(jnp.concatenate([wh, wl], axis=1), jnp.concatenate([x, x], axis=0))
            upd_ref[2 * b] = out[:, :D]
            upd_ref[2 * b + 1] = out[:, D:]

        either(flipped, tall, wide)
        return carry

    lax.fori_loop(0, npairs, apply, 0)


def take_first(s_ref, chunks, dst):
    me, core, zed = s_ref[0], s_ref[1], s_ref[2]
    for c, ref in enumerate(chunks):
        for y in range(2):
            part = ((me // 2) ^ 1) ^ y
            rs = pl.ds(pl.multiple_of((core ^ c) * 192 + part * 96, 96), 96)
            for z in range(4):
                dst[zed ^ z, rs, :] = ref[y, z].astype(F32)


def take_second(s_ref, chunks, dst):
    me, core, zed = s_ref[0], s_ref[1], s_ref[2]
    for c, ref in enumerate(chunks):
        for m in range(4):
            rs = pl.ds(pl.multiple_of((core ^ c) * 192 + (me ^ m) * 48, 48), 48)
            for z in range(4):
                dst[zed ^ z, rs, :] = ref[m, z].astype(F32)


def adaln_grads(kept, grd, kf):
    ndev = 2 * kept[0].shape[0] // KEPT_ROWS
    for i, ref in enumerate(kept):
        n = ref.shape[0]
        for j in range(3):
            kf[j, i * n : (i + 1) * n, :] = ref[:, 128 * j : 128 * j + 128].astype(F32)

    def rows(first):
        part = [kf[j, pl.ds(first, ndev, stride=KEPT_ROWS), :] for j in range(3)]
        return jnp.concatenate(part, axis=1).astype(BF16)

    sil = jnp.concatenate([rows(12), rows(13)], axis=0)
    for b in range(6):
        gm = jnp.concatenate([rows(2 * b), rows(2 * b + 1)], axis=0)
        grd[b] = mm(sil, gm, 0, 0)


def add_momentum(t, target, mom, grd, mat, base=0):
    first = MATS[target][2]
    for _, block, r0, n, _, frow, stride in [p for p in shard_pieces(t, 4) if p[0] == target]:
        b = block - first
        for j in range(3):
            cs = slice(128 * j, 128 * j + 128)
            m = mom[pl.ds(frow + j, n, stride=stride), :]
            mat[b, r0 : r0 + n, cs] = MOMENTUM_RATE * m + grd[base + b, r0 : r0 + n, cs]


def add_foreign(s_ref, t, target, foreign, grd, mat):
    core = s_ref[1]
    half = foreign[0].shape[0]
    for _, block, r0, n, crow, _, _ in [p for p in shard_pieces(t ^ 1, 4) if p[0] == target]:
        b = block - MATS[target][2]
        cuts = sorted({crow, crow + n} | {c for c in (half,) if crow < c < crow + n})
        for lo, hi in zip(cuts[:-1], cuts[1:]):
            h = lo // half
            for mine, src in enumerate(foreign):

                @pl.when(core == (h ^ mine))
                def _(b=b, r0=r0, lo=lo, hi=hi, h=h, crow=crow, src=src):
                    dst = slice(r0 + lo - crow, r0 + hi - crow)
                    m = src[lo - h * half : hi - h * half, :].astype(F32)
                    mat[b, dst, :] = MOMENTUM_RATE * m + grd[b, dst, :]


TAIL = 48


def ns_a_kernel(s_ref, ints, coeffs, mom, fx0, fx1, kz0, kz1, ch0, ch1, upd, grd, tail, mat, bufs, kf):
    me = s_ref[0]

    @pl.when(me < 2)
    def _():
        adaln_grads((kz0, kz1), grd, kf)

    @pl.when(me >= 2)
    def _():
        take_first(s_ref, (ch0, ch1), grd)

    for t, target in enumerate((ADALN, ADALN, UP, DOWN)):

        @pl.when(me == t)
        def _(t=t, target=target):
            add_momentum(t, target, mom, grd, mat)
            if target != DOWN:
                add_foreign(s_ref, t, target, (fx0, fx1), grd, mat)

    npairs = jnp.where(me < 2, 3, 2)
    factor = jnp.where(me < 2, update_scale(ADALN), update_scale(UP))
    newton_schulz(ints, coeffs, mat, upd, bufs, npairs, me == 3, factor)

    for b in range(4):
        rs = slice(TAIL * b, TAIL * b + TAIL)
        tail[0, rs, :] = grd[b, D - TAIL :, :].astype(BF16)
        tail[1, rs, :] = upd[b, D - TAIL :, :].astype(BF16)


def ns_a(sidx, tables, mom, foreign, kept, chunks):
    sd = jax.ShapeDtypeStruct((6, D, D), F32)
    return pl.pallas_call(
        ns_a_kernel,
        out_shape=(sd, sd, jax.ShapeDtypeStruct((2, 4 * TAIL, D), BF16)),
        in_specs=[sspec()] * 3 + [vspec()] * 7,
        out_specs=(vspec(),) * 3,
        scratch_shapes=[
            pltpu.VMEM((6, D, D), F32),
            pltpu.VMEM((4, D, D), F32),
            pltpu.VMEM((3, 2 * kept[0].shape[0], 128), F32),
        ],
        compiler_params=params_of(14),
        cost_estimate=pl.CostEstimate(flops=8_000_000_000, bytes_accessed=12_000_000, transcendentals=0),
        name="ns_a",
    )(sidx, *tables, mom, *foreign, *kept, *chunks)


def final_kernel(
    s_ref, ints, coeffs, par, mom, ch0, ch1, upa, grda, tail, ograd, onew, omom, upb, gb, mat, bufs
):
    me = s_ref[0]
    inner = jnp.logical_or(me == 1, me == 2)

    @pl.when(inner)
    def _():
        take_second(s_ref, (ch0, ch1), gb)
        for b in range(1, 4):
            mat[b] = jnp.zeros((D, D), F32)

    @pl.when(me == 1)
    def _():
        add_momentum(1, QKV, mom, gb, mat)

    @pl.when(me == 2)
    def _():
        add_momentum(2, OUTW, mom, gb, mat, 3)

    @pl.when(inner)
    def _():
        npairs = jnp.where(me == 1, 2, 1)
        factor = jnp.where(me == 1, update_scale(QKV), update_scale(OUTW))
        newton_schulz(ints, coeffs, mat, upb, bufs, npairs, None, factor)

    for t in range(4):

        @pl.when(me == t)
        def _(t=t):
            for mat_id, block, r0, n, crow, frow, stride in shard_pieces(t, 4):
                b = block - MATS[mat_id][2]
                for j in range(3):
                    cs = slice(128 * j, 128 * j + 128)
                    fl = pl.ds(frow + j, n, stride=stride)
                    if mat_id == UP and t == 3:
                        assert r0 == D - TAIL and n == TAIL
                        g = tail[0, TAIL * b : TAIL * b + TAIL, cs].astype(F32)
                        u = tail[1, TAIL * b : TAIL * b + TAIL, cs].astype(F32)
                    elif mat_id in (QKV, OUTW):
                        g = gb[b + 3 * (mat_id == OUTW), r0 : r0 + n, cs]
                        u = upb[b, r0 : r0 + n, cs]
                    else:
                        g = grda[b, r0 : r0 + n, cs]
                        u = upa[b, r0 : r0 + n, cs]
                    ograd[fl, :] = g
                    omom[fl, :] = MOMENTUM_RATE * mom[fl, :] + g
                    onew[fl, :] = par[fl, :] - u


def final_call(sidx, tables, par, mom, chunks, upa, grda, tail):
    sd = jax.ShapeDtypeStruct(par.shape, F32)
    block4 = pltpu.VMEM((4, D, D), F32)
    return pl.pallas_call(
        final_kernel,
        out_shape=(sd, sd, sd),
        in_specs=[sspec()] * 3 + [vspec()] * 7,
        out_specs=(vspec(),) * 3,
        scratch_shapes=[block4, block4, block4, block4],
        compiler_params=params_of(20),
        cost_estimate=pl.CostEstimate(flops=8_000_000_000, bytes_accessed=24_000_000, transcendentals=0),
        name="finish",
    )(sidx, *tables, par, mom, *chunks, upa, grda, tail)


def swap(x, axis, mask):
    count = lax.axis_size(axis)
    return lax.ppermute(x, axis, [(i, i ^ mask) for i in range(count)])


def more_rows(x, hops):
    for axis, mask in hops:
        x = jnp.concatenate([x, swap(x, axis, mask)], axis=0)
    return x


def wide_sum(parts):
    total = None
    for p in parts:
        total = p.astype(F32) if total is None else total + p.astype(F32)
    return total


def at(x, i):
    return lax.dynamic_index_in_dim(x, i, 0, keepdims=False)


def z_scatter(s, zed, extra=None):
    size = s.shape[0] // 4
    blocks = s.reshape(4, size, D)
    got = []
    for m in (1, 2, 3):
        piece = at(blocks, zed ^ m).astype(BF16)
        if extra is not None:
            piece = jnp.concatenate([piece, extra], axis=0)
        got.append(swap(piece, "rep", 2 * m))
    total = wide_sum([at(blocks, zed)] + [g[:size] for g in got]).astype(BF16)
    if extra is None:
        return total
    return total, jnp.concatenate([extra] + [g[size:] for g in got], axis=0)


def fan(x, axis, masks):
    got = [x]
    for m in masks:
        got.append(swap(x, axis, m))
    return jnp.stack(got)


def fast_device(tokens, conditions, assignment, params, momentum, cotangent):
    return fast_body(tokens, conditions, assignment, params, momentum, cotangent)


def fast_body(tokens, conditions, assignment, params, momentum, cotangent):
    me = lax.axis_index("fsdp")
    rep = lax.axis_index("rep")
    core, zed = rep % 2, rep // 2
    lat = tokens.shape[0]
    rows = lat * SEQ
    par = params.reshape(-1, 128)
    mom = momentum.reshape(-1, 128)
    source = assignment // lat
    apart = ((source // 8) ^ me) + 4 * ((source % 8) ^ rep)
    pick = apart * lat + assignment % lat
    sidx = jnp.concatenate([jnp.stack([me, core, zed]), pick]).astype(jnp.int32)

    hop = swap(conditions, "fsdp", 1)
    wc, wh = prep(sidx, par, 4)
    table = jnp.concatenate([conditions, hop], axis=0)
    table, wh = lax.optimization_barrier((table, wh))
    hop = swap(table, "fsdp", 2)
    rx = swap(wh, "fsdp", 1)
    ry = swap(wh, "fsdp", 2)
    table = jnp.concatenate([table, hop], axis=0)
    table = more_rows(table, (("rep", 1), ("rep", 2), ("rep", 4)))
    rx, ry, table = lax.optimization_barrier((rx, ry, table))
    quarter = wh.shape[0] // 2
    rda, rdb = swap(rx[:quarter], "fsdp", 2), swap(ry[quarter:], "fsdp", 1)
    px, py = swap(rx, "rep", 1), swap(ry, "rep", 1)
    pda, pdb = swap(rda, "rep", 1), swap(rdb, "rep", 1)
    bufs = (wc, rx, ry, rda, rdb, px, py, pda, pdb)
    _, mh = prep(sidx, mom, 4)
    fx0 = swap(mh, "fsdp", 1)

    tok2, cot2 = tokens.reshape(rows, D), cotangent.reshape(rows, D)
    (blend, qkv, probs, ai, gafter, gmx, mods, gmod1, silu, wqkv, gout, keep1, send1) = main_call(
        sidx, table, tok2, cot2, bufs, True
    )
    fx1 = swap(fx0, "rep", 1)

    other = swap(send1, "rep", 1)
    gqkv = heads_call(qkv, probs, gmx)
    got = []
    for m in (1, 2, 3):
        got.append(swap((keep1[m] + other[m].astype(F32)).astype(BF16), "fsdp", m))
    gtok, keep2, send2, keep = input_call(sidx, tok2, gqkv, ai, gafter, mods, gmod1, silu, wqkv, gout)
    s1 = wide_sum([keep1[0] + other[0].astype(F32)] + got)
    col = fan(z_scatter(s1, zed), "rep", (2, 4, 6))
    pair = fan(col, "fsdp", (2,))
    pairs = (pair, swap(pair, "rep", 1))

    other = swap(send2, "rep", 1)
    got = []
    for m in (1, 2, 3):
        part = (keep2[m] + other[m].astype(F32)).astype(BF16)
        got.append(swap(jnp.concatenate([part, keep], axis=0), "fsdp", m))
    size = keep2.shape[1]
    s2 = wide_sum([keep2[0] + other[0].astype(F32)] + [g[:size] for g in got])
    q2, kz = z_scatter(s2, zed, jnp.concatenate([keep] + [g[size:] for g in got], axis=0))
    kept = (kz, swap(kz, "rep", 1))
    quad = fan(fan(q2, "rep", (2, 4, 6)), "fsdp", (1, 2, 3))
    quads = (quad, swap(quad, "rep", 1))

    tables = step_tables()
    upa, grda, tail = ns_a(sidx, tables, mom, (fx0, fx1), kept, pairs)
    tail = lax.ppermute(tail, "fsdp", [(2, 3)])
    ograd, onew, omom = final_call(sidx, tables, par, mom, quads, upa, grda, tail)
    shape = tokens.shape
    return (
        blend.reshape(shape),
        gtok.reshape(shape),
        ograd.reshape(-1),
        onew.reshape(-1),
        omom.reshape(-1),
    )


def unpack(flat):
    pieces, offset = [], 0
    for rows_count, cols_count, _, _ in MATS:
        pieces.append(flat[offset : offset + rows_count * cols_count].reshape(rows_count, cols_count))
        offset += rows_count * cols_count
    return pieces


def to_blocks(mats):
    out = []
    for matrix, (rows_count, cols_count, _, by_cols) in zip(mats, MATS):
        if by_cols:
            out.append(matrix.reshape(D, cols_count // D, D).transpose(1, 0, 2))
        else:
            out.append(matrix.reshape(rows_count // D, D, D))
    return jnp.concatenate(out, axis=0)


def from_blocks(blocks, by_cols):
    if by_cols:
        return blocks.transpose(1, 0, 2).reshape(-1)
    return blocks.reshape(-1)


def orthogonalize(matrix):
    flipped = matrix.shape[0] > matrix.shape[1]
    current = matrix.T if flipped else matrix
    current = current / (jnp.sqrt(jnp.sum(current * current)) + 1e-07)
    for _ in range(NS_ITERS):
        square = jnp.dot(current, current.T, precision=lax.Precision.HIGHEST)
        polynomial = COEFF_B * square + COEFF_C * jnp.dot(square, square, precision=lax.Precision.HIGHEST)
        current = COEFF_A * current + jnp.dot(polynomial, current, precision=lax.Precision.HIGHEST)
    return current.T if flipped else current


def scaled_update(matrix, factor):
    return (factor * orthogonalize(matrix)).reshape(-1)


def empty_update(matrix, factor):
    return jnp.zeros((matrix.shape[0] * matrix.shape[1],), F32)


def any_device(tokens, conditions, assignment, params, momentum, cotangent):
    lat = tokens.shape[0]
    rows = lat * SEQ
    table = lax.all_gather(conditions, ("fsdp", "rep"), axis=0, tiled=True)
    gathered = lax.all_gather(params.astype(BF16), "fsdp", axis=0, tiled=True)
    blocks = to_blocks(unpack(gathered))
    me = lax.axis_index("fsdp")
    sidx = jnp.concatenate([jnp.zeros((3,), jnp.int32), assignment.astype(jnp.int32)])
    tok2, cot2 = tokens.reshape(rows, D), cotangent.reshape(rows, D)
    (blend, qkv, probs, ai, gafter, gmx, mods, gmod1, silu, wqkv, gout, keep1, send1) = main_call(
        sidx, table, tok2, cot2, (blocks,), False
    )
    gqkv = heads_call(qkv, probs, gmx)
    gtok, keep2, send2, keep = input_call(sidx, tok2, gqkv, ai, gafter, mods, gmod1, silu, wqkv, gout)
    halves1 = jnp.stack([keep1, send1.astype(F32)]).reshape(2, 4, 4, 96, D)
    up = halves1[:, jnp.array([2, 0])].transpose(2, 0, 1, 3, 4).reshape(4, D, D)
    down = halves1[:, jnp.array([3, 1])].transpose(2, 0, 1, 3, 4).reshape(4, D, D)
    halves2 = jnp.stack([keep2, send2.astype(F32)]).reshape(2, 4, 4, 48, D)
    last = halves2.transpose(2, 0, 1, 3, 4).reshape(4, D, D)
    rest = jnp.concatenate(
        [from_blocks(last[:3], True), last[3].reshape(-1), from_blocks(up, True), down.reshape(-1)]
    )
    kept = lax.all_gather(keep, ("fsdp", "rep"), axis=0, tiled=True).reshape(-1, KEPT_ROWS, D)
    silu_all = kept[:, 6 * lat : 7 * lat].reshape(-1, D)
    mod_all = kept[:, : 6 * lat].reshape(-1, 6, lat, D).transpose(0, 2, 1, 3).reshape(-1, 6 * D)
    adaln = lax.dot_general(silu_all, mod_all, (((0,), (0,)), ((), ())), preferred_element_type=F32)
    shard_len = params.shape[0]
    head = jnp.concatenate([adaln.reshape(-1), jnp.zeros_like(rest)])
    flat = jnp.concatenate([jnp.zeros((D * 6 * D,), F32), rest])
    part = lax.psum_scatter(flat, "fsdp", scatter_dimension=0, tiled=True)
    full_grad = lax.psum(part, "rep") + lax.dynamic_slice_in_dim(head, me * shard_len, shard_len, 0)
    new_momentum = MOMENTUM_RATE * momentum + full_grad
    whole_mom = lax.all_gather(new_momentum, "fsdp", axis=0, tiled=True)
    group_size = lax.axis_size("fsdp")
    updates, offset = [], 0
    for mat, piece in enumerate(unpack(whole_mom)):
        factor = F32(update_scale(mat))
        owner = (offset // shard_len + group_size // 2) % group_size
        updates.append(lax.cond(me == owner, scaled_update, empty_update, piece, factor))
        offset += piece.size
    update = lax.psum_scatter(jnp.concatenate(updates), "fsdp", scatter_dimension=0, tiled=True)
    shape = tokens.shape
    return (blend.reshape(shape), gtok.reshape(shape), full_grad, params - update, new_momentum)


def solution(mesh):
    both = ("fsdp", "rep")
    in_specs = (P(both, None, None), P(both, None), P(both), P("fsdp"), P("fsdp"), P(both, None, None))
    out_specs = (P(both, None, None), P(both, None, None), P("fsdp"), P("fsdp"), P("fsdp"))
    small = dict(mesh.shape) == {"fsdp": 4, "rep": 8}
    return jax.shard_map(
        fast_device if small else any_device,
        mesh=mesh,
        in_specs=in_specs,
        out_specs=out_specs,
        check_vma=False,
    )
```

```python
import functools
import math

import jax
import jax.numpy as jnp
from jax import lax
from jax.experimental import pallas as pl
from jax.experimental.pallas import tpu as pltpu
from jax.sharding import PartitionSpec as P


D = 384
HEADS = 6
HD = 64
FF = 1536
SEQ = 256
NS_ITERS = 3

LN_EPSILON = 1e-06
MOMENTUM_RATE = 0.95
LEARN_RATE = 0.2
COEFF_A = 3.4445
COEFF_B = -4.775
COEFF_C = 2.0315


F32 = jnp.float32
BF16 = jnp.bfloat16

MATS = ((D, 6 * D, 0, True), (D, 3 * D, 6, True), (D, D, 9, True), (D, FF, 10, True), (FF, D, 14, False))
NBLOCKS = 18
ADALN, QKV, OUTW, UP, DOWN = range(5)
P_SIZE = sum(m[0] * m[1] for m in MATS)
KEPT_ROWS = 16


def update_scale(mat):
    return LEARN_RATE * 0.2 * math.sqrt(max(MATS[mat][0], MATS[mat][1]))


def shard_pieces(shard, count):
    size = P_SIZE // count
    begin, end = shard * size, (shard + 1) * size
    pieces, crow, offset = [], 0, 0
    for mat, (rows, cols, first, by_cols) in enumerate(MATS):
        lo, hi = max(begin, offset), min(end, offset + rows * cols)
        if lo < hi:
            r0, r1 = (lo - offset) // cols, (hi - offset) // cols
            stride = cols // 128
            base = (offset - begin) // 128
            if by_cols:
                for b in range(cols // D):
                    pieces.append((mat, first + b, r0, r1 - r0, crow, base + r0 * stride + 3 * b, stride))
                    crow += r1 - r0
            else:
                r = r0
                while r < r1:
                    n = min(r1, (r // D + 1) * D) - r
                    pieces.append((mat, first + r // D, r % D, n, crow, base + r * stride, stride))
                    crow += n
                    r += n
        offset += rows * cols
    return pieces


def mm(a, b, ca=1, cb=0):
    return lax.dot_general(a, b, (((ca,), (cb,)), ((), ())), preferred_element_type=F32)


def vspec():
    return pl.BlockSpec(memory_space=pltpu.VMEM)


def hspec():
    return pl.BlockSpec(memory_space=pltpu.HBM)


def in_hbm(x):
    return pltpu.with_memory_space_constraint(x, pltpu.HBM)


def sspec():
    return pl.BlockSpec(memory_space=pltpu.SMEM)


def params_of(mib):
    return pltpu.CompilerParams(vmem_limit_bytes=mib * 1024 * 1024)


def prep_kernel(count, s_ref, p_ref, w_ref, half_ref):
    for shard in range(count):

        @pl.when(s_ref[0] == shard)
        def _(shard=shard):
            for _, _, _, n, crow, frow, stride in shard_pieces(shard, count):
                for j in range(3):
                    src = pl.ds(frow + j, n, stride=stride)
                    w_ref[crow : crow + n, 128 * j : 128 * j + 128] = p_ref[src, :].astype(BF16)

    half = half_ref.shape[0]
    half_ref[...] = w_ref[pl.ds(pl.multiple_of(s_ref[1] * half, half), half), :]


def prep(sidx, flat, count):
    rows = P_SIZE // count // D
    out = (jax.ShapeDtypeStruct((rows, D), BF16), jax.ShapeDtypeStruct((rows // 2, D), BF16))
    return pl.pallas_call(
        functools.partial(prep_kernel, count),
        out_shape=out,
        in_specs=[sspec(), vspec()],
        out_specs=(vspec(), vspec()),
        compiler_params=params_of(4),
        cost_estimate=pl.CostEstimate(flops=0, bytes_accessed=4_000_000, transcendentals=0),
        name="prep",
    )(sidx, flat)


def layer_norm(h):
    center = jnp.mean(h, axis=-1, keepdims=True)
    cent = h - center
    spread = jnp.mean(jnp.square(cent), axis=-1, keepdims=True)
    rstd = lax.rsqrt(spread + LN_EPSILON)
    return cent * rstd, rstd


def layer_norm_grad(xhat, rstd, gx):
    m1 = jnp.mean(gx, axis=-1, keepdims=True)
    m2 = jnp.mean(gx * xhat, axis=-1, keepdims=True)
    return rstd * (gx - m1 - xhat * m2)


def gather_plan(count):
    plan = []
    half = P_SIZE // count // D // 2
    for shard in range(count):
        for _, block, r0, n, crow, _, _ in shard_pieces(shard, count):
            cuts = sorted({crow, crow + n} | {c for c in range(0, 2 * half + 1, half // 2) if crow < c < crow + n})
            for a, b in zip(cuts[:-1], cuts[1:]):
                plan.append((shard, a // half, a % half, b - a, block, r0 + a - crow))
    return plan


def load_weights_fast(s_ref, bufs, wts, own_ready):
    own, rx, ry, rda, rdb, px, py, pda, pdb = bufs
    me, core = s_ref[0], s_ref[1]
    half = own.shape[0] // 2
    quarter = half // 2
    plan = gather_plan(4)

    def move(src, row, n, block, brow):
        size = 96 if n % 96 == 0 else 48

        def chunk(i, carry):
            a = pl.multiple_of(row + i * size, 16)
            b = pl.multiple_of(brow + i * size, 16)
            wts[block, pl.ds(b, size), :] = src[pl.ds(a, size), :]
            return carry

        lax.fori_loop(0, n // size, chunk, 0)

    for shard in range(4):
        for h in range(2):
            pieces = [p for p in plan if p[0] == shard and p[1] == h]
            for m in (1, 2, 3):
                for mine in (True, False):

                    @pl.when(jnp.logical_and(me == (shard ^ m), (core == h) if mine else (core != h)))
                    def _(pieces=pieces, m=m, mine=mine):
                        for _, _, r, n, block, br in pieces:
                            if m < 3:
                                move(((rx, ry) if mine else (px, py))[m - 1], r, n, block, br)
                            else:
                                k = r // quarter
                                pair = (rda, rdb) if mine else (pda, pdb)
                                move(pair[k], r - k * quarter, n, block, br)

    own_ready()
    for shard in range(4):

        @pl.when(me == shard)
        def _(shard=shard):
            for _, h, r, n, block, br in [p for p in plan if p[0] == shard]:
                move(own, h * half + r, n, block, br)


def by_core(value, core):
    half = value.shape[0] // 2
    top, bottom = value[:half], value[half:]
    return jnp.where(core == 0, top, bottom), jnp.where(core == 0, bottom, top)


def main_kernel(nbuf, fast, rows, s_ref, table, tok_hbm, cot_hbm, *refs):
    bufs = refs[:nbuf]
    (blend, qkv, probs, amix_in, gafter, gmx, mods, gmod, silu, wqkv, gout, keep1, send1) = refs[nbuf : nbuf + 13]
    wts, ao_s, aa_s, amix, minp, gmi, mo, tok, cot, own, sems = refs[nbuf + 13 :]
    lat = rows // SEQ
    get_tok = pltpu.make_async_copy(tok_hbm, tok, sems.at[1])
    get_cot = pltpu.make_async_copy(cot_hbm, cot, sems.at[2])
    first = pltpu.make_async_copy(bufs[0], own if fast else wts, sems.at[0])
    first.start()
    get_tok.start()
    get_cot.start()
    if fast:
        load_weights_fast(s_ref, (own,) + bufs[1:], wts, first.wait)
    else:
        first.wait()
    get_tok.wait()
    get_cot.wait()
    nt = table.shape[0]
    lanes = lax.broadcasted_iota(jnp.int32, (16, nt), 1)
    rws = lax.broadcasted_iota(jnp.int32, (16, nt), 0)
    pick = jnp.zeros((16, nt), jnp.bool_)
    for l in range(lat):
        pick = pick | ((rws == l) & (lanes == s_ref[3 + l]))
    cond = mm(pick.astype(F32).astype(BF16), table[...])
    sc = (cond * (1.0 / (1.0 + jnp.exp(-cond)))).astype(BF16)
    silu[...] = sc.astype(F32)
    for b in range(6):
        mods[b] = mm(sc, wts[b])[:8]
    for j in range(3):
        wqkv[j] = wts[6 + j]

    def mod(b, l):
        return mods[b, l : l + 1, :]

    for l in range(lat):
        rs = slice(l * SEQ, (l + 1) * SEQ)
        xhat, _ = layer_norm(tok[rs, :].astype(F32))
        amix_in[rs, :] = (xhat * (1.0 + mod(1, l)) + mod(0, l)).astype(BF16)
    ai = amix_in[...]
    for j in range(3):
        qkv[j] = mm(ai, wts[6 + j]).astype(BF16)

    low = lax.broadcasted_iota(jnp.int32, (SEQ, 128), 1) < HD
    zero = jnp.zeros((SEQ, 128), BF16)

    def attend(l, carry):
        rs = pl.ds(pl.multiple_of(l * SEQ, SEQ), SEQ)
        for hp in range(HEADS // 2):
            cs = slice(hp * 128, hp * 128 + 128)
            q, k, v = qkv[0, rs, cs], qkv[1, rs, cs], qkv[2, rs, cs]
            outs = []
            for h in range(2):
                qm = jnp.where(low if h == 0 else jnp.logical_not(low), q, zero)
                s = mm(qm, k, 1, 1) * HD ** (-0.5)
                top = jnp.max(s, axis=-1, keepdims=True)
                e = jnp.exp(s - top)
                pr = e * (1.0 / jnp.sum(e, axis=-1, keepdims=True))
                probs[l * HEADS + hp * 2 + h] = pr
                outs.append(mm(pr.astype(BF16), v))
            amix[rs, cs] = jnp.where(low, outs[0], outs[1]).astype(BF16)
        return carry

    lax.fori_loop(0, lat, attend, 0)

    ao = mm(amix[...], wts[9])
    ao_s[...] = ao
    for l in range(lat):
        rs = slice(l * SEQ, (l + 1) * SEQ)
        aa = tok[rs, :].astype(F32) + mod(2, l) * ao_s[rs, :]
        aa_s[rs, :] = aa
        xhat, _ = layer_norm(aa)
        minp[rs, :] = (xhat * (1.0 + mod(4, l)) + mod(3, l)).astype(BF16)
        gmx[rs, :] = (cot[rs, :].astype(F32) * mod(5, l)).astype(BF16)
    gmi[...] = jnp.zeros_like(gmi)
    mo[...] = jnp.zeros_like(mo)

    me, core = s_ref[0], s_ref[1]

    def put(value, members, j):
        mine, other = by_core(value, core)
        for i, member in enumerate(members):
            rs = pl.ds(pl.multiple_of(j * 96, 96), 96)
            keep1[member ^ me, rs, :] = mine[96 * i : 96 * i + 96]
            send1[member ^ me, rs, :] = other[96 * i : 96 * i + 96].astype(BF16)

    def mlp(j, carry):
        wu, wd = wts[10 + j], wts[14 + j]
        u = mm(minp[...], wu)
        c = math.sqrt(2.0 / math.pi)
        u2 = u * u
        t = jnp.tanh(c * (u + 0.044715 * (u2 * u)))
        half = 0.5 * (1.0 + t)
        act = (u * half).astype(BF16)
        slope = half + 0.5 * u * (1.0 - t * t) * (c * (1.0 + 3.0 * 0.044715 * u2))
        mo[...] += mm(act, wd)
        gmo = gmx[...]
        gp = (mm(gmo, wd, 1, 1) * slope).astype(BF16)
        put(mm(act, gmo, 0, 0), (3, 1), j)
        put(mm(minp[...], gp, 0, 0), (2, 0), j)
        gmi[...] += mm(gp, wu, 1, 1)
        return carry

    lax.fori_loop(0, FF // D, mlp, 0)

    gmod[...] = jnp.zeros_like(gmod)
    for l in range(lat):
        rs = slice(l * SEQ, (l + 1) * SEQ)
        up = cot[rs, :].astype(F32)
        blend[rs, :] = (aa_s[rs, :] + mod(5, l) * mo[rs, :]).astype(BF16)
        gmod[5, l : l + 1, :] = jnp.sum(up * mo[rs, :], axis=0, keepdims=True)
        xhat, rstd = layer_norm(aa_s[rs, :])
        g = gmi[rs, :]
        gmod[3, l : l + 1, :] = jnp.sum(g, axis=0, keepdims=True)
        gmod[4, l : l + 1, :] = jnp.sum(g * xhat, axis=0, keepdims=True)
        ga = up + layer_norm_grad(xhat, rstd, g * (1.0 + mod(4, l)))
        gafter[rs, :] = ga
        gmod[2, l : l + 1, :] = jnp.sum(ga * ao_s[rs, :], axis=0, keepdims=True)
        minp[rs, :] = (ga * mod(2, l)).astype(BF16)
    gao = minp[...]
    gout[...] = mm(amix[...], gao, 0, 0)
    gmx[...] = mm(gao, wts[9], 1, 1).astype(BF16)


def main_call(sidx, table, tokens, cotangent, bufs, fast):
    rows = tokens.shape[0]
    lat = rows // SEQ
    sd = jax.ShapeDtypeStruct
    outs = (
        sd((rows, D), BF16),
        sd((3, rows, D), BF16),
        sd((lat * HEADS, SEQ, SEQ), F32),
        sd((rows, D), BF16),
        sd((rows, D), F32),
        sd((rows, D), BF16),
        sd((6, 8, D), F32),
        sd((6, 8, D), F32),
        sd((16, D), F32),
        sd((3, D, D), BF16),
        sd((D, D), F32),
        sd((4, D, D), F32),
        sd((4, D, D), BF16),
    )
    return pl.pallas_call(
        functools.partial(main_kernel, len(bufs), fast, rows),
        out_shape=outs,
        in_specs=[sspec(), vspec(), hspec(), hspec(), hspec()] + [vspec()] * (len(bufs) - 1),
        out_specs=(vspec(),) * len(outs),
        scratch_shapes=[
            pltpu.VMEM((NBLOCKS, D, D), BF16),
            pltpu.VMEM((rows, D), F32),
            pltpu.VMEM((rows, D), F32),
            pltpu.VMEM((rows, D), BF16),
            pltpu.VMEM((rows, D), BF16),
            pltpu.VMEM((rows, D), F32),
            pltpu.VMEM((rows, D), F32),
            pltpu.VMEM((rows, D), BF16),
            pltpu.VMEM((rows, D), BF16),
            pltpu.VMEM(bufs[0].shape if fast else (16, D), BF16),
            pltpu.SemaphoreType.DMA((3,)),
        ],
        compiler_params=params_of(20),
        cost_estimate=pl.CostEstimate(flops=20_000_000_000, bytes_accessed=30_000_000, transcendentals=0),
        name="main",
    )(sidx, table, *(in_hbm(x) for x in (tokens, cotangent, bufs[0])), *bufs[1:])


def heads_kernel(rows, qkv, probs, gmx, gqkv):
    lat = rows // SEQ
    low = lax.broadcasted_iota(jnp.int32, (SEQ, 128), 1) < HD
    zero = jnp.zeros((SEQ, 128), BF16)

    def back(l, carry):
        rs = pl.ds(pl.multiple_of(l * SEQ, SEQ), SEQ)
        for hp in range(HEADS // 2):
            cs = slice(hp * 128, hp * 128 + 128)
            q, k, v = qkv[0, rs, cs], qkv[1, rs, cs], qkv[2, rs, cs]
            g = gmx[rs, cs]
            res = []
            for h in range(2):
                p = probs[l * HEADS + hp * 2 + h]
                gm = jnp.where(low if h == 0 else jnp.logical_not(low), g, zero)
                gv = mm(p.astype(BF16), g, 0, 0)
                gpr = mm(gm, v, 1, 1)
                dots = jnp.sum(p * gpr, axis=-1, keepdims=True)
                gs = (p * (gpr - dots) * HD ** (-0.5)).astype(BF16)
                res.append((mm(gs, k), mm(gs, q, 0, 0), gv))
            for j in range(3):
                gqkv[j, rs, cs] = jnp.where(low, res[0][j], res[1][j]).astype(BF16)
        return carry

    lax.fori_loop(0, lat, back, 0)


def heads_call(qkv, probs, gmx):
    rows = gmx.shape[0]
    return pl.pallas_call(
        functools.partial(heads_kernel, rows),
        out_shape=jax.ShapeDtypeStruct((3, rows, D), BF16),
        in_specs=[vspec()] * 3,
        out_specs=vspec(),
        compiler_params=params_of(4),
        cost_estimate=pl.CostEstimate(flops=6_000_000_000, bytes_accessed=6_000_000, transcendentals=0),
        name="heads",
    )(qkv, probs, gmx)


def input_kernel(rows, s_ref, tok, gqkv, ai, gafter, mods, gmod1, silu, wqkv, gout, gtok, keep2, send2, keep, srow):
    me, core = s_ref[0], s_ref[1]
    lat = rows // SEQ
    gai = None
    for j in range(4):
        if j < 3:
            part = mm(gqkv[j], wqkv[j], 1, 1)
            gai = part if gai is None else gai + part
            value = mm(ai[...], gqkv[j], 0, 0)
        else:
            value = gout[...]
        mine, other = by_core(value, core)
        for m in range(4):
            rs = slice(48 * j, 48 * j + 48)
            keep2[m ^ me, rs, :] = mine[48 * m : 48 * m + 48]
            send2[m ^ me, rs, :] = other[48 * m : 48 * m + 48].astype(BF16)
    srow[...] = jnp.zeros_like(srow)
    for l in range(lat):
        rs = slice(l * SEQ, (l + 1) * SEQ)
        xhat, rstd = layer_norm(tok[rs, :].astype(F32))
        g = gai[rs, :]
        srow[l : l + 1, :] = jnp.sum(g, axis=0, keepdims=True)
        srow[lat + l : lat + l + 1, :] = jnp.sum(g * xhat, axis=0, keepdims=True)
        gtok[rs, :] = gafter[rs, :] + layer_norm_grad(xhat, rstd, g * (1.0 + mods[1, l : l + 1, :]))
        for b in range(2, 6):
            srow[lat * b + l : lat * b + l + 1, :] = gmod1[b, l : l + 1, :]
        srow[lat * 6 + l : lat * 6 + l + 1, :] = silu[l : l + 1, :]
    keep[...] = srow[...].astype(BF16)


def input_call(sidx, tokens, gqkv, ai, gafter, mods, gmod1, silu, wqkv, gout):
    rows = tokens.shape[0]
    sd = jax.ShapeDtypeStruct
    outs = (sd((rows, D), F32), sd((4, D // 2, D), F32), sd((4, D // 2, D), BF16), sd((KEPT_ROWS, D), BF16))
    return pl.pallas_call(
        functools.partial(input_kernel, rows),
        out_shape=outs,
        in_specs=[sspec()] + [vspec()] * 9,
        out_specs=(vspec(),) * 4,
        scratch_shapes=[pltpu.VMEM((KEPT_ROWS, D), F32)],
        compiler_params=params_of(6),
        cost_estimate=pl.CostEstimate(flops=6_000_000_000, bytes_accessed=6_000_000, transcendentals=0),
        name="input",
    )(sidx, tokens, gqkv, ai, gafter, mods, gmod1, silu, wqkv, gout)


def split(x):
    hi = x.astype(BF16)
    return hi, (x - hi.astype(F32)).astype(BF16)


POLY = (COEFF_C, COEFF_B, COEFF_A)
PLAIN = (1.0, 0.0, 0.0)
STEPS = (
    (0, 0, 2, 1, POLY),
    (2, 0, 3, 2, PLAIN),
    (3, 2, 0, 2, PLAIN),
    (0, 0, 1, 1, POLY),
    (1, 2, 2, 3, PLAIN),
    (1, 0, 3, 2, PLAIN),
    (3, 1, 0, 2, PLAIN),
    (0, 0, 1, 3, POLY),
    (1, 2, 2, 3, PLAIN),
)


def step_tables():
    ints = jnp.array([x for st in STEPS for x in st[:4]], jnp.int32)
    coeffs = jnp.array([x for st in STEPS for x in st[4]], F32)
    return ints, coeffs


def either(flipped, tall, wide):
    if flipped is None:
        wide()
    else:
        pl.when(flipped)(tall)
        pl.when(jnp.logical_not(flipped))(wide)


def newton_schulz(ints, coeffs, mat_ref, upd_ref, bufs, npairs, flipped, factor):
    bufs[0] = jnp.zeros((D, D), F32)

    def gram(b, carry):
        x0, x1 = mat_ref[2 * b].astype(BF16), mat_ref[2 * b + 1].astype(BF16)

        def tall():
            x = jnp.concatenate([x0, x1], axis=0)
            bufs[0] += mm(x, x, 0, 0)

        def wide():
            x = jnp.concatenate([x0, x1], axis=1)
            bufs[0] += mm(x, x, 1, 1)

        either(flipped, tall, wide)

        return carry

    lax.fori_loop(0, npairs, gram, 0)
    g = bufs[0]
    ri = lax.broadcasted_iota(jnp.int32, (D, D), 0)
    ci = lax.broadcasted_iota(jnp.int32, (D, D), 1)
    eye = jnp.where(ri == ci, 1.0, 0.0)
    diag = jnp.sum(g * eye, axis=1, keepdims=True)
    total = jnp.sum(diag, axis=0, keepdims=True)
    inv = 1.0 / (jnp.sqrt(total) + 1e-07)
    bufs[0] = g * (inv * inv)

    def step(k, carry):
        i, j, d, passes = (ints[4 * k + n] for n in range(4))

        def product(count):
            x = bufs[i]
            xh, xl = split(x)
            yh, yl = split(bufs[j])
            lhs = (xh, xl, xh)[:count]
            rhs = (yh, yh, yl)[:count]
            prod = mm(jnp.concatenate(lhs, axis=1), jnp.concatenate(rhs, axis=0))
            r0 = lax.broadcasted_iota(jnp.int32, (D, D), 0)
            r1 = lax.broadcasted_iota(jnp.int32, (D, D), 1)
            ident = jnp.where(r0 == r1, coeffs[3 * k + 2], 0.0)
            bufs[d] = coeffs[3 * k] * prod + (coeffs[3 * k + 1] * x + ident)

        for count in (1, 2, 3):
            pl.when(passes == count)(functools.partial(product, count))
        return carry

    lax.fori_loop(0, len(STEPS), step, 0)
    bufs[0] = bufs[2] * (inv * factor)

    def apply(b, carry):
        wh, wl = split(bufs[0])
        xs = [mat_ref[2 * b + i] for i in range(2)]

        def tall():
            for i in range(2):
                x = xs[i].astype(BF16)
                upd_ref[2 * b + i] = mm(
                    jnp.concatenate([x, x], axis=1), jnp.concatenate([wh, wl], axis=0)
                )

        def wide():
            x = jnp.concatenate([xs[0].astype(BF16), xs[1].astype(BF16)], axis=1)
            out = mm(jnp.concatenate([wh, wl], axis=1), jnp.concatenate([x, x], axis=0))
            upd_ref[2 * b] = out[:, :D]
            upd_ref[2 * b + 1] = out[:, D:]

        either(flipped, tall, wide)
        return carry

    lax.fori_loop(0, npairs, apply, 0)


def take_first(s_ref, chunks, dst):
    me, core, zed = s_ref[0], s_ref[1], s_ref[2]
    for c, ref in enumerate(chunks):
        for y in range(2):
            part = ((me // 2) ^ 1) ^ y
            rs = pl.ds(pl.multiple_of((core ^ c) * 192 + part * 96, 96), 96)
            for z in range(4):
                dst[zed ^ z, rs, :] = ref[y, z].astype(F32)


def take_second(s_ref, chunks, dst):
    me, core, zed = s_ref[0], s_ref[1], s_ref[2]
    for c, ref in enumerate(chunks):
        for m in range(4):
            rs = pl.ds(pl.multiple_of((core ^ c) * 192 + (me ^ m) * 48, 48), 48)
            for z in range(4):
                dst[zed ^ z, rs, :] = ref[m, z].astype(F32)


def adaln_grads(kept, grd, kf):
    ndev = 2 * kept[0].shape[0] // KEPT_ROWS
    for i, ref in enumerate(kept):
        n = ref.shape[0]
        for j in range(3):
            kf[j, i * n : (i + 1) * n, :] = ref[:, 128 * j : 128 * j + 128].astype(F32)

    def rows(first):
        part = [kf[j, pl.ds(first, ndev, stride=KEPT_ROWS), :] for j in range(3)]
        return jnp.concatenate(part, axis=1).astype(BF16)

    sil = jnp.concatenate([rows(12), rows(13)], axis=0)
    for b in range(6):
        gm = jnp.concatenate([rows(2 * b), rows(2 * b + 1)], axis=0)
        grd[b] = mm(sil, gm, 0, 0)


def add_momentum(t, target, mom, grd, mat, base=0):
    first = MATS[target][2]
    for _, block, r0, n, _, frow, stride in [p for p in shard_pieces(t, 4) if p[0] == target]:
        b = block - first
        for j in range(3):
            cs = slice(128 * j, 128 * j + 128)
            m = mom[pl.ds(frow + j, n, stride=stride), :]
            mat[b, r0 : r0 + n, cs] = MOMENTUM_RATE * m + grd[base + b, r0 : r0 + n, cs]


def add_foreign(s_ref, t, target, foreign, grd, mat):
    core = s_ref[1]
    half = foreign[0].shape[0]
    for _, block, r0, n, crow, _, _ in [p for p in shard_pieces(t ^ 1, 4) if p[0] == target]:
        b = block - MATS[target][2]
        cuts = sorted({crow, crow + n} | {c for c in (half,) if crow < c < crow + n})
        for lo, hi in zip(cuts[:-1], cuts[1:]):
            h = lo // half
            for mine, src in enumerate(foreign):

                @pl.when(core == (h ^ mine))
                def _(b=b, r0=r0, lo=lo, hi=hi, h=h, crow=crow, src=src):
                    dst = slice(r0 + lo - crow, r0 + hi - crow)
                    m = src[lo - h * half : hi - h * half, :].astype(F32)
                    mat[b, dst, :] = MOMENTUM_RATE * m + grd[b, dst, :]


TAIL = 48


def ns_a_kernel(s_ref, ints, coeffs, mom, fx0, fx1, kz0, kz1, ch0, ch1, upd, grd, tail, mat, bufs, kf):
    me = s_ref[0]

    @pl.when(me < 2)
    def _():
        adaln_grads((kz0, kz1), grd, kf)

    @pl.when(me >= 2)
    def _():
        take_first(s_ref, (ch0, ch1), grd)

    for t, target in enumerate((ADALN, ADALN, UP, DOWN)):

        @pl.when(me == t)
        def _(t=t, target=target):
            add_momentum(t, target, mom, grd, mat)
            if target != DOWN:
                add_foreign(s_ref, t, target, (fx0, fx1), grd, mat)

    npairs = jnp.where(me < 2, 3, 2)
    factor = jnp.where(me < 2, update_scale(ADALN), update_scale(UP))
    newton_schulz(ints, coeffs, mat, upd, bufs, npairs, me == 3, factor)

    for b in range(4):
        rs = slice(TAIL * b, TAIL * b + TAIL)
        tail[0, rs, :] = grd[b, D - TAIL :, :].astype(BF16)
        tail[1, rs, :] = upd[b, D - TAIL :, :].astype(BF16)


def ns_a(sidx, tables, mom, foreign, kept, chunks):
    sd = jax.ShapeDtypeStruct((6, D, D), F32)
    return pl.pallas_call(
        ns_a_kernel,
        out_shape=(sd, sd, jax.ShapeDtypeStruct((2, 4 * TAIL, D), BF16)),
        in_specs=[sspec()] * 3 + [vspec()] * 7,
        out_specs=(vspec(),) * 3,
        scratch_shapes=[
            pltpu.VMEM((6, D, D), F32),
            pltpu.VMEM((4, D, D), F32),
            pltpu.VMEM((3, 2 * kept[0].shape[0], 128), F32),
        ],
        compiler_params=params_of(14),
        cost_estimate=pl.CostEstimate(flops=8_000_000_000, bytes_accessed=12_000_000, transcendentals=0),
        name="ns_a",
    )(sidx, *tables, mom, *foreign, *kept, *chunks)


def final_kernel(
    s_ref, ints, coeffs, par, mom, ch0, ch1, upa, grda, tail, ograd, onew, omom, upb, gb, mat, bufs
):
    me = s_ref[0]
    inner = jnp.logical_or(me == 1, me == 2)

    @pl.when(inner)
    def _():
        take_second(s_ref, (ch0, ch1), gb)
        for b in range(1, 4):
            mat[b] = jnp.zeros((D, D), F32)

    @pl.when(me == 1)
    def _():
        add_momentum(1, QKV, mom, gb, mat)

    @pl.when(me == 2)
    def _():
        add_momentum(2, OUTW, mom, gb, mat, 3)

    @pl.when(inner)
    def _():
        npairs = jnp.where(me == 1, 2, 1)
        factor = jnp.where(me == 1, update_scale(QKV), update_scale(OUTW))
        newton_schulz(ints, coeffs, mat, upb, bufs, npairs, None, factor)

    for t in range(4):

        @pl.when(me == t)
        def _(t=t):
            for mat_id, block, r0, n, crow, frow, stride in shard_pieces(t, 4):
                b = block - MATS[mat_id][2]
                for j in range(3):
                    cs = slice(128 * j, 128 * j + 128)
                    fl = pl.ds(frow + j, n, stride=stride)
                    if mat_id == UP and t == 3:
                        assert r0 == D - TAIL and n == TAIL
                        g = tail[0, TAIL * b : TAIL * b + TAIL, cs].astype(F32)
                        u = tail[1, TAIL * b : TAIL * b + TAIL, cs].astype(F32)
                    elif mat_id in (QKV, OUTW):
                        g = gb[b + 3 * (mat_id == OUTW), r0 : r0 + n, cs]
                        u = upb[b, r0 : r0 + n, cs]
                    else:
                        g = grda[b, r0 : r0 + n, cs]
                        u = upa[b, r0 : r0 + n, cs]
                    ograd[fl, :] = g
                    omom[fl, :] = MOMENTUM_RATE * mom[fl, :] + g
                    onew[fl, :] = par[fl, :] - u


def final_call(sidx, tables, par, mom, chunks, upa, grda, tail):
    sd = jax.ShapeDtypeStruct(par.shape, F32)
    block4 = pltpu.VMEM((4, D, D), F32)
    return pl.pallas_call(
        final_kernel,
        out_shape=(sd, sd, sd),
        in_specs=[sspec()] * 3 + [vspec()] * 7,
        out_specs=(vspec(),) * 3,
        scratch_shapes=[block4, block4, block4, block4],
        compiler_params=params_of(20),
        cost_estimate=pl.CostEstimate(flops=8_000_000_000, bytes_accessed=24_000_000, transcendentals=0),
        name="finish",
    )(sidx, *tables, par, mom, *chunks, upa, grda, tail)


def swap(x, axis, mask):
    count = lax.axis_size(axis)
    return lax.ppermute(x, axis, [(i, i ^ mask) for i in range(count)])


def more_rows(x, hops):
    for axis, mask in hops:
        x = jnp.concatenate([x, swap(x, axis, mask)], axis=0)
    return x


def wide_sum(parts):
    total = None
    for p in parts:
        total = p.astype(F32) if total is None else total + p.astype(F32)
    return total


def at(x, i):
    return lax.dynamic_index_in_dim(x, i, 0, keepdims=False)


def z_scatter(s, zed, extra=None):
    size = s.shape[0] // 4
    blocks = s.reshape(4, size, D)
    got = []
    for m in (1, 2, 3):
        piece = at(blocks, zed ^ m).astype(BF16)
        if extra is not None:
            piece = jnp.concatenate([piece, extra], axis=0)
        got.append(swap(piece, "rep", 2 * m))
    total = wide_sum([at(blocks, zed)] + [g[:size] for g in got]).astype(BF16)
    if extra is None:
        return total
    return total, jnp.concatenate([extra] + [g[size:] for g in got], axis=0)


def fan(x, axis, masks):
    got = [x]
    for m in masks:
        got.append(swap(x, axis, m))
    return jnp.stack(got)


def fast_device(tokens, conditions, assignment, params, momentum, cotangent):
    return fast_body(tokens, conditions, assignment, params, momentum, cotangent)


def fast_body(tokens, conditions, assignment, params, momentum, cotangent):
    me = lax.axis_index("fsdp")
    rep = lax.axis_index("rep")
    core, zed = rep % 2, rep // 2
    lat = tokens.shape[0]
    rows = lat * SEQ
    par = params.reshape(-1, 128)
    mom = momentum.reshape(-1, 128)
    source = assignment // lat
    apart = ((source // 8) ^ me) + 4 * ((source % 8) ^ rep)
    pick = apart * lat + assignment % lat
    sidx = jnp.concatenate([jnp.stack([me, core, zed]), pick]).astype(jnp.int32)

    hop = swap(conditions, "fsdp", 1)
    wc, wh = prep(sidx, par, 4)
    table = jnp.concatenate([conditions, hop], axis=0)
    table, wh = lax.optimization_barrier((table, wh))
    hop = swap(table, "fsdp", 2)
    rx = swap(wh, "fsdp", 1)
    ry = swap(wh, "fsdp", 2)
    table = jnp.concatenate([table, hop], axis=0)
    table = more_rows(table, (("rep", 1), ("rep", 2), ("rep", 4)))
    rx, ry, table = lax.optimization_barrier((rx, ry, table))
    quarter = wh.shape[0] // 2
    rda, rdb = swap(rx[:quarter], "fsdp", 2), swap(ry[quarter:], "fsdp", 1)
    px, py = swap(rx, "rep", 1), swap(ry, "rep", 1)
    pda, pdb = swap(rda, "rep", 1), swap(rdb, "rep", 1)
    bufs = (wc, rx, ry, rda, rdb, px, py, pda, pdb)
    _, mh = prep(sidx, mom, 4)
    fx0 = swap(mh, "fsdp", 1)

    tok2, cot2 = tokens.reshape(rows, D), cotangent.reshape(rows, D)
    (blend, qkv, probs, ai, gafter, gmx, mods, gmod1, silu, wqkv, gout, keep1, send1) = main_call(
        sidx, table, tok2, cot2, bufs, True
    )
    fx1 = swap(fx0, "rep", 1)

    other = swap(send1, "rep", 1)
    gqkv = heads_call(qkv, probs, gmx)
    got = []
    for m in (1, 2, 3):
        got.append(swap((keep1[m] + other[m].astype(F32)).astype(BF16), "fsdp", m))
    gtok, keep2, send2, keep = input_call(sidx, tok2, gqkv, ai, gafter, mods, gmod1, silu, wqkv, gout)
    s1 = wide_sum([keep1[0] + other[0].astype(F32)] + got)
    col = fan(z_scatter(s1, zed), "rep", (2, 4, 6))
    pair = fan(col, "fsdp", (2,))
    pairs = (pair, swap(pair, "rep", 1))

    other = swap(send2, "rep", 1)
    got = []
    for m in (1, 2, 3):
        part = (keep2[m] + other[m].astype(F32)).astype(BF16)
        got.append(swap(jnp.concatenate([part, keep], axis=0), "fsdp", m))
    size = keep2.shape[1]
    s2 = wide_sum([keep2[0] + other[0].astype(F32)] + [g[:size] for g in got])
    q2, kz = z_scatter(s2, zed, jnp.concatenate([keep] + [g[size:] for g in got], axis=0))
    kept = (kz, swap(kz, "rep", 1))
    quad = fan(fan(q2, "rep", (2, 4, 6)), "fsdp", (1, 2, 3))
    quads = (quad, swap(quad, "rep", 1))

    tables = step_tables()
    upa, grda, tail = ns_a(sidx, tables, mom, (fx0, fx1), kept, pairs)
    tail = lax.ppermute(tail, "fsdp", [(2, 3)])
    ograd, onew, omom = final_call(sidx, tables, par, mom, quads, upa, grda, tail)
    shape = tokens.shape
    return (
        blend.reshape(shape),
        gtok.reshape(shape),
        ograd.reshape(-1),
        onew.reshape(-1),
        omom.reshape(-1),
    )


def unpack(flat):
    pieces, offset = [], 0
    for rows_count, cols_count, _, _ in MATS:
        pieces.append(flat[offset : offset + rows_count * cols_count].reshape(rows_count, cols_count))
        offset += rows_count * cols_count
    return pieces


def to_blocks(mats):
    out = []
    for matrix, (rows_count, cols_count, _, by_cols) in zip(mats, MATS):
        if by_cols:
            out.append(matrix.reshape(D, cols_count // D, D).transpose(1, 0, 2))
        else:
            out.append(matrix.reshape(rows_count // D, D, D))
    return jnp.concatenate(out, axis=0)


def from_blocks(blocks, by_cols):
    if by_cols:
        return blocks.transpose(1, 0, 2).reshape(-1)
    return blocks.reshape(-1)


def orthogonalize(matrix):
    flipped = matrix.shape[0] > matrix.shape[1]
    current = matrix.T if flipped else matrix
    current = current / (jnp.sqrt(jnp.sum(current * current)) + 1e-07)
    for _ in range(NS_ITERS):
        square = jnp.dot(current, current.T, precision=lax.Precision.HIGHEST)
        polynomial = COEFF_B * square + COEFF_C * jnp.dot(square, square, precision=lax.Precision.HIGHEST)
        current = COEFF_A * current + jnp.dot(polynomial, current, precision=lax.Precision.HIGHEST)
    return current.T if flipped else current


def scaled_update(matrix, factor):
    return (factor * orthogonalize(matrix)).reshape(-1)


def empty_update(matrix, factor):
    return jnp.zeros((matrix.shape[0] * matrix.shape[1],), F32)


def any_device(tokens, conditions, assignment, params, momentum, cotangent):
    lat = tokens.shape[0]
    rows = lat * SEQ
    table = lax.all_gather(conditions, ("fsdp", "rep"), axis=0, tiled=True)
    gathered = lax.all_gather(params.astype(BF16), "fsdp", axis=0, tiled=True)
    blocks = to_blocks(unpack(gathered))
    me = lax.axis_index("fsdp")
    sidx = jnp.concatenate([jnp.zeros((3,), jnp.int32), assignment.astype(jnp.int32)])
    tok2, cot2 = tokens.reshape(rows, D), cotangent.reshape(rows, D)
    (blend, qkv, probs, ai, gafter, gmx, mods, gmod1, silu, wqkv, gout, keep1, send1) = main_call(
        sidx, table, tok2, cot2, (blocks,), False
    )
    gqkv = heads_call(qkv, probs, gmx)
    gtok, keep2, send2, keep = input_call(sidx, tok2, gqkv, ai, gafter, mods, gmod1, silu, wqkv, gout)
    halves1 = jnp.stack([keep1, send1.astype(F32)]).reshape(2, 4, 4, 96, D)
    up = halves1[:, jnp.array([2, 0])].transpose(2, 0, 1, 3, 4).reshape(4, D, D)
    down = halves1[:, jnp.array([3, 1])].transpose(2, 0, 1, 3, 4).reshape(4, D, D)
    halves2 = jnp.stack([keep2, send2.astype(F32)]).reshape(2, 4, 4, 48, D)
    last = halves2.transpose(2, 0, 1, 3, 4).reshape(4, D, D)
    rest = jnp.concatenate(
        [from_blocks(last[:3], True), last[3].reshape(-1), from_blocks(up, True), down.reshape(-1)]
    )
    kept = lax.all_gather(keep, ("fsdp", "rep"), axis=0, tiled=True).reshape(-1, KEPT_ROWS, D)
    silu_all = kept[:, 6 * lat : 7 * lat].reshape(-1, D)
    mod_all = kept[:, : 6 * lat].reshape(-1, 6, lat, D).transpose(0, 2, 1, 3).reshape(-1, 6 * D)
    adaln = lax.dot_general(silu_all, mod_all, (((0,), (0,)), ((), ())), preferred_element_type=F32)
    shard_len = params.shape[0]
    head = jnp.concatenate([adaln.reshape(-1), jnp.zeros_like(rest)])
    flat = jnp.concatenate([jnp.zeros((D * 6 * D,), F32), rest])
    part = lax.psum_scatter(flat, "fsdp", scatter_dimension=0, tiled=True)
    full_grad = lax.psum(part, "rep") + lax.dynamic_slice_in_dim(head, me * shard_len, shard_len, 0)
    new_momentum = MOMENTUM_RATE * momentum + full_grad
    whole_mom = lax.all_gather(new_momentum, "fsdp", axis=0, tiled=True)
    group_size = lax.axis_size("fsdp")
    updates, offset = [], 0
    for mat, piece in enumerate(unpack(whole_mom)):
        factor = F32(update_scale(mat))
        owner = (offset // shard_len + group_size // 2) % group_size
        updates.append(lax.cond(me == owner, scaled_update, empty_update, piece, factor))
        offset += piece.size
    update = lax.psum_scatter(jnp.concatenate(updates), "fsdp", scatter_dimension=0, tiled=True)
    shape = tokens.shape
    return (blend.reshape(shape), gtok.reshape(shape), full_grad, params - update, new_momentum)


def solution(mesh):
    both = ("fsdp", "rep")
    in_specs = (P(both, None, None), P(both, None), P(both), P("fsdp"), P("fsdp"), P(both, None, None))
    out_specs = (P(both, None, None), P(both, None, None), P("fsdp"), P("fsdp"), P("fsdp"))
    small = dict(mesh.shape) == {"fsdp": 4, "rep": 8}
    return jax.shard_map(
        fast_device if small else any_device,
        mesh=mesh,
        in_specs=in_specs,
        out_specs=out_specs,
        check_vma=False,
    )
```

```python
import functools
import math

import jax
import jax.numpy as jnp
from jax import lax
from jax.experimental import pallas as pl
from jax.experimental.pallas import tpu as pltpu
from jax.sharding import PartitionSpec as P


D = 384
HEADS = 6
HD = 64
FF = 1536
SEQ = 256
NS_ITERS = 3

LN_EPSILON = 1e-06
MOMENTUM_RATE = 0.95
LEARN_RATE = 0.2
COEFF_A = 3.4445
COEFF_B = -4.775
COEFF_C = 2.0315


F32 = jnp.float32
BF16 = jnp.bfloat16

MATS = ((D, 6 * D, 0, True), (D, 3 * D, 6, True), (D, D, 9, True), (D, FF, 10, True), (FF, D, 14, False))
NBLOCKS = 18
ADALN, QKV, OUTW, UP, DOWN = range(5)
P_SIZE = sum(m[0] * m[1] for m in MATS)
KEPT_ROWS = 16


def update_scale(mat):
    return LEARN_RATE * 0.2 * math.sqrt(max(MATS[mat][0], MATS[mat][1]))


def shard_pieces(shard, count):
    size = P_SIZE // count
    begin, end = shard * size, (shard + 1) * size
    pieces, crow, offset = [], 0, 0
    for mat, (rows, cols, first, by_cols) in enumerate(MATS):
        lo, hi = max(begin, offset), min(end, offset + rows * cols)
        if lo < hi:
            r0, r1 = (lo - offset) // cols, (hi - offset) // cols
            stride = cols // 128
            base = (offset - begin) // 128
            if by_cols:
                for b in range(cols // D):
                    pieces.append((mat, first + b, r0, r1 - r0, crow, base + r0 * stride + 3 * b, stride))
                    crow += r1 - r0
            else:
                r = r0
                while r < r1:
                    n = min(r1, (r // D + 1) * D) - r
                    pieces.append((mat, first + r // D, r % D, n, crow, base + r * stride, stride))
                    crow += n
                    r += n
        offset += rows * cols
    return pieces


def mm(a, b, ca=1, cb=0):
    return lax.dot_general(a, b, (((ca,), (cb,)), ((), ())), preferred_element_type=F32)


def vspec():
    return pl.BlockSpec(memory_space=pltpu.VMEM)


def hspec():
    return pl.BlockSpec(memory_space=pltpu.HBM)


def in_hbm(x):
    return pltpu.with_memory_space_constraint(x, pltpu.HBM)


def sspec():
    return pl.BlockSpec(memory_space=pltpu.SMEM)


def params_of(mib):
    return pltpu.CompilerParams(vmem_limit_bytes=mib * 1024 * 1024)


def prep_kernel(count, parts, s_ref, p_ref, *refs):
    w_ref = refs[-1]
    for shard in range(count):

        @pl.when(s_ref[0] == shard)
        def _(shard=shard):
            for _, _, _, n, crow, frow, stride in shard_pieces(shard, count):
                for j in range(3):
                    src = pl.ds(frow + j, n, stride=stride)
                    w_ref[crow : crow + n, 128 * j : 128 * j + 128] = p_ref[src, :].astype(BF16)

    for i in range(parts):
        n = refs[i].shape[0]
        row = s_ref[1] * (n * parts) + i * n
        refs[i][...] = w_ref[pl.ds(pl.multiple_of(row, n), n), :]


def prep(sidx, flat, count, parts):
    rows = P_SIZE // count // D
    sd = jax.ShapeDtypeStruct
    outs = (sd((rows // 2 // parts, D), BF16),) * parts if parts else (sd((rows, D), BF16),)
    return pl.pallas_call(
        functools.partial(prep_kernel, count, parts),
        out_shape=outs,
        in_specs=[sspec(), vspec()],
        out_specs=(vspec(),) * len(outs),
        scratch_shapes=[pltpu.VMEM((rows, D), BF16)] if parts else [],
        compiler_params=params_of(4),
        cost_estimate=pl.CostEstimate(flops=0, bytes_accessed=4_000_000, transcendentals=0),
        name="prep",
    )(sidx, flat)


def layer_norm(h):
    center = jnp.mean(h, axis=-1, keepdims=True)
    cent = h - center
    spread = jnp.mean(jnp.square(cent), axis=-1, keepdims=True)
    rstd = lax.rsqrt(spread + LN_EPSILON)
    return cent * rstd, rstd


def layer_norm_grad(xhat, rstd, gx):
    m1 = jnp.mean(gx, axis=-1, keepdims=True)
    m2 = jnp.mean(gx * xhat, axis=-1, keepdims=True)
    return rstd * (gx - m1 - xhat * m2)


def gather_plan(count):
    plan = []
    half = P_SIZE // count // D // 2
    for shard in range(count):
        for _, block, r0, n, crow, _, _ in shard_pieces(shard, count):
            cuts = sorted({crow, crow + n} | {c for c in range(0, 2 * half + 1, half // 2) if crow < c < crow + n})
            for a, b in zip(cuts[:-1], cuts[1:]):
                plan.append((shard, a // half, a % half, b - a, block, r0 + a - crow))
    return plan


def load_weights_fast(s_ref, bufs, wts, own_ready):
    own = bufs[0]
    me, core = s_ref[0], s_ref[1]
    half = own.shape[0] // 2
    quarter = half // 2
    plan = gather_plan(4)

    def move(src, row, n, block, brow):
        size = 96 if n % 96 == 0 else 48

        def chunk(i, carry):
            a = pl.multiple_of(row + i * size, 16)
            b = pl.multiple_of(brow + i * size, 16)
            wts[block, pl.ds(b, size), :] = src[pl.ds(a, size), :]
            return carry

        lax.fori_loop(0, n // size, chunk, 0)

    for shard in range(4):
        for h in range(2):
            pieces = [p for p in plan if p[0] == shard and p[1] == h]
            for m in (1, 2, 3):
                for mine in (True, False):

                    @pl.when(jnp.logical_and(me == (shard ^ m), (core == h) if mine else (core != h)))
                    def _(pieces=pieces, m=m, mine=mine):
                        for _, _, r, n, block, br in pieces:
                            k = r // quarter
                            src = bufs[(1 if mine else 7) + 2 * (m - 1) + k]
                            move(src, r - k * quarter, n, block, br)

    own_ready()
    for shard in range(4):

        @pl.when(me == shard)
        def _(shard=shard):
            for _, h, r, n, block, br in [p for p in plan if p[0] == shard]:
                move(own, h * half + r, n, block, br)


def by_core(value, core):
    half = value.shape[0] // 2
    top, bottom = value[:half], value[half:]
    return jnp.where(core == 0, top, bottom), jnp.where(core == 0, bottom, top)


def main_kernel(nbuf, fast, rows, s_ref, table, tok_hbm, cot_hbm, *refs):
    bufs = refs[:nbuf]
    (blend, qkv, probs, amix_in, gafter, gmx, mods, gmod, silu, wqkv, gout, keep1, send1) = refs[nbuf : nbuf + 13]
    wts, ao_s, aa_s, amix, minp, gmi, mo, tok, cot, own, sems = refs[nbuf + 13 :]
    lat = rows // SEQ
    get_tok = pltpu.make_async_copy(tok_hbm, tok, sems.at[1])
    get_cot = pltpu.make_async_copy(cot_hbm, cot, sems.at[2])
    first = pltpu.make_async_copy(bufs[0], own if fast else wts, sems.at[0])
    first.start()
    get_tok.start()
    get_cot.start()
    if fast:
        load_weights_fast(s_ref, (own,) + bufs[1:], wts, first.wait)
    else:
        first.wait()
    get_tok.wait()
    get_cot.wait()
    nt = table.shape[0]
    lanes = lax.broadcasted_iota(jnp.int32, (16, nt), 1)
    rws = lax.broadcasted_iota(jnp.int32, (16, nt), 0)
    pick = jnp.zeros((16, nt), jnp.bool_)
    for l in range(lat):
        pick = pick | ((rws == l) & (lanes == s_ref[3 + l]))
    cond = mm(pick.astype(F32).astype(BF16), table[...])
    sc = (cond * (1.0 / (1.0 + jnp.exp(-cond)))).astype(BF16)
    silu[...] = sc.astype(F32)
    for b in range(6):
        mods[b] = mm(sc, wts[b])[:8]
    for j in range(3):
        wqkv[j] = wts[6 + j]

    def mod(b, l):
        return mods[b, l : l + 1, :]

    for l in range(lat):
        rs = slice(l * SEQ, (l + 1) * SEQ)
        xhat, _ = layer_norm(tok[rs, :].astype(F32))
        amix_in[rs, :] = (xhat * (1.0 + mod(1, l)) + mod(0, l)).astype(BF16)
    ai = amix_in[...]
    for j in range(3):
        qkv[j] = mm(ai, wts[6 + j]).astype(BF16)

    low = lax.broadcasted_iota(jnp.int32, (SEQ, 128), 1) < HD
    zero = jnp.zeros((SEQ, 128), BF16)

    def attend(l, carry):
        rs = pl.ds(pl.multiple_of(l * SEQ, SEQ), SEQ)
        for hp in range(HEADS // 2):
            cs = slice(hp * 128, hp * 128 + 128)
            q, k, v = qkv[0, rs, cs], qkv[1, rs, cs], qkv[2, rs, cs]
            outs = []
            for h in range(2):
                qm = jnp.where(low if h == 0 else jnp.logical_not(low), q, zero)
                s = mm(qm, k, 1, 1) * HD ** (-0.5)
                top = jnp.max(s, axis=-1, keepdims=True)
                e = jnp.exp(s - top)
                pr = e * (1.0 / jnp.sum(e, axis=-1, keepdims=True))
                probs[l * HEADS + hp * 2 + h] = pr
                outs.append(mm(pr.astype(BF16), v))
            amix[rs, cs] = jnp.where(low, outs[0], outs[1]).astype(BF16)
        return carry

    lax.fori_loop(0, lat, attend, 0)

    ao = mm(amix[...], wts[9])
    ao_s[...] = ao
    for l in range(lat):
        rs = slice(l * SEQ, (l + 1) * SEQ)
        aa = tok[rs, :].astype(F32) + mod(2, l) * ao_s[rs, :]
        aa_s[rs, :] = aa
        xhat, _ = layer_norm(aa)
        minp[rs, :] = (xhat * (1.0 + mod(4, l)) + mod(3, l)).astype(BF16)
        gmx[rs, :] = (cot[rs, :].astype(F32) * mod(5, l)).astype(BF16)
    gmi[...] = jnp.zeros_like(gmi)
    mo[...] = jnp.zeros_like(mo)

    me, core = s_ref[0], s_ref[1]

    def put(value, members, j):
        mine, other = by_core(value, core)
        for i, member in enumerate(members):
            rs = pl.ds(pl.multiple_of(j * 96, 96), 96)
            keep1[member ^ me, rs, :] = mine[96 * i : 96 * i + 96]
            send1[member ^ me, rs, :] = other[96 * i : 96 * i + 96].astype(BF16)

    def mlp(jj, carry):
        j = 2 * jj
        wu = jnp.concatenate([wts[10 + j], wts[11 + j]], axis=1)
        wd = jnp.concatenate([wts[14 + j], wts[15 + j]], axis=0)
        u = mm(minp[...], wu)
        c = math.sqrt(2.0 / math.pi)
        u2 = u * u
        t = jnp.tanh(c * (u + 0.044715 * (u2 * u)))
        half = 0.5 * (1.0 + t)
        act = (u * half).astype(BF16)
        slope = half + 0.5 * u * (1.0 - t * t) * (c * (1.0 + 3.0 * 0.044715 * u2))
        mo[...] += mm(act, wd)
        gmo = gmx[...]
        gp = (mm(gmo, wd, 1, 1) * slope).astype(BF16)
        gd = mm(act, gmo, 0, 0)
        gu = mm(minp[...], gp, 0, 0)
        for i in range(2):
            put(gd[i * D : (i + 1) * D], (3, 1), j + i)
            put(gu[:, i * D : (i + 1) * D], (2, 0), j + i)
        gmi[...] += mm(gp, wu, 1, 1)
        return carry

    lax.fori_loop(0, FF // D // 2, mlp, 0)

    gmod[...] = jnp.zeros_like(gmod)
    for l in range(lat):
        rs = slice(l * SEQ, (l + 1) * SEQ)
        up = cot[rs, :].astype(F32)
        blend[rs, :] = (aa_s[rs, :] + mod(5, l) * mo[rs, :]).astype(BF16)
        gmod[5, l : l + 1, :] = jnp.sum(up * mo[rs, :], axis=0, keepdims=True)
        xhat, rstd = layer_norm(aa_s[rs, :])
        g = gmi[rs, :]
        gmod[3, l : l + 1, :] = jnp.sum(g, axis=0, keepdims=True)
        gmod[4, l : l + 1, :] = jnp.sum(g * xhat, axis=0, keepdims=True)
        ga = up + layer_norm_grad(xhat, rstd, g * (1.0 + mod(4, l)))
        gafter[rs, :] = ga
        gmod[2, l : l + 1, :] = jnp.sum(ga * ao_s[rs, :], axis=0, keepdims=True)
        minp[rs, :] = (ga * mod(2, l)).astype(BF16)
    gao = minp[...]
    gout[...] = mm(amix[...], gao, 0, 0)
    gmx[...] = mm(gao, wts[9], 1, 1).astype(BF16)


def main_call(sidx, table, tokens, cotangent, bufs, fast):
    rows = tokens.shape[0]
    lat = rows // SEQ
    sd = jax.ShapeDtypeStruct
    outs = (
        sd((rows, D), BF16),
        sd((3, rows, D), BF16),
        sd((lat * HEADS, SEQ, SEQ), F32),
        sd((rows, D), BF16),
        sd((rows, D), F32),
        sd((rows, D), BF16),
        sd((6, 8, D), F32),
        sd((6, 8, D), F32),
        sd((16, D), F32),
        sd((3, D, D), BF16),
        sd((D, D), F32),
        sd((4, D, D), F32),
        sd((4, D, D), BF16),
    )
    return pl.pallas_call(
        functools.partial(main_kernel, len(bufs), fast, rows),
        out_shape=outs,
        in_specs=[sspec(), vspec(), hspec(), hspec(), hspec()] + [vspec()] * (len(bufs) - 1),
        out_specs=(vspec(),) * len(outs),
        scratch_shapes=[
            pltpu.VMEM((NBLOCKS, D, D), BF16),
            pltpu.VMEM((rows, D), F32),
            pltpu.VMEM((rows, D), F32),
            pltpu.VMEM((rows, D), BF16),
            pltpu.VMEM((rows, D), BF16),
            pltpu.VMEM((rows, D), F32),
            pltpu.VMEM((rows, D), F32),
            pltpu.VMEM((rows, D), BF16),
            pltpu.VMEM((rows, D), BF16),
            pltpu.VMEM(bufs[0].shape if fast else (16, D), BF16),
            pltpu.SemaphoreType.DMA((3,)),
        ],
        compiler_params=params_of(30),
        cost_estimate=pl.CostEstimate(flops=20_000_000_000, bytes_accessed=30_000_000, transcendentals=0),
        name="main",
    )(sidx, table, *(in_hbm(x) for x in (tokens, cotangent, bufs[0])), *bufs[1:])


def heads_kernel(rows, qkv, probs, gmx, gqkv):
    lat = rows // SEQ
    low = lax.broadcasted_iota(jnp.int32, (SEQ, 128), 1) < HD
    zero = jnp.zeros((SEQ, 128), BF16)

    def back(l, carry):
        rs = pl.ds(pl.multiple_of(l * SEQ, SEQ), SEQ)
        for hp in range(HEADS // 2):
            cs = slice(hp * 128, hp * 128 + 128)
            q, k, v = qkv[0, rs, cs], qkv[1, rs, cs], qkv[2, rs, cs]
            g = gmx[rs, cs]
            res = []
            for h in range(2):
                p = probs[l * HEADS + hp * 2 + h]
                gm = jnp.where(low if h == 0 else jnp.logical_not(low), g, zero)
                gv = mm(p.astype(BF16), g, 0, 0)
                gpr = mm(gm, v, 1, 1)
                dots = jnp.sum(p * gpr, axis=-1, keepdims=True)
                gs = (p * (gpr - dots) * HD ** (-0.5)).astype(BF16)
                res.append((mm(gs, k), mm(gs, q, 0, 0), gv))
            for j in range(3):
                gqkv[j, rs, cs] = jnp.where(low, res[0][j], res[1][j]).astype(BF16)
        return carry

    lax.fori_loop(0, lat, back, 0)


def heads_call(qkv, probs, gmx):
    rows = gmx.shape[0]
    return pl.pallas_call(
        functools.partial(heads_kernel, rows),
        out_shape=jax.ShapeDtypeStruct((3, rows, D), BF16),
        in_specs=[vspec()] * 3,
        out_specs=vspec(),
        compiler_params=params_of(4),
        cost_estimate=pl.CostEstimate(flops=6_000_000_000, bytes_accessed=6_000_000, transcendentals=0),
        name="heads",
    )(qkv, probs, gmx)


def input_kernel(rows, s_ref, tok, gqkv, ai, gafter, mods, gmod1, silu, wqkv, gout, gtok, keep2, send2, keep, srow):
    me, core = s_ref[0], s_ref[1]
    lat = rows // SEQ
    gai = None
    for j in range(4):
        if j < 3:
            part = mm(gqkv[j], wqkv[j], 1, 1)
            gai = part if gai is None else gai + part
            value = mm(ai[...], gqkv[j], 0, 0)
        else:
            value = gout[...]
        mine, other = by_core(value, core)
        for m in range(4):
            rs = slice(48 * j, 48 * j + 48)
            keep2[m ^ me, rs, :] = mine[48 * m : 48 * m + 48]
            send2[m ^ me, rs, :] = other[48 * m : 48 * m + 48].astype(BF16)
    srow[...] = jnp.zeros_like(srow)
    for l in range(lat):
        rs = slice(l * SEQ, (l + 1) * SEQ)
        xhat, rstd = layer_norm(tok[rs, :].astype(F32))
        g = gai[rs, :]
        srow[l : l + 1, :] = jnp.sum(g, axis=0, keepdims=True)
        srow[lat + l : lat + l + 1, :] = jnp.sum(g * xhat, axis=0, keepdims=True)
        gtok[rs, :] = gafter[rs, :] + layer_norm_grad(xhat, rstd, g * (1.0 + mods[1, l : l + 1, :]))
        for b in range(2, 6):
            srow[lat * b + l : lat * b + l + 1, :] = gmod1[b, l : l + 1, :]
        srow[lat * 6 + l : lat * 6 + l + 1, :] = silu[l : l + 1, :]
    keep[...] = srow[...].astype(BF16)


def input_call(sidx, tokens, gqkv, ai, gafter, mods, gmod1, silu, wqkv, gout):
    rows = tokens.shape[0]
    sd = jax.ShapeDtypeStruct
    outs = (sd((rows, D), F32), sd((4, D // 2, D), F32), sd((4, D // 2, D), BF16), sd((KEPT_ROWS, D), BF16))
    return pl.pallas_call(
        functools.partial(input_kernel, rows),
        out_shape=outs,
        in_specs=[sspec()] + [vspec()] * 9,
        out_specs=(vspec(),) * 4,
        scratch_shapes=[pltpu.VMEM((KEPT_ROWS, D), F32)],
        compiler_params=params_of(6),
        cost_estimate=pl.CostEstimate(flops=6_000_000_000, bytes_accessed=6_000_000, transcendentals=0),
        name="input",
    )(sidx, tokens, gqkv, ai, gafter, mods, gmod1, silu, wqkv, gout)


def split(x):
    hi = x.astype(BF16)
    return hi, (x - hi.astype(F32)).astype(BF16)


POLY = (COEFF_C, COEFF_B, COEFF_A)
PLAIN = (1.0, 0.0, 0.0)
STEPS = (
    (0, 0, 2, 1, POLY),
    (2, 0, 3, 2, PLAIN),
    (3, 2, 0, 2, PLAIN),
    (0, 0, 1, 1, POLY),
    (1, 2, 2, 3, PLAIN),
    (1, 0, 3, 2, PLAIN),
    (3, 1, 0, 2, PLAIN),
    (0, 0, 1, 3, POLY),
    (1, 2, 2, 3, PLAIN),
)


def step_tables():
    ints = jnp.array([x for st in STEPS for x in st[:4]], jnp.int32)
    coeffs = jnp.array([x for st in STEPS for x in st[4]], F32)
    return ints, coeffs


def either(flipped, tall, wide):
    if flipped is None:
        wide()
    else:
        pl.when(flipped)(tall)
        pl.when(jnp.logical_not(flipped))(wide)


def newton_schulz(ints, coeffs, mat_ref, upd_ref, bufs, npairs, flipped, factor):
    bufs[0] = jnp.zeros((D, D), F32)

    def gram(b, carry):
        x0, x1 = mat_ref[2 * b].astype(BF16), mat_ref[2 * b + 1].astype(BF16)

        def tall():
            x = jnp.concatenate([x0, x1], axis=0)
            bufs[0] += mm(x, x, 0, 0)

        def wide():
            x = jnp.concatenate([x0, x1], axis=1)
            bufs[0] += mm(x, x, 1, 1)

        either(flipped, tall, wide)

        return carry

    lax.fori_loop(0, npairs, gram, 0)
    g = bufs[0]
    ri = lax.broadcasted_iota(jnp.int32, (D, D), 0)
    ci = lax.broadcasted_iota(jnp.int32, (D, D), 1)
    eye = jnp.where(ri == ci, 1.0, 0.0)
    diag = jnp.sum(g * eye, axis=1, keepdims=True)
    total = jnp.sum(diag, axis=0, keepdims=True)
    inv = 1.0 / (jnp.sqrt(total) + 1e-07)
    bufs[0] = g * (inv * inv)

    def step(k, carry):
        i, j, d, passes = (ints[4 * k + n] for n in range(4))

        def product(count):
            x = bufs[i]
            xh, xl = split(x)
            yh, yl = split(bufs[j])
            lhs = (xh, xl, xh)[:count]
            rhs = (yh, yh, yl)[:count]
            prod = mm(jnp.concatenate(lhs, axis=1), jnp.concatenate(rhs, axis=0))
            r0 = lax.broadcasted_iota(jnp.int32, (D, D), 0)
            r1 = lax.broadcasted_iota(jnp.int32, (D, D), 1)
            ident = jnp.where(r0 == r1, coeffs[3 * k + 2], 0.0)
            bufs[d] = coeffs[3 * k] * prod + (coeffs[3 * k + 1] * x + ident)

        for count in (1, 2, 3):
            pl.when(passes == count)(functools.partial(product, count))
        return carry

    lax.fori_loop(0, len(STEPS), step, 0)
    bufs[0] = bufs[2] * (inv * factor)

    def apply(b, carry):
        wh, wl = split(bufs[0])
        xs = [mat_ref[2 * b + i] for i in range(2)]

        def tall():
            for i in range(2):
                x = xs[i].astype(BF16)
                upd_ref[2 * b + i] = mm(
                    jnp.concatenate([x, x], axis=1), jnp.concatenate([wh, wl], axis=0)
                )

        def wide():
            x = jnp.concatenate([xs[0].astype(BF16), xs[1].astype(BF16)], axis=1)
            out = mm(jnp.concatenate([wh, wl], axis=1), jnp.concatenate([x, x], axis=0))
            upd_ref[2 * b] = out[:, :D]
            upd_ref[2 * b + 1] = out[:, D:]

        either(flipped, tall, wide)
        return carry

    lax.fori_loop(0, npairs, apply, 0)


def take_first(s_ref, chunks, dst):
    me, core, zed = s_ref[0], s_ref[1], s_ref[2]
    for c, ref in enumerate(chunks):
        for y in range(2):
            part = ((me // 2) ^ 1) ^ y
            rs = pl.ds(pl.multiple_of((core ^ c) * 192 + part * 96, 96), 96)
            for z in range(4):
                dst[zed ^ z, rs, :] = ref[y, z].astype(F32)


def take_second(s_ref, chunks, dst):
    me, core, zed = s_ref[0], s_ref[1], s_ref[2]
    for c, ref in enumerate(chunks):
        for m in range(4):
            rs = pl.ds(pl.multiple_of((core ^ c) * 192 + (me ^ m) * 48, 48), 48)
            for z in range(4):
                dst[zed ^ z, rs, :] = ref[m, z].astype(F32)


def adaln_grads(kept, grd, kf):
    ndev = 2 * kept[0].shape[0] // KEPT_ROWS
    for i, ref in enumerate(kept):
        n = ref.shape[0]
        for j in range(3):
            kf[j, i * n : (i + 1) * n, :] = ref[:, 128 * j : 128 * j + 128].astype(F32)

    def rows(first):
        part = [kf[j, pl.ds(first, ndev, stride=KEPT_ROWS), :] for j in range(3)]
        return jnp.concatenate(part, axis=1).astype(BF16)

    sil = jnp.concatenate([rows(12), rows(13)], axis=0)
    for b in range(6):
        gm = jnp.concatenate([rows(2 * b), rows(2 * b + 1)], axis=0)
        grd[b] = mm(sil, gm, 0, 0)


def add_momentum(t, target, mom, grd, mat, base=0):
    first = MATS[target][2]
    for _, block, r0, n, _, frow, stride in [p for p in shard_pieces(t, 4) if p[0] == target]:
        b = block - first
        for j in range(3):
            cs = slice(128 * j, 128 * j + 128)
            m = mom[pl.ds(frow + j, n, stride=stride), :]
            mat[b, r0 : r0 + n, cs] = MOMENTUM_RATE * m + grd[base + b, r0 : r0 + n, cs]


def add_foreign(s_ref, t, target, foreign, grd, mat):
    core = s_ref[1]
    half = foreign[0].shape[0]
    for _, block, r0, n, crow, _, _ in [p for p in shard_pieces(t ^ 1, 4) if p[0] == target]:
        b = block - MATS[target][2]
        cuts = sorted({crow, crow + n} | {c for c in (half,) if crow < c < crow + n})
        for lo, hi in zip(cuts[:-1], cuts[1:]):
            h = lo // half
            for mine, src in enumerate(foreign):

                @pl.when(core == (h ^ mine))
                def _(b=b, r0=r0, lo=lo, hi=hi, h=h, crow=crow, src=src):
                    dst = slice(r0 + lo - crow, r0 + hi - crow)
                    m = src[lo - h * half : hi - h * half, :].astype(F32)
                    mat[b, dst, :] = MOMENTUM_RATE * m + grd[b, dst, :]


TAIL = 48


def ns_a_kernel(s_ref, ints, coeffs, mom, fx0, fx1, kz0, kz1, ch0, ch1, upd, grd, tail, mat, bufs, kf):
    me = s_ref[0]

    @pl.when(me < 2)
    def _():
        adaln_grads((kz0, kz1), grd, kf)

    @pl.when(me >= 2)
    def _():
        take_first(s_ref, (ch0, ch1), grd)

    for t, target in enumerate((ADALN, ADALN, UP, DOWN)):

        @pl.when(me == t)
        def _(t=t, target=target):
            add_momentum(t, target, mom, grd, mat)
            if target != DOWN:
                add_foreign(s_ref, t, target, (fx0, fx1), grd, mat)

    npairs = jnp.where(me < 2, 3, 2)
    factor = jnp.where(me < 2, update_scale(ADALN), update_scale(UP))
    newton_schulz(ints, coeffs, mat, upd, bufs, npairs, me == 3, factor)

    for b in range(4):
        rs = slice(TAIL * b, TAIL * b + TAIL)
        tail[0, rs, :] = grd[b, D - TAIL :, :].astype(BF16)
        tail[1, rs, :] = upd[b, D - TAIL :, :].astype(BF16)


def ns_a(sidx, tables, mom, foreign, kept, chunks):
    sd = jax.ShapeDtypeStruct((6, D, D), F32)
    return pl.pallas_call(
        ns_a_kernel,
        out_shape=(sd, sd, jax.ShapeDtypeStruct((2, 4 * TAIL, D), BF16)),
        in_specs=[sspec()] * 3 + [vspec()] * 7,
        out_specs=(vspec(),) * 3,
        scratch_shapes=[
            pltpu.VMEM((6, D, D), F32),
            pltpu.VMEM((4, D, D), F32),
            pltpu.VMEM((3, 2 * kept[0].shape[0], 128), F32),
        ],
        compiler_params=params_of(14),
        cost_estimate=pl.CostEstimate(flops=8_000_000_000, bytes_accessed=12_000_000, transcendentals=0),
        name="ns_a",
    )(sidx, *tables, mom, *foreign, *kept, *chunks)


def final_kernel(
    s_ref, ints, coeffs, par, mom, ch0, ch1, upa, grda, tail, ograd, onew, omom, upb, gb, mat, bufs
):
    me = s_ref[0]
    inner = jnp.logical_or(me == 1, me == 2)

    @pl.when(inner)
    def _():
        take_second(s_ref, (ch0, ch1), gb)
        for b in range(1, 4):
            mat[b] = jnp.zeros((D, D), F32)

    @pl.when(me == 1)
    def _():
        add_momentum(1, QKV, mom, gb, mat)

    @pl.when(me == 2)
    def _():
        add_momentum(2, OUTW, mom, gb, mat, 3)

    @pl.when(inner)
    def _():
        npairs = jnp.where(me == 1, 2, 1)
        factor = jnp.where(me == 1, update_scale(QKV), update_scale(OUTW))
        newton_schulz(ints, coeffs, mat, upb, bufs, npairs, None, factor)

    for t in range(4):

        @pl.when(me == t)
        def _(t=t):
            for mat_id, block, r0, n, crow, frow, stride in shard_pieces(t, 4):
                b = block - MATS[mat_id][2]
                for j in range(3):
                    cs = slice(128 * j, 128 * j + 128)
                    fl = pl.ds(frow + j, n, stride=stride)
                    if mat_id == UP and t == 3:
                        assert r0 == D - TAIL and n == TAIL
                        g = tail[0, TAIL * b : TAIL * b + TAIL, cs].astype(F32)
                        u = tail[1, TAIL * b : TAIL * b + TAIL, cs].astype(F32)
                    elif mat_id in (QKV, OUTW):
                        g = gb[b + 3 * (mat_id == OUTW), r0 : r0 + n, cs]
                        u = upb[b, r0 : r0 + n, cs]
                    else:
                        g = grda[b, r0 : r0 + n, cs]
                        u = upa[b, r0 : r0 + n, cs]
                    ograd[fl, :] = g
                    omom[fl, :] = MOMENTUM_RATE * mom[fl, :] + g
                    onew[fl, :] = par[fl, :] - u


def final_call(sidx, tables, par, mom, chunks, upa, grda, tail):
    sd = jax.ShapeDtypeStruct(par.shape, F32)
    block4 = pltpu.VMEM((4, D, D), F32)
    return pl.pallas_call(
        final_kernel,
        out_shape=(sd, sd, sd),
        in_specs=[sspec()] * 3 + [vspec()] * 7,
        out_specs=(vspec(),) * 3,
        scratch_shapes=[block4, block4, block4, block4],
        compiler_params=params_of(20),
        cost_estimate=pl.CostEstimate(flops=8_000_000_000, bytes_accessed=24_000_000, transcendentals=0),
        name="finish",
    )(sidx, *tables, par, mom, *chunks, upa, grda, tail)


def swap(x, axis, mask):
    count = lax.axis_size(axis)
    return lax.ppermute(x, axis, [(i, i ^ mask) for i in range(count)])


def more_rows(x, hops):
    for axis, mask in hops:
        x = jnp.concatenate([x, swap(x, axis, mask)], axis=0)
    return x


def wide_sum(parts):
    total = None
    for p in parts:
        total = p.astype(F32) if total is None else total + p.astype(F32)
    return total


def at(x, i):
    return lax.dynamic_index_in_dim(x, i, 0, keepdims=False)


def z_scatter(s, zed, extra=None):
    size = s.shape[0] // 4
    blocks = s.reshape(4, size, D)
    got = []
    for m in (1, 2, 3):
        piece = at(blocks, zed ^ m).astype(BF16)
        if extra is not None:
            piece = jnp.concatenate([piece, extra], axis=0)
        got.append(swap(piece, "rep", 2 * m))
    total = wide_sum([at(blocks, zed)] + [g[:size] for g in got]).astype(BF16)
    if extra is None:
        return total
    return total, jnp.concatenate([extra] + [g[size:] for g in got], axis=0)


def fan(x, axis, masks):
    got = [x]
    for m in masks:
        got.append(swap(x, axis, m))
    return jnp.stack(got)


def fast_device(tokens, conditions, assignment, params, momentum, cotangent):
    return fast_body(tokens, conditions, assignment, params, momentum, cotangent)


def fast_body(tokens, conditions, assignment, params, momentum, cotangent):
    me = lax.axis_index("fsdp")
    rep = lax.axis_index("rep")
    core, zed = rep % 2, rep // 2
    lat = tokens.shape[0]
    rows = lat * SEQ
    par = params.reshape(-1, 128)
    mom = momentum.reshape(-1, 128)
    source = assignment // lat
    apart = ((source // 8) ^ me) + 4 * ((source % 8) ^ rep)
    pick = apart * lat + assignment % lat
    sidx = jnp.concatenate([jnp.stack([me, core, zed]), pick]).astype(jnp.int32)

    hop = swap(conditions, "fsdp", 1)
    top, bottom = prep(sidx, par, 4, 2)
    table = jnp.concatenate([conditions, hop], axis=0)
    table, top, bottom = lax.optimization_barrier((table, top, bottom))
    hop = swap(table, "fsdp", 2)
    x0 = swap(top, "fsdp", 1)
    y1 = swap(bottom, "fsdp", 2)
    x1 = swap(bottom, "fsdp", 1)
    y0 = swap(top, "fsdp", 2)
    table = jnp.concatenate([table, hop], axis=0)
    table = more_rows(table, (("rep", 1),))
    table = more_rows(table, (("rep", 2), ("rep", 4)))
    x0, y1, table = lax.optimization_barrier((x0, y1, table))
    d0 = swap(x0, "fsdp", 2)
    d1 = swap(y1, "fsdp", 1)
    received = (x0, x1, y0, y1, d0, d1)
    (wc,) = prep(sidx, par, 4, 0)
    bufs = (wc,) + received + tuple(swap(r, "rep", 1) for r in received)
    (mh,) = prep(sidx, mom, 4, 1)
    fx0 = swap(mh, "fsdp", 1)

    tok2, cot2 = tokens.reshape(rows, D), cotangent.reshape(rows, D)
    (blend, qkv, probs, ai, gafter, gmx, mods, gmod1, silu, wqkv, gout, keep1, send1) = main_call(
        sidx, table, tok2, cot2, bufs, True
    )
    fx1 = swap(fx0, "rep", 1)

    other = swap(send1, "rep", 1)
    gqkv = heads_call(qkv, probs, gmx)
    got = []
    for m in (1, 2, 3):
        got.append(swap((keep1[m] + other[m].astype(F32)).astype(BF16), "fsdp", m))
    gtok, keep2, send2, keep = input_call(sidx, tok2, gqkv, ai, gafter, mods, gmod1, silu, wqkv, gout)
    s1 = wide_sum([keep1[0] + other[0].astype(F32)] + got)
    col = fan(z_scatter(s1, zed), "rep", (2, 4, 6))
    pair = fan(col, "fsdp", (2,))
    pairs = (pair, swap(pair, "rep", 1))

    other = swap(send2, "rep", 1)
    got = []
    for m in (1, 2, 3):
        part = (keep2[m] + other[m].astype(F32)).astype(BF16)
        got.append(swap(jnp.concatenate([part, keep], axis=0), "fsdp", m))
    size = keep2.shape[1]
    s2 = wide_sum([keep2[0] + other[0].astype(F32)] + [g[:size] for g in got])
    q2, kz = z_scatter(s2, zed, jnp.concatenate([keep] + [g[size:] for g in got], axis=0))
    kept = (kz, swap(kz, "rep", 1))
    quad = fan(fan(q2, "rep", (2, 4, 6)), "fsdp", (1, 2, 3))
    quads = (quad, swap(quad, "rep", 1))

    tables = step_tables()
    upa, grda, tail = ns_a(sidx, tables, mom, (fx0, fx1), kept, pairs)
    tail = lax.ppermute(tail, "fsdp", [(2, 3)])
    ograd, onew, omom = final_call(sidx, tables, par, mom, quads, upa, grda, tail)
    shape = tokens.shape
    return (
        blend.reshape(shape),
        gtok.reshape(shape),
        ograd.reshape(-1),
        onew.reshape(-1),
        omom.reshape(-1),
    )


def unpack(flat):
    pieces, offset = [], 0
    for rows_count, cols_count, _, _ in MATS:
        pieces.append(flat[offset : offset + rows_count * cols_count].reshape(rows_count, cols_count))
        offset += rows_count * cols_count
    return pieces


def to_blocks(mats):
    out = []
    for matrix, (rows_count, cols_count, _, by_cols) in zip(mats, MATS):
        if by_cols:
            out.append(matrix.reshape(D, cols_count // D, D).transpose(1, 0, 2))
        else:
            out.append(matrix.reshape(rows_count // D, D, D))
    return jnp.concatenate(out, axis=0)


def from_blocks(blocks, by_cols):
    if by_cols:
        return blocks.transpose(1, 0, 2).reshape(-1)
    return blocks.reshape(-1)


def orthogonalize(matrix):
    flipped = matrix.shape[0] > matrix.shape[1]
    current = matrix.T if flipped else matrix
    current = current / (jnp.sqrt(jnp.sum(current * current)) + 1e-07)
    for _ in range(NS_ITERS):
        square = jnp.dot(current, current.T, precision=lax.Precision.HIGHEST)
        polynomial = COEFF_B * square + COEFF_C * jnp.dot(square, square, precision=lax.Precision.HIGHEST)
        current = COEFF_A * current + jnp.dot(polynomial, current, precision=lax.Precision.HIGHEST)
    return current.T if flipped else current


def scaled_update(matrix, factor):
    return (factor * orthogonalize(matrix)).reshape(-1)


def empty_update(matrix, factor):
    return jnp.zeros((matrix.shape[0] * matrix.shape[1],), F32)


def any_device(tokens, conditions, assignment, params, momentum, cotangent):
    lat = tokens.shape[0]
    rows = lat * SEQ
    table = lax.all_gather(conditions, ("fsdp", "rep"), axis=0, tiled=True)
    gathered = lax.all_gather(params.astype(BF16), "fsdp", axis=0, tiled=True)
    blocks = to_blocks(unpack(gathered))
    me = lax.axis_index("fsdp")
    sidx = jnp.concatenate([jnp.zeros((3,), jnp.int32), assignment.astype(jnp.int32)])
    tok2, cot2 = tokens.reshape(rows, D), cotangent.reshape(rows, D)
    (blend, qkv, probs, ai, gafter, gmx, mods, gmod1, silu, wqkv, gout, keep1, send1) = main_call(
        sidx, table, tok2, cot2, (blocks,), False
    )
    gqkv = heads_call(qkv, probs, gmx)
    gtok, keep2, send2, keep = input_call(sidx, tok2, gqkv, ai, gafter, mods, gmod1, silu, wqkv, gout)
    halves1 = jnp.stack([keep1, send1.astype(F32)]).reshape(2, 4, 4, 96, D)
    up = halves1[:, jnp.array([2, 0])].transpose(2, 0, 1, 3, 4).reshape(4, D, D)
    down = halves1[:, jnp.array([3, 1])].transpose(2, 0, 1, 3, 4).reshape(4, D, D)
    halves2 = jnp.stack([keep2, send2.astype(F32)]).reshape(2, 4, 4, 48, D)
    last = halves2.transpose(2, 0, 1, 3, 4).reshape(4, D, D)
    rest = jnp.concatenate(
        [from_blocks(last[:3], True), last[3].reshape(-1), from_blocks(up, True), down.reshape(-1)]
    )
    kept = lax.all_gather(keep, ("fsdp", "rep"), axis=0, tiled=True).reshape(-1, KEPT_ROWS, D)
    silu_all = kept[:, 6 * lat : 7 * lat].reshape(-1, D)
    mod_all = kept[:, : 6 * lat].reshape(-1, 6, lat, D).transpose(0, 2, 1, 3).reshape(-1, 6 * D)
    adaln = lax.dot_general(silu_all, mod_all, (((0,), (0,)), ((), ())), preferred_element_type=F32)
    shard_len = params.shape[0]
    head = jnp.concatenate([adaln.reshape(-1), jnp.zeros_like(rest)])
    flat = jnp.concatenate([jnp.zeros((D * 6 * D,), F32), rest])
    part = lax.psum_scatter(flat, "fsdp", scatter_dimension=0, tiled=True)
    full_grad = lax.psum(part, "rep") + lax.dynamic_slice_in_dim(head, me * shard_len, shard_len, 0)
    new_momentum = MOMENTUM_RATE * momentum + full_grad
    whole_mom = lax.all_gather(new_momentum, "fsdp", axis=0, tiled=True)
    group_size = lax.axis_size("fsdp")
    updates, offset = [], 0
    for mat, piece in enumerate(unpack(whole_mom)):
        factor = F32(update_scale(mat))
        owner = (offset // shard_len + group_size // 2) % group_size
        updates.append(lax.cond(me == owner, scaled_update, empty_update, piece, factor))
        offset += piece.size
    update = lax.psum_scatter(jnp.concatenate(updates), "fsdp", scatter_dimension=0, tiled=True)
    shape = tokens.shape
    return (blend.reshape(shape), gtok.reshape(shape), full_grad, params - update, new_momentum)


def solution(mesh):
    both = ("fsdp", "rep")
    in_specs = (P(both, None, None), P(both, None), P(both), P("fsdp"), P("fsdp"), P(both, None, None))
    out_specs = (P(both, None, None), P(both, None, None), P("fsdp"), P("fsdp"), P("fsdp"))
    small = dict(mesh.shape) == {"fsdp": 4, "rep": 8}
    return jax.shard_map(
        fast_device if small else any_device,
        mesh=mesh,
        in_specs=in_specs,
        out_specs=out_specs,
        check_vma=False,
    )
```

```python
import functools
import math

import jax
import jax.numpy as jnp
from jax import lax
from jax.experimental import pallas as pl
from jax.experimental.pallas import tpu as pltpu
from jax.sharding import PartitionSpec as P


D = 384
HEADS = 6
HD = 64
FF = 1536
SEQ = 256
NS_ITERS = 3

LN_EPSILON = 1e-06
MOMENTUM_RATE = 0.95
LEARN_RATE = 0.2
COEFF_A = 3.4445
COEFF_B = -4.775
COEFF_C = 2.0315


F32 = jnp.float32
BF16 = jnp.bfloat16

MATS = ((D, 6 * D, 0, True), (D, 3 * D, 6, True), (D, D, 9, True), (D, FF, 10, True), (FF, D, 14, False))
NBLOCKS = 18
ADALN, QKV, OUTW, UP, DOWN = range(5)
P_SIZE = sum(m[0] * m[1] for m in MATS)
KEPT_ROWS = 16


def update_scale(mat):
    return LEARN_RATE * 0.2 * math.sqrt(max(MATS[mat][0], MATS[mat][1]))


def shard_pieces(shard, count):
    size = P_SIZE // count
    begin, end = shard * size, (shard + 1) * size
    pieces, crow, offset = [], 0, 0
    for mat, (rows, cols, first, by_cols) in enumerate(MATS):
        lo, hi = max(begin, offset), min(end, offset + rows * cols)
        if lo < hi:
            r0, r1 = (lo - offset) // cols, (hi - offset) // cols
            stride = cols // 128
            base = (offset - begin) // 128
            if by_cols:
                for b in range(cols // D):
                    pieces.append((mat, first + b, r0, r1 - r0, crow, base + r0 * stride + 3 * b, stride))
                    crow += r1 - r0
            else:
                r = r0
                while r < r1:
                    n = min(r1, (r // D + 1) * D) - r
                    pieces.append((mat, first + r // D, r % D, n, crow, base + r * stride, stride))
                    crow += n
                    r += n
        offset += rows * cols
    return pieces


def mm(a, b, ca=1, cb=0):
    return lax.dot_general(a, b, (((ca,), (cb,)), ((), ())), preferred_element_type=F32)


def vspec():
    return pl.BlockSpec(memory_space=pltpu.VMEM)


def hspec():
    return pl.BlockSpec(memory_space=pltpu.HBM)


def in_hbm(x):
    return pltpu.with_memory_space_constraint(x, pltpu.HBM)


def sspec():
    return pl.BlockSpec(memory_space=pltpu.SMEM)


def params_of(mib):
    return pltpu.CompilerParams(vmem_limit_bytes=mib * 1024 * 1024)


def prep_kernel(count, parts, s_ref, p_ref, *refs):
    w_ref = refs[-1]
    for shard in range(count):

        @pl.when(s_ref[0] == shard)
        def _(shard=shard):
            for _, _, _, n, crow, frow, stride in shard_pieces(shard, count):
                for j in range(3):
                    src = pl.ds(frow + j, n, stride=stride)
                    w_ref[crow : crow + n, 128 * j : 128 * j + 128] = p_ref[src, :].astype(BF16)

    for i in range(parts):
        n = refs[i].shape[0]
        row = s_ref[1] * (n * parts) + i * n
        refs[i][...] = w_ref[pl.ds(pl.multiple_of(row, n), n), :]


def prep(sidx, flat, count, parts):
    rows = P_SIZE // count // D
    sd = jax.ShapeDtypeStruct
    outs = (sd((rows // 2 // parts, D), BF16),) * parts if parts else (sd((rows, D), BF16),)
    return pl.pallas_call(
        functools.partial(prep_kernel, count, parts),
        out_shape=outs,
        in_specs=[sspec(), vspec()],
        out_specs=(vspec(),) * len(outs),
        scratch_shapes=[pltpu.VMEM((rows, D), BF16)] if parts else [],
        compiler_params=params_of(4),
        cost_estimate=pl.CostEstimate(flops=0, bytes_accessed=4_000_000, transcendentals=0),
        name="prep",
    )(sidx, flat)


def layer_norm(h):
    center = jnp.mean(h, axis=-1, keepdims=True)
    cent = h - center
    spread = jnp.mean(jnp.square(cent), axis=-1, keepdims=True)
    rstd = lax.rsqrt(spread + LN_EPSILON)
    return cent * rstd, rstd


def layer_norm_grad(xhat, rstd, gx):
    m1 = jnp.mean(gx, axis=-1, keepdims=True)
    m2 = jnp.mean(gx * xhat, axis=-1, keepdims=True)
    return rstd * (gx - m1 - xhat * m2)


def gather_plan(count):
    plan = []
    half = P_SIZE // count // D // 2
    for shard in range(count):
        for _, block, r0, n, crow, _, _ in shard_pieces(shard, count):
            cuts = sorted({crow, crow + n} | {c for c in range(0, 2 * half + 1, half // 2) if crow < c < crow + n})
            for a, b in zip(cuts[:-1], cuts[1:]):
                plan.append((shard, a // half, a % half, b - a, block, r0 + a - crow))
    return plan


def load_weights_fast(s_ref, bufs, wts, own_ready):
    own = bufs[0]
    me, core = s_ref[0], s_ref[1]
    half = own.shape[0] // 2
    quarter = half // 2
    plan = gather_plan(4)

    def move(src, row, n, block, brow):
        size = 96 if n % 96 == 0 else 48

        def chunk(i, carry):
            a = pl.multiple_of(row + i * size, 16)
            b = pl.multiple_of(brow + i * size, 16)
            wts[block, pl.ds(b, size), :] = src[pl.ds(a, size), :]
            return carry

        lax.fori_loop(0, n // size, chunk, 0)

    for shard in range(4):
        for h in range(2):
            pieces = [p for p in plan if p[0] == shard and p[1] == h]
            for m in (1, 2, 3):
                for mine in (True, False):

                    @pl.when(jnp.logical_and(me == (shard ^ m), (core == h) if mine else (core != h)))
                    def _(pieces=pieces, m=m, mine=mine):
                        for _, _, r, n, block, br in pieces:
                            k = r // quarter
                            src = bufs[(1 if mine else 7) + 2 * (m - 1) + k]
                            move(src, r - k * quarter, n, block, br)

    own_ready()
    for shard in range(4):

        @pl.when(me == shard)
        def _(shard=shard):
            for _, h, r, n, block, br in [p for p in plan if p[0] == shard]:
                move(own, h * half + r, n, block, br)


def by_core(value, core):
    half = value.shape[0] // 2
    top, bottom = value[:half], value[half:]
    return jnp.where(core == 0, top, bottom), jnp.where(core == 0, bottom, top)


def main_kernel(nbuf, fast, rows, s_ref, table, tok_hbm, cot_hbm, *refs):
    bufs = refs[:nbuf]
    (blend, qkv, probs, amix_in, gafter, gmx, mods, gmod, silu, wqkv, gout, keep1, send1) = refs[nbuf : nbuf + 13]
    wts, ao_s, aa_s, amix, minp, gmi, mo, tok, cot, own, sems = refs[nbuf + 13 :]
    lat = rows // SEQ
    get_tok = pltpu.make_async_copy(tok_hbm, tok, sems.at[1])
    get_cot = pltpu.make_async_copy(cot_hbm, cot, sems.at[2])
    first = pltpu.make_async_copy(bufs[0], own if fast else wts, sems.at[0])
    first.start()
    get_tok.start()
    get_cot.start()
    if fast:
        load_weights_fast(s_ref, (own,) + bufs[1:], wts, first.wait)
    else:
        first.wait()
    get_tok.wait()
    get_cot.wait()
    nt = table.shape[0]
    lanes = lax.broadcasted_iota(jnp.int32, (16, nt), 1)
    rws = lax.broadcasted_iota(jnp.int32, (16, nt), 0)
    pick = jnp.zeros((16, nt), jnp.bool_)
    for l in range(lat):
        pick = pick | ((rws == l) & (lanes == s_ref[3 + l]))
    cond = mm(pick.astype(F32).astype(BF16), table[...])
    sc = (cond * (1.0 / (1.0 + jnp.exp(-cond)))).astype(BF16)
    silu[...] = sc.astype(F32)
    for b in range(6):
        mods[b] = mm(sc, wts[b])[:8]
    for j in range(3):
        wqkv[j] = wts[6 + j]

    def mod(b, l):
        return mods[b, l : l + 1, :]

    for l in range(lat):
        rs = slice(l * SEQ, (l + 1) * SEQ)
        xhat, _ = layer_norm(tok[rs, :].astype(F32))
        amix_in[rs, :] = (xhat * (1.0 + mod(1, l)) + mod(0, l)).astype(BF16)
    ai = amix_in[...]
    for j in range(3):
        qkv[j] = mm(ai, wts[6 + j]).astype(BF16)

    low = lax.broadcasted_iota(jnp.int32, (SEQ, 128), 1) < HD
    zero = jnp.zeros((SEQ, 128), BF16)

    def attend(l, carry):
        rs = pl.ds(pl.multiple_of(l * SEQ, SEQ), SEQ)
        for hp in range(HEADS // 2):
            cs = slice(hp * 128, hp * 128 + 128)
            q, k, v = qkv[0, rs, cs], qkv[1, rs, cs], qkv[2, rs, cs]
            outs = []
            for h in range(2):
                qm = jnp.where(low if h == 0 else jnp.logical_not(low), q, zero)
                s = mm(qm, k, 1, 1) * HD ** (-0.5)
                top = jnp.max(s, axis=-1, keepdims=True)
                e = jnp.exp(s - top)
                pr = e * (1.0 / jnp.sum(e, axis=-1, keepdims=True))
                probs[l * HEADS + hp * 2 + h] = pr
                outs.append(mm(pr.astype(BF16), v))
            amix[rs, cs] = jnp.where(low, outs[0], outs[1]).astype(BF16)
        return carry

    lax.fori_loop(0, lat, attend, 0)

    ao = mm(amix[...], wts[9])
    ao_s[...] = ao
    for l in range(lat):
        rs = slice(l * SEQ, (l + 1) * SEQ)
        aa = tok[rs, :].astype(F32) + mod(2, l) * ao_s[rs, :]
        aa_s[rs, :] = aa
        xhat, _ = layer_norm(aa)
        minp[rs, :] = (xhat * (1.0 + mod(4, l)) + mod(3, l)).astype(BF16)
        gmx[rs, :] = (cot[rs, :].astype(F32) * mod(5, l)).astype(BF16)
    gmi[...] = jnp.zeros_like(gmi)
    mo[...] = jnp.zeros_like(mo)

    me, core = s_ref[0], s_ref[1]

    def put(value, members, j):
        mine, other = by_core(value, core)
        for i, member in enumerate(members):
            rs = pl.ds(pl.multiple_of(j * 96, 96), 96)
            keep1[member ^ me, rs, :] = mine[96 * i : 96 * i + 96]
            send1[member ^ me, rs, :] = other[96 * i : 96 * i + 96].astype(BF16)

    def mlp(jj, carry):
        j = 2 * jj
        wu = jnp.concatenate([wts[10 + j], wts[11 + j]], axis=1)
        wd = jnp.concatenate([wts[14 + j], wts[15 + j]], axis=0)
        u = mm(minp[...], wu)
        c = math.sqrt(2.0 / math.pi)
        u2 = u * u
        t = jnp.tanh(c * (u + 0.044715 * (u2 * u)))
        half = 0.5 * (1.0 + t)
        act = (u * half).astype(BF16)
        slope = half + 0.5 * u * (1.0 - t * t) * (c * (1.0 + 3.0 * 0.044715 * u2))
        mo[...] += mm(act, wd)
        gmo = gmx[...]
        gp = (mm(gmo, wd, 1, 1) * slope).astype(BF16)
        gd = mm(act, gmo, 0, 0)
        gu = mm(minp[...], gp, 0, 0)
        for i in range(2):
            put(gd[i * D : (i + 1) * D], (3, 1), j + i)
            put(gu[:, i * D : (i + 1) * D], (2, 0), j + i)
        gmi[...] += mm(gp, wu, 1, 1)
        return carry

    lax.fori_loop(0, FF // D // 2, mlp, 0)

    gmod[...] = jnp.zeros_like(gmod)
    for l in range(lat):
        rs = slice(l * SEQ, (l + 1) * SEQ)
        up = cot[rs, :].astype(F32)
        blend[rs, :] = (aa_s[rs, :] + mod(5, l) * mo[rs, :]).astype(BF16)
        gmod[5, l : l + 1, :] = jnp.sum(up * mo[rs, :], axis=0, keepdims=True)
        xhat, rstd = layer_norm(aa_s[rs, :])
        g = gmi[rs, :]
        gmod[3, l : l + 1, :] = jnp.sum(g, axis=0, keepdims=True)
        gmod[4, l : l + 1, :] = jnp.sum(g * xhat, axis=0, keepdims=True)
        ga = up + layer_norm_grad(xhat, rstd, g * (1.0 + mod(4, l)))
        gafter[rs, :] = ga
        gmod[2, l : l + 1, :] = jnp.sum(ga * ao_s[rs, :], axis=0, keepdims=True)
        minp[rs, :] = (ga * mod(2, l)).astype(BF16)
    gao = minp[...]
    gout[...] = mm(amix[...], gao, 0, 0)
    gmx[...] = mm(gao, wts[9], 1, 1).astype(BF16)


def main_call(sidx, table, tokens, cotangent, bufs, fast):
    rows = tokens.shape[0]
    lat = rows // SEQ
    sd = jax.ShapeDtypeStruct
    outs = (
        sd((rows, D), BF16),
        sd((3, rows, D), BF16),
        sd((lat * HEADS, SEQ, SEQ), F32),
        sd((rows, D), BF16),
        sd((rows, D), F32),
        sd((rows, D), BF16),
        sd((6, 8, D), F32),
        sd((6, 8, D), F32),
        sd((16, D), F32),
        sd((3, D, D), BF16),
        sd((D, D), F32),
        sd((4, D, D), F32),
        sd((4, D, D), BF16),
    )
    return pl.pallas_call(
        functools.partial(main_kernel, len(bufs), fast, rows),
        out_shape=outs,
        in_specs=[sspec(), vspec(), hspec(), hspec(), hspec()] + [vspec()] * (len(bufs) - 1),
        out_specs=(vspec(),) * len(outs),
        scratch_shapes=[
            pltpu.VMEM((NBLOCKS, D, D), BF16),
            pltpu.VMEM((rows, D), F32),
            pltpu.VMEM((rows, D), F32),
            pltpu.VMEM((rows, D), BF16),
            pltpu.VMEM((rows, D), BF16),
            pltpu.VMEM((rows, D), F32),
            pltpu.VMEM((rows, D), F32),
            pltpu.VMEM((rows, D), BF16),
            pltpu.VMEM((rows, D), BF16),
            pltpu.VMEM(bufs[0].shape if fast else (16, D), BF16),
            pltpu.SemaphoreType.DMA((3,)),
        ],
        compiler_params=params_of(30),
        cost_estimate=pl.CostEstimate(flops=20_000_000_000, bytes_accessed=30_000_000, transcendentals=0),
        name="main",
    )(sidx, table, *(in_hbm(x) for x in (tokens, cotangent, bufs[0])), *bufs[1:])


def heads_kernel(rows, qkv, probs, gmx, gqkv):
    lat = rows // SEQ
    low = lax.broadcasted_iota(jnp.int32, (SEQ, 128), 1) < HD
    zero = jnp.zeros((SEQ, 128), BF16)

    def back(l, carry):
        rs = pl.ds(pl.multiple_of(l * SEQ, SEQ), SEQ)
        for hp in range(HEADS // 2):
            cs = slice(hp * 128, hp * 128 + 128)
            q, k, v = qkv[0, rs, cs], qkv[1, rs, cs], qkv[2, rs, cs]
            g = gmx[rs, cs]
            res = []
            for h in range(2):
                p = probs[l * HEADS + hp * 2 + h]
                gm = jnp.where(low if h == 0 else jnp.logical_not(low), g, zero)
                gv = mm(p.astype(BF16), g, 0, 0)
                gpr = mm(gm, v, 1, 1)
                dots = jnp.sum(p * gpr, axis=-1, keepdims=True)
                gs = (p * (gpr - dots) * HD ** (-0.5)).astype(BF16)
                res.append((mm(gs, k), mm(gs, q, 0, 0), gv))
            for j in range(3):
                gqkv[j, rs, cs] = jnp.where(low, res[0][j], res[1][j]).astype(BF16)
        return carry

    lax.fori_loop(0, lat, back, 0)


def heads_call(qkv, probs, gmx):
    rows = gmx.shape[0]
    return pl.pallas_call(
        functools.partial(heads_kernel, rows),
        out_shape=jax.ShapeDtypeStruct((3, rows, D), BF16),
        in_specs=[vspec()] * 3,
        out_specs=vspec(),
        compiler_params=params_of(4),
        cost_estimate=pl.CostEstimate(flops=6_000_000_000, bytes_accessed=6_000_000, transcendentals=0),
        name="heads",
    )(qkv, probs, gmx)


def input_kernel(rows, s_ref, tok, gqkv, ai, gafter, mods, gmod1, silu, wqkv, gout, gtok, keep2, send2, keep, srow):
    me, core = s_ref[0], s_ref[1]
    lat = rows // SEQ
    gai = None
    for j in range(4):
        if j < 3:
            part = mm(gqkv[j], wqkv[j], 1, 1)
            gai = part if gai is None else gai + part
            value = mm(ai[...], gqkv[j], 0, 0)
        else:
            value = gout[...]
        mine, other = by_core(value, core)
        for m in range(4):
            rs = slice(48 * j, 48 * j + 48)
            keep2[m ^ me, rs, :] = mine[48 * m : 48 * m + 48]
            send2[m ^ me, rs, :] = other[48 * m : 48 * m + 48].astype(BF16)
    srow[...] = jnp.zeros_like(srow)
    for l in range(lat):
        rs = slice(l * SEQ, (l + 1) * SEQ)
        xhat, rstd = layer_norm(tok[rs, :].astype(F32))
        g = gai[rs, :]
        srow[l : l + 1, :] = jnp.sum(g, axis=0, keepdims=True)
        srow[lat + l : lat + l + 1, :] = jnp.sum(g * xhat, axis=0, keepdims=True)
        gtok[rs, :] = gafter[rs, :] + layer_norm_grad(xhat, rstd, g * (1.0 + mods[1, l : l + 1, :]))
        for b in range(2, 6):
            srow[lat * b + l : lat * b + l + 1, :] = gmod1[b, l : l + 1, :]
        srow[lat * 6 + l : lat * 6 + l + 1, :] = silu[l : l + 1, :]
    keep[...] = srow[...].astype(BF16)


def input_call(sidx, tokens, gqkv, ai, gafter, mods, gmod1, silu, wqkv, gout):
    rows = tokens.shape[0]
    sd = jax.ShapeDtypeStruct
    outs = (sd((rows, D), F32), sd((4, D // 2, D), F32), sd((4, D // 2, D), BF16), sd((KEPT_ROWS, D), BF16))
    return pl.pallas_call(
        functools.partial(input_kernel, rows),
        out_shape=outs,
        in_specs=[sspec()] + [vspec()] * 9,
        out_specs=(vspec(),) * 4,
        scratch_shapes=[pltpu.VMEM((KEPT_ROWS, D), F32)],
        compiler_params=params_of(6),
        cost_estimate=pl.CostEstimate(flops=6_000_000_000, bytes_accessed=6_000_000, transcendentals=0),
        name="input",
    )(sidx, tokens, gqkv, ai, gafter, mods, gmod1, silu, wqkv, gout)


def split(x):
    hi = x.astype(BF16)
    return hi, (x - hi.astype(F32)).astype(BF16)


POLY = (COEFF_C, COEFF_B, COEFF_A)
PLAIN = (1.0, 0.0, 0.0)
STEPS = (
    (0, 0, 2, 1, POLY),
    (2, 0, 3, 2, PLAIN),
    (3, 2, 0, 2, PLAIN),
    (0, 0, 1, 1, POLY),
    (1, 2, 2, 3, PLAIN),
    (1, 0, 3, 2, PLAIN),
    (3, 1, 0, 2, PLAIN),
    (0, 0, 1, 3, POLY),
    (1, 2, 2, 3, PLAIN),
)


def step_tables():
    ints = jnp.array([x for st in STEPS for x in st[:4]], jnp.int32)
    coeffs = jnp.array([x for st in STEPS for x in st[4]], F32)
    return ints, coeffs


HALF = 256


def symmetric(lhs, rhs):
    left = mm(lhs, rhs[:, :HALF])
    corner = mm(lhs[HALF:], rhs[:, HALF:])
    return jnp.concatenate([left, jnp.concatenate([left[HALF:].T, corner], axis=0)], axis=1)


def either(flipped, tall, wide):
    if flipped is None:
        wide()
    else:
        pl.when(flipped)(tall)
        pl.when(jnp.logical_not(flipped))(wide)


def newton_schulz(ints, coeffs, mat_ref, upd_ref, bufs, npairs, flipped, factor):
    bufs[0] = jnp.zeros((D, D), F32)

    def gram(b, carry):
        x0, x1 = mat_ref[2 * b].astype(BF16), mat_ref[2 * b + 1].astype(BF16)

        def tall():
            x = jnp.concatenate([x0, x1], axis=0)
            bufs[0, :, :HALF] += mm(x, x[:, :HALF], 0, 0)
            bufs[0, HALF:, HALF:] += mm(x[:, HALF:], x[:, HALF:], 0, 0)

        def wide():
            x = jnp.concatenate([x0, x1], axis=1)
            bufs[0, :, :HALF] += mm(x, x[:HALF], 1, 1)
            bufs[0, HALF:, HALF:] += mm(x[HALF:], x[HALF:], 1, 1)

        either(flipped, tall, wide)

        return carry

    lax.fori_loop(0, npairs, gram, 0)
    bufs[0, :HALF, HALF:] = bufs[0, HALF:, :HALF].T
    g = bufs[0]
    ri = lax.broadcasted_iota(jnp.int32, (D, D), 0)
    ci = lax.broadcasted_iota(jnp.int32, (D, D), 1)
    eye = jnp.where(ri == ci, 1.0, 0.0)
    diag = jnp.sum(g * eye, axis=1, keepdims=True)
    total = jnp.sum(diag, axis=0, keepdims=True)
    inv = 1.0 / (jnp.sqrt(total) + 1e-07)
    bufs[0] = g * (inv * inv)

    def step(k, carry):
        i, j, d, passes = (ints[4 * k + n] for n in range(4))

        def product(count):
            x = bufs[i]
            xh, xl = split(x)
            yh, yl = split(bufs[j])
            lhs = (xh, xl, xh)[:count]
            rhs = (yh, yh, yl)[:count]
            prod = symmetric(jnp.concatenate(lhs, axis=1), jnp.concatenate(rhs, axis=0))
            r0 = lax.broadcasted_iota(jnp.int32, (D, D), 0)
            r1 = lax.broadcasted_iota(jnp.int32, (D, D), 1)
            ident = jnp.where(r0 == r1, coeffs[3 * k + 2], 0.0)
            bufs[d] = coeffs[3 * k] * prod + (coeffs[3 * k + 1] * x + ident)

        for count in (1, 2, 3):
            pl.when(passes == count)(functools.partial(product, count))
        return carry

    lax.fori_loop(0, len(STEPS), step, 0)
    bufs[0] = bufs[2] * (inv * factor)

    def apply(b, carry):
        wh, wl = split(bufs[0])
        xs = [mat_ref[2 * b + i] for i in range(2)]

        def tall():
            for i in range(2):
                x = xs[i].astype(BF16)
                upd_ref[2 * b + i] = mm(
                    jnp.concatenate([x, x], axis=1), jnp.concatenate([wh, wl], axis=0)
                )

        def wide():
            x = jnp.concatenate([xs[0].astype(BF16), xs[1].astype(BF16)], axis=1)
            out = mm(jnp.concatenate([wh, wl], axis=1), jnp.concatenate([x, x], axis=0))
            upd_ref[2 * b] = out[:, :D]
            upd_ref[2 * b + 1] = out[:, D:]

        either(flipped, tall, wide)
        return carry

    lax.fori_loop(0, npairs, apply, 0)


def take_first(s_ref, chunks, dst):
    me, core, zed = s_ref[0], s_ref[1], s_ref[2]
    for c, ref in enumerate(chunks):
        for y in range(2):
            part = ((me // 2) ^ 1) ^ y
            rs = pl.ds(pl.multiple_of((core ^ c) * 192 + part * 96, 96), 96)
            for z in range(4):
                dst[zed ^ z, rs, :] = ref[y, z].astype(F32)


def take_second(s_ref, chunks, dst):
    me, core, zed = s_ref[0], s_ref[1], s_ref[2]
    for c, ref in enumerate(chunks):
        for m in range(4):
            rs = pl.ds(pl.multiple_of((core ^ c) * 192 + (me ^ m) * 48, 48), 48)
            for z in range(4):
                dst[zed ^ z, rs, :] = ref[m, z].astype(F32)


def adaln_grads(kept, grd, kf):
    ndev = 2 * kept[0].shape[0] // KEPT_ROWS
    for i, ref in enumerate(kept):
        n = ref.shape[0]
        for j in range(3):
            kf[j, i * n : (i + 1) * n, :] = ref[:, 128 * j : 128 * j + 128].astype(F32)

    def rows(first):
        part = [kf[j, pl.ds(first, ndev, stride=KEPT_ROWS), :] for j in range(3)]
        return jnp.concatenate(part, axis=1).astype(BF16)

    sil = jnp.concatenate([rows(12), rows(13)], axis=0)
    for b in range(6):
        gm = jnp.concatenate([rows(2 * b), rows(2 * b + 1)], axis=0)
        grd[b] = mm(sil, gm, 0, 0)


def add_momentum(t, target, mom, grd, mat, base=0):
    first = MATS[target][2]
    for _, block, r0, n, _, frow, stride in [p for p in shard_pieces(t, 4) if p[0] == target]:
        b = block - first
        for j in range(3):
            cs = slice(128 * j, 128 * j + 128)
            m = mom[pl.ds(frow + j, n, stride=stride), :]
            mat[b, r0 : r0 + n, cs] = MOMENTUM_RATE * m + grd[base + b, r0 : r0 + n, cs]


def add_foreign(s_ref, t, target, foreign, grd, mat):
    core = s_ref[1]
    half = foreign[0].shape[0]
    for _, block, r0, n, crow, _, _ in [p for p in shard_pieces(t ^ 1, 4) if p[0] == target]:
        b = block - MATS[target][2]
        cuts = sorted({crow, crow + n} | {c for c in (half,) if crow < c < crow + n})
        for lo, hi in zip(cuts[:-1], cuts[1:]):
            h = lo // half
            for mine, src in enumerate(foreign):

                @pl.when(core == (h ^ mine))
                def _(b=b, r0=r0, lo=lo, hi=hi, h=h, crow=crow, src=src):
                    dst = slice(r0 + lo - crow, r0 + hi - crow)
                    m = src[lo - h * half : hi - h * half, :].astype(F32)
                    mat[b, dst, :] = MOMENTUM_RATE * m + grd[b, dst, :]


TAIL = 48


def ns_a_kernel(s_ref, ints, coeffs, mom, fx0, fx1, kz0, kz1, ch0, ch1, upd, grd, tail, mat, bufs, kf):
    me = s_ref[0]

    @pl.when(me < 2)
    def _():
        adaln_grads((kz0, kz1), grd, kf)

    @pl.when(me >= 2)
    def _():
        take_first(s_ref, (ch0, ch1), grd)

    for t, target in enumerate((ADALN, ADALN, UP, DOWN)):

        @pl.when(me == t)
        def _(t=t, target=target):
            add_momentum(t, target, mom, grd, mat)
            if target != DOWN:
                add_foreign(s_ref, t, target, (fx0, fx1), grd, mat)

    npairs = jnp.where(me < 2, 3, 2)
    factor = jnp.where(me < 2, update_scale(ADALN), update_scale(UP))
    newton_schulz(ints, coeffs, mat, upd, bufs, npairs, me == 3, factor)

    for b in range(4):
        rs = slice(TAIL * b, TAIL * b + TAIL)
        tail[0, rs, :] = grd[b, D - TAIL :, :].astype(BF16)
        tail[1, rs, :] = upd[b, D - TAIL :, :].astype(BF16)


def ns_a(sidx, tables, mom, foreign, kept, chunks):
    sd = jax.ShapeDtypeStruct((6, D, D), F32)
    return pl.pallas_call(
        ns_a_kernel,
        out_shape=(sd, sd, jax.ShapeDtypeStruct((2, 4 * TAIL, D), BF16)),
        in_specs=[sspec()] * 3 + [vspec()] * 7,
        out_specs=(vspec(),) * 3,
        scratch_shapes=[
            pltpu.VMEM((6, D, D), F32),
            pltpu.VMEM((4, D, D), F32),
            pltpu.VMEM((3, 2 * kept[0].shape[0], 128), F32),
        ],
        compiler_params=params_of(14),
        cost_estimate=pl.CostEstimate(flops=8_000_000_000, bytes_accessed=12_000_000, transcendentals=0),
        name="ns_a",
    )(sidx, *tables, mom, *foreign, *kept, *chunks)


def final_kernel(
    s_ref, ints, coeffs, par, mom, ch0, ch1, upa, grda, tail, ograd, onew, omom,
    upb, gb, mat, bufs, og, on, om, sems
):
    me = s_ref[0]
    inner = jnp.logical_or(me == 1, me == 2)

    @pl.when(inner)
    def _():
        take_second(s_ref, (ch0, ch1), gb)
        for b in range(1, 4):
            mat[b] = jnp.zeros((D, D), F32)

    @pl.when(me == 1)
    def _():
        add_momentum(1, QKV, mom, gb, mat)

    @pl.when(me == 2)
    def _():
        add_momentum(2, OUTW, mom, gb, mat, 3)

    def each(t, body):
        for mat_id, block, r0, n, _, frow, stride in shard_pieces(t, 4):
            b = block - MATS[mat_id][2]
            for j in range(3):
                cs = slice(128 * j, 128 * j + 128)
                fl = pl.ds(frow + j, n, stride=stride)
                if mat_id == UP and t == 3:
                    assert r0 == D - TAIL and n == TAIL
                    ts = slice(TAIL * b, TAIL * b + TAIL)
                    body(fl, lambda: tail[0, ts, cs].astype(F32), lambda: tail[1, ts, cs].astype(F32))
                    continue
                rs = slice(r0, r0 + n)
                if mat_id in (QKV, OUTW):
                    gb_at = b + 3 * (mat_id == OUTW)
                    body(fl, lambda: gb[gb_at, rs, cs], lambda: upb[b, rs, cs])
                else:
                    body(fl, lambda: grda[b, rs, cs], lambda: upa[b, rs, cs])

    def gradient(fl, g, u):
        value = g()
        og[fl, :] = value
        om[fl, :] = MOMENTUM_RATE * mom[fl, :] + value

    def update(fl, g, u):
        on[fl, :] = par[fl, :] - u()

    for t in range(4):
        pl.when(me == t)(functools.partial(each, t, gradient))
    early = [pltpu.make_async_copy(og, ograd, sems.at[0]), pltpu.make_async_copy(om, omom, sems.at[1])]
    for copy in early:
        copy.start()

    @pl.when(inner)
    def _():
        npairs = jnp.where(me == 1, 2, 1)
        factor = jnp.where(me == 1, update_scale(QKV), update_scale(OUTW))
        newton_schulz(ints, coeffs, mat, upb, bufs, npairs, None, factor)

    for t in range(4):
        pl.when(me == t)(functools.partial(each, t, update))
    late = pltpu.make_async_copy(on, onew, sems.at[2])
    late.start()
    for copy in early + [late]:
        copy.wait()


def final_call(sidx, tables, par, mom, chunks, upa, grda, tail):
    sd = jax.ShapeDtypeStruct(par.shape, F32)
    block4 = pltpu.VMEM((4, D, D), F32)
    return pl.pallas_call(
        final_kernel,
        out_shape=(sd, sd, sd),
        in_specs=[sspec()] * 3 + [vspec()] * 7,
        out_specs=(hspec(),) * 3,
        scratch_shapes=[block4] * 4 + [pltpu.VMEM(par.shape, F32)] * 3 + [pltpu.SemaphoreType.DMA((3,))],
        compiler_params=params_of(22),
        cost_estimate=pl.CostEstimate(flops=8_000_000_000, bytes_accessed=24_000_000, transcendentals=0),
        name="finish",
    )(sidx, *tables, par, mom, *chunks, upa, grda, tail)


def swap(x, axis, mask):
    count = lax.axis_size(axis)
    return lax.ppermute(x, axis, [(i, i ^ mask) for i in range(count)])


def more_rows(x, hops):
    for axis, mask in hops:
        x = jnp.concatenate([x, swap(x, axis, mask)], axis=0)
    return x


def wide_sum(parts):
    total = None
    for p in parts:
        total = p.astype(F32) if total is None else total + p.astype(F32)
    return total


def join_kernel(own, other, keep, *msgs):
    n = own.shape[1]
    for m, msg in enumerate(msgs, 1):
        msg[:n, :] = (own[m] + other[m].astype(F32)).astype(BF16)
        msg[n:, :] = keep[...]


def join_call(own, other, keep):
    out = jax.ShapeDtypeStruct((own.shape[1] + keep.shape[0], D), BF16)
    return pl.pallas_call(
        join_kernel,
        out_shape=(out,) * 3,
        in_specs=[vspec()] * 3,
        out_specs=(vspec(),) * 3,
        compiler_params=params_of(4),
        cost_estimate=pl.CostEstimate(flops=0, bytes_accessed=2_000_000, transcendentals=0),
        name="join",
    )(own, other, keep)


def piece_kernel(has_keep, s_ref, own, other, *refs):
    keep = refs[0] if has_keep else None
    got = refs[has_keep : has_keep + 3]
    outs = refs[has_keep + 3 :]
    zed = s_ref[2]
    n = outs[0].shape[0]
    size = 4 * n
    if has_keep:
        rows = outs[4]
        kr = keep.shape[0]
        rows[:kr, :] = keep[...]
        for m in range(3):
            rows[kr * (m + 1) : kr * (m + 2), :] = got[m][size:, :]
    for i in range(4):
        rs = pl.ds(pl.multiple_of((zed ^ i) * n, n), n)
        total = own[0, rs, :] + other[0, rs, :].astype(F32)
        for g in got:
            total = total + g[rs, :].astype(F32)
        if i == 0:
            outs[0][...] = total
        else:
            outs[i][:n, :] = total.astype(BF16)
            if has_keep:
                outs[i][n:, :] = rows[...]


def piece_call(sidx, own, other, got, keep=None):
    size = own.shape[1]
    n = size // 4
    extra = 0 if keep is None else 4 * keep.shape[0]
    sd = jax.ShapeDtypeStruct
    outs = (sd((n, D), F32),) + (sd((n + extra, D), BF16),) * 3
    if extra:
        outs += (sd((extra, D), BF16),)
    kept = [] if keep is None else [keep]
    return pl.pallas_call(
        functools.partial(piece_kernel, len(kept)),
        out_shape=outs,
        in_specs=[sspec()] + [vspec()] * (len(kept) + 5),
        out_specs=(vspec(),) * len(outs),
        compiler_params=params_of(6),
        cost_estimate=pl.CostEstimate(flops=0, bytes_accessed=2_000_000, transcendentals=0),
        name="piece",
    )(sidx, own, other, *kept, *got)


def z_sum(mine, pieces):
    n = mine.shape[0]
    got = []
    for m, piece in enumerate(pieces, 1):
        got.append(swap(piece, "rep", 2 * m))
    return wide_sum([mine] + [g[:n] for g in got]).astype(BF16), [g[n:] for g in got]


def fan(x, axis, masks):
    got = [x]
    for m in masks:
        got.append(swap(x, axis, m))
    return jnp.stack(got)


def fast_device(tokens, conditions, assignment, params, momentum, cotangent):
    return fast_body(tokens, conditions, assignment, params, momentum, cotangent)


def fast_body(tokens, conditions, assignment, params, momentum, cotangent):
    me = lax.axis_index("fsdp")
    rep = lax.axis_index("rep")
    core, zed = rep % 2, rep // 2
    lat = tokens.shape[0]
    rows = lat * SEQ
    par = params.reshape(-1, 128)
    mom = momentum.reshape(-1, 128)
    source = assignment // lat
    apart = ((source // 8) ^ me) + 4 * ((source % 8) ^ rep)
    pick = apart * lat + assignment % lat
    sidx = jnp.concatenate([jnp.stack([me, core, zed]), pick]).astype(jnp.int32)

    hop = swap(conditions, "fsdp", 1)
    top, bottom = prep(sidx, par, 4, 2)
    table = jnp.concatenate([conditions, hop], axis=0)
    table, top, bottom = lax.optimization_barrier((table, top, bottom))
    hop = swap(table, "fsdp", 2)
    x0 = swap(top, "fsdp", 1)
    y1 = swap(bottom, "fsdp", 2)
    x1 = swap(bottom, "fsdp", 1)
    y0 = swap(top, "fsdp", 2)
    table = jnp.concatenate([table, hop], axis=0)
    table = more_rows(table, (("rep", 1),))
    table = more_rows(table, (("rep", 2), ("rep", 4)))
    x0, y1, table = lax.optimization_barrier((x0, y1, table))
    d0 = swap(x0, "fsdp", 2)
    d1 = swap(y1, "fsdp", 1)
    received = (x0, x1, y0, y1, d0, d1)
    (wc,) = prep(sidx, par, 4, 0)
    bufs = (wc,) + received + tuple(swap(r, "rep", 1) for r in received)
    (mh,) = prep(sidx, mom, 4, 1)
    fx0 = swap(mh, "fsdp", 1)

    tok2, cot2 = tokens.reshape(rows, D), cotangent.reshape(rows, D)
    (blend, qkv, probs, ai, gafter, gmx, mods, gmod1, silu, wqkv, gout, keep1, send1) = main_call(
        sidx, table, tok2, cot2, bufs, True
    )
    fx1 = swap(fx0, "rep", 1)

    other = swap(send1, "rep", 1)
    gqkv = heads_call(qkv, probs, gmx)
    got = []
    for m in (1, 2, 3):
        got.append(swap((keep1[m] + other[m].astype(F32)).astype(BF16), "fsdp", m))
    gtok, keep2, send2, keep = input_call(sidx, tok2, gqkv, ai, gafter, mods, gmod1, silu, wqkv, gout)
    mine, *pieces = piece_call(sidx, keep1, other, got)
    total, _ = z_sum(mine, pieces)
    col = fan(total, "rep", (2, 4, 6))
    pair = fan(col, "fsdp", (2,))
    pairs = (pair, swap(pair, "rep", 1))

    other = swap(send2, "rep", 1)
    msgs = join_call(keep2, other, keep)
    got = []
    for m in (1, 2, 3):
        got.append(swap(msgs[m - 1], "fsdp", m))
    mine, *pieces, rows2 = piece_call(sidx, keep2, other, got, keep)
    q2, more = z_sum(mine, pieces)
    kz = jnp.concatenate([rows2] + more, axis=0)
    kept = (kz, swap(kz, "rep", 1))
    quad = fan(fan(q2, "rep", (2, 4, 6)), "fsdp", (1, 2, 3))
    quads = (quad, swap(quad, "rep", 1))

    tables = step_tables()
    upa, grda, tail = ns_a(sidx, tables, mom, (fx0, fx1), kept, pairs)
    tail = lax.ppermute(tail, "fsdp", [(2, 3)])
    ograd, onew, omom = final_call(sidx, tables, par, mom, quads, upa, grda, tail)
    shape = tokens.shape
    return (
        blend.reshape(shape),
        gtok.reshape(shape),
        ograd.reshape(-1),
        onew.reshape(-1),
        omom.reshape(-1),
    )


def unpack(flat):
    pieces, offset = [], 0
    for rows_count, cols_count, _, _ in MATS:
        pieces.append(flat[offset : offset + rows_count * cols_count].reshape(rows_count, cols_count))
        offset += rows_count * cols_count
    return pieces


def to_blocks(mats):
    out = []
    for matrix, (rows_count, cols_count, _, by_cols) in zip(mats, MATS):
        if by_cols:
            out.append(matrix.reshape(D, cols_count // D, D).transpose(1, 0, 2))
        else:
            out.append(matrix.reshape(rows_count // D, D, D))
    return jnp.concatenate(out, axis=0)


def from_blocks(blocks, by_cols):
    if by_cols:
        return blocks.transpose(1, 0, 2).reshape(-1)
    return blocks.reshape(-1)


def orthogonalize(matrix):
    flipped = matrix.shape[0] > matrix.shape[1]
    current = matrix.T if flipped else matrix
    current = current / (jnp.sqrt(jnp.sum(current * current)) + 1e-07)
    for _ in range(NS_ITERS):
        square = jnp.dot(current, current.T, precision=lax.Precision.HIGHEST)
        polynomial = COEFF_B * square + COEFF_C * jnp.dot(square, square, precision=lax.Precision.HIGHEST)
        current = COEFF_A * current + jnp.dot(polynomial, current, precision=lax.Precision.HIGHEST)
    return current.T if flipped else current


def scaled_update(matrix, factor):
    return (factor * orthogonalize(matrix)).reshape(-1)


def empty_update(matrix, factor):
    return jnp.zeros((matrix.shape[0] * matrix.shape[1],), F32)


def any_device(tokens, conditions, assignment, params, momentum, cotangent):
    lat = tokens.shape[0]
    rows = lat * SEQ
    table = lax.all_gather(conditions, ("fsdp", "rep"), axis=0, tiled=True)
    gathered = lax.all_gather(params.astype(BF16), "fsdp", axis=0, tiled=True)
    blocks = to_blocks(unpack(gathered))
    me = lax.axis_index("fsdp")
    sidx = jnp.concatenate([jnp.zeros((3,), jnp.int32), assignment.astype(jnp.int32)])
    tok2, cot2 = tokens.reshape(rows, D), cotangent.reshape(rows, D)
    (blend, qkv, probs, ai, gafter, gmx, mods, gmod1, silu, wqkv, gout, keep1, send1) = main_call(
        sidx, table, tok2, cot2, (blocks,), False
    )
    gqkv = heads_call(qkv, probs, gmx)
    gtok, keep2, send2, keep = input_call(sidx, tok2, gqkv, ai, gafter, mods, gmod1, silu, wqkv, gout)
    halves1 = jnp.stack([keep1, send1.astype(F32)]).reshape(2, 4, 4, 96, D)
    up = halves1[:, jnp.array([2, 0])].transpose(2, 0, 1, 3, 4).reshape(4, D, D)
    down = halves1[:, jnp.array([3, 1])].transpose(2, 0, 1, 3, 4).reshape(4, D, D)
    halves2 = jnp.stack([keep2, send2.astype(F32)]).reshape(2, 4, 4, 48, D)
    last = halves2.transpose(2, 0, 1, 3, 4).reshape(4, D, D)
    rest = jnp.concatenate(
        [from_blocks(last[:3], True), last[3].reshape(-1), from_blocks(up, True), down.reshape(-1)]
    )
    kept = lax.all_gather(keep, ("fsdp", "rep"), axis=0, tiled=True).reshape(-1, KEPT_ROWS, D)
    silu_all = kept[:, 6 * lat : 7 * lat].reshape(-1, D)
    mod_all = kept[:, : 6 * lat].reshape(-1, 6, lat, D).transpose(0, 2, 1, 3).reshape(-1, 6 * D)
    adaln = lax.dot_general(silu_all, mod_all, (((0,), (0,)), ((), ())), preferred_element_type=F32)
    shard_len = params.shape[0]
    head = jnp.concatenate([adaln.reshape(-1), jnp.zeros_like(rest)])
    flat = jnp.concatenate([jnp.zeros((D * 6 * D,), F32), rest])
    part = lax.psum_scatter(flat, "fsdp", scatter_dimension=0, tiled=True)
    full_grad = lax.psum(part, "rep") + lax.dynamic_slice_in_dim(head, me * shard_len, shard_len, 0)
    new_momentum = MOMENTUM_RATE * momentum + full_grad
    whole_mom = lax.all_gather(new_momentum, "fsdp", axis=0, tiled=True)
    group_size = lax.axis_size("fsdp")
    updates, offset = [], 0
    for mat, piece in enumerate(unpack(whole_mom)):
        factor = F32(update_scale(mat))
        owner = (offset // shard_len + group_size // 2) % group_size
        updates.append(lax.cond(me == owner, scaled_update, empty_update, piece, factor))
        offset += piece.size
    update = lax.psum_scatter(jnp.concatenate(updates), "fsdp", scatter_dimension=0, tiled=True)
    shape = tokens.shape
    return (blend.reshape(shape), gtok.reshape(shape), full_grad, params - update, new_momentum)


def solution(mesh):
    both = ("fsdp", "rep")
    in_specs = (P(both, None, None), P(both, None), P(both), P("fsdp"), P("fsdp"), P(both, None, None))
    out_specs = (P(both, None, None), P(both, None, None), P("fsdp"), P("fsdp"), P("fsdp"))
    small = dict(mesh.shape) == {"fsdp": 4, "rep": 8}
    return jax.shard_map(
        fast_device if small else any_device,
        mesh=mesh,
        in_specs=in_specs,
        out_specs=out_specs,
        check_vma=False,
    )
```

```python
import functools
import math

import jax
import jax.numpy as jnp
from jax import lax
from jax.experimental import pallas as pl
from jax.experimental.pallas import tpu as pltpu
from jax.sharding import PartitionSpec as P


D = 384
HEADS = 6
HD = 64
FF = 1536
SEQ = 256
NS_ITERS = 3

LN_EPSILON = 1e-06
MOMENTUM_RATE = 0.95
LEARN_RATE = 0.2
COEFF_A = 3.4445
COEFF_B = -4.775
COEFF_C = 2.0315


F32 = jnp.float32
BF16 = jnp.bfloat16

MATS = ((D, 6 * D, 0, True), (D, 3 * D, 6, True), (D, D, 9, True), (D, FF, 10, True), (FF, D, 14, False))
NBLOCKS = 18
ADALN, QKV, OUTW, UP, DOWN = range(5)
P_SIZE = sum(m[0] * m[1] for m in MATS)
KEPT_ROWS = 16


def update_scale(mat):
    return LEARN_RATE * 0.2 * math.sqrt(max(MATS[mat][0], MATS[mat][1]))


def shard_pieces(shard, count):
    size = P_SIZE // count
    begin, end = shard * size, (shard + 1) * size
    pieces, crow, offset = [], 0, 0
    for mat, (rows, cols, first, by_cols) in enumerate(MATS):
        lo, hi = max(begin, offset), min(end, offset + rows * cols)
        if lo < hi:
            r0, r1 = (lo - offset) // cols, (hi - offset) // cols
            stride = cols // 128
            base = (offset - begin) // 128
            if by_cols:
                for b in range(cols // D):
                    pieces.append((mat, first + b, r0, r1 - r0, crow, base + r0 * stride + 3 * b, stride))
                    crow += r1 - r0
            else:
                r = r0
                while r < r1:
                    n = min(r1, (r // D + 1) * D) - r
                    pieces.append((mat, first + r // D, r % D, n, crow, base + r * stride, stride))
                    crow += n
                    r += n
        offset += rows * cols
    return pieces


def mm(a, b, ca=1, cb=0):
    return lax.dot_general(a, b, (((ca,), (cb,)), ((), ())), preferred_element_type=F32)


def vspec():
    return pl.BlockSpec(memory_space=pltpu.VMEM)


def hspec():
    return pl.BlockSpec(memory_space=pltpu.HBM)


def in_hbm(x):
    return pltpu.with_memory_space_constraint(x, pltpu.HBM)


def sspec():
    return pl.BlockSpec(memory_space=pltpu.SMEM)


def params_of(mib):
    return pltpu.CompilerParams(vmem_limit_bytes=mib * 1024 * 1024)


def prep_kernel(count, parts, s_ref, p_ref, *refs):
    w_ref = refs[-1]
    for shard in range(count):

        @pl.when(s_ref[0] == shard)
        def _(shard=shard):
            for _, _, _, n, crow, frow, stride in shard_pieces(shard, count):
                for j in range(3):
                    src = pl.ds(frow + j, n, stride=stride)
                    w_ref[crow : crow + n, 128 * j : 128 * j + 128] = p_ref[src, :].astype(BF16)

    for i in range(parts):
        n = refs[i].shape[0]
        row = s_ref[1] * (n * parts) + i * n
        refs[i][...] = w_ref[pl.ds(pl.multiple_of(row, n), n), :]


def prep(sidx, flat, count, parts):
    rows = P_SIZE // count // D
    sd = jax.ShapeDtypeStruct
    outs = (sd((rows // 2 // parts, D), BF16),) * parts if parts else (sd((rows, D), BF16),)
    return pl.pallas_call(
        functools.partial(prep_kernel, count, parts),
        out_shape=outs,
        in_specs=[sspec(), vspec()],
        out_specs=(vspec(),) * len(outs),
        scratch_shapes=[pltpu.VMEM((rows, D), BF16)] if parts else [],
        compiler_params=params_of(4),
        cost_estimate=pl.CostEstimate(flops=0, bytes_accessed=4_000_000, transcendentals=0),
        name="prep",
    )(sidx, flat)


def layer_norm(h):
    center = jnp.mean(h, axis=-1, keepdims=True)
    cent = h - center
    spread = jnp.mean(jnp.square(cent), axis=-1, keepdims=True)
    rstd = lax.rsqrt(spread + LN_EPSILON)
    return cent * rstd, rstd


def layer_norm_grad(xhat, rstd, gx):
    m1 = jnp.mean(gx, axis=-1, keepdims=True)
    m2 = jnp.mean(gx * xhat, axis=-1, keepdims=True)
    return rstd * (gx - m1 - xhat * m2)


def gather_plan(count):
    plan = []
    half = P_SIZE // count // D // 2
    for shard in range(count):
        for _, block, r0, n, crow, _, _ in shard_pieces(shard, count):
            cuts = sorted({crow, crow + n} | {c for c in range(0, 2 * half + 1, half // 2) if crow < c < crow + n})
            for a, b in zip(cuts[:-1], cuts[1:]):
                plan.append((shard, a // half, a % half, b - a, block, r0 + a - crow))
    return plan


def load_weights_fast(s_ref, bufs, wts, own_ready):
    own = bufs[0]
    me, core = s_ref[0], s_ref[1]
    half = own.shape[0] // 2
    quarter = half // 2
    plan = gather_plan(4)

    def move(src, row, n, block, brow):
        size = 96 if n % 96 == 0 else 48

        def chunk(i, carry):
            a = pl.multiple_of(row + i * size, 16)
            b = pl.multiple_of(brow + i * size, 16)
            wts[block, pl.ds(b, size), :] = src[pl.ds(a, size), :]
            return carry

        lax.fori_loop(0, n // size, chunk, 0)

    for shard in range(4):
        for h in range(2):
            pieces = [p for p in plan if p[0] == shard and p[1] == h]
            for m in (1, 2, 3):
                for mine in (True, False):

                    @pl.when(jnp.logical_and(me == (shard ^ m), (core == h) if mine else (core != h)))
                    def _(pieces=pieces, m=m, mine=mine):
                        for _, _, r, n, block, br in pieces:
                            k = r // quarter
                            src = bufs[(1 if mine else 7) + 2 * (m - 1) + k]
                            move(src, r - k * quarter, n, block, br)

    own_ready()
    for shard in range(4):

        @pl.when(me == shard)
        def _(shard=shard):
            for _, h, r, n, block, br in [p for p in plan if p[0] == shard]:
                move(own, h * half + r, n, block, br)


def by_core(value, core):
    half = value.shape[0] // 2
    top, bottom = value[:half], value[half:]
    return jnp.where(core == 0, top, bottom), jnp.where(core == 0, bottom, top)


def main_kernel(nbuf, fast, rows, s_ref, table, tok_hbm, cot_hbm, *refs):
    bufs = refs[:nbuf]
    (blend, qkv, probs, amix_in, gafter, gmx, mods, gmod, silu, wqkv, gout, keep1, send1) = refs[nbuf : nbuf + 13]
    wts, ao_s, aa_s, amix, minp, gmi, mo, tok, cot, own, sems = refs[nbuf + 13 :]
    lat = rows // SEQ
    get_tok = pltpu.make_async_copy(tok_hbm, tok, sems.at[1])
    get_cot = pltpu.make_async_copy(cot_hbm, cot, sems.at[2])
    first = pltpu.make_async_copy(bufs[0], own if fast else wts, sems.at[0])
    first.start()
    get_tok.start()
    get_cot.start()
    if fast:
        load_weights_fast(s_ref, (own,) + bufs[1:], wts, first.wait)
    else:
        first.wait()
    get_tok.wait()
    get_cot.wait()
    nt = table.shape[0]
    lanes = lax.broadcasted_iota(jnp.int32, (16, nt), 1)
    rws = lax.broadcasted_iota(jnp.int32, (16, nt), 0)
    pick = jnp.zeros((16, nt), jnp.bool_)
    for l in range(lat):
        pick = pick | ((rws == l) & (lanes == s_ref[3 + l]))
    cond = mm(pick.astype(F32).astype(BF16), table[...])
    sc = (cond * (1.0 / (1.0 + jnp.exp(-cond)))).astype(BF16)
    silu[...] = sc.astype(F32)
    for b in range(6):
        mods[b] = mm(sc, wts[b])[:8]
    for j in range(3):
        wqkv[j] = wts[6 + j]

    def mod(b, l):
        return mods[b, l : l + 1, :]

    for l in range(lat):
        rs = slice(l * SEQ, (l + 1) * SEQ)
        xhat, _ = layer_norm(tok[rs, :].astype(F32))
        amix_in[rs, :] = (xhat * (1.0 + mod(1, l)) + mod(0, l)).astype(BF16)
    ai = amix_in[...]
    for j in range(3):
        qkv[j] = mm(ai, wts[6 + j]).astype(BF16)

    low = lax.broadcasted_iota(jnp.int32, (SEQ, 128), 1) < HD
    zero = jnp.zeros((SEQ, 128), BF16)

    def attend(l, carry):
        rs = pl.ds(pl.multiple_of(l * SEQ, SEQ), SEQ)
        for hp in range(HEADS // 2):
            cs = slice(hp * 128, hp * 128 + 128)
            q, k, v = qkv[0, rs, cs], qkv[1, rs, cs], qkv[2, rs, cs]
            outs = []
            for h in range(2):
                qm = jnp.where(low if h == 0 else jnp.logical_not(low), q, zero)
                s = mm(qm, k, 1, 1) * HD ** (-0.5)
                top = jnp.max(s, axis=-1, keepdims=True)
                e = jnp.exp(s - top)
                pr = e * (1.0 / jnp.sum(e, axis=-1, keepdims=True))
                probs[l * HEADS + hp * 2 + h] = pr
                outs.append(mm(pr.astype(BF16), v))
            amix[rs, cs] = jnp.where(low, outs[0], outs[1]).astype(BF16)
        return carry

    lax.fori_loop(0, lat, attend, 0)

    ao = mm(amix[...], wts[9])
    ao_s[...] = ao
    for l in range(lat):
        rs = slice(l * SEQ, (l + 1) * SEQ)
        aa = tok[rs, :].astype(F32) + mod(2, l) * ao_s[rs, :]
        aa_s[rs, :] = aa
        xhat, _ = layer_norm(aa)
        minp[rs, :] = (xhat * (1.0 + mod(4, l)) + mod(3, l)).astype(BF16)
        gmx[rs, :] = (cot[rs, :].astype(F32) * mod(5, l)).astype(BF16)
    gmi[...] = jnp.zeros_like(gmi)
    mo[...] = jnp.zeros_like(mo)

    me, core = s_ref[0], s_ref[1]

    def put(value, members, j):
        mine, other = by_core(value, core)
        for i, member in enumerate(members):
            rs = pl.ds(pl.multiple_of(j * 96, 96), 96)
            keep1[member ^ me, rs, :] = mine[96 * i : 96 * i + 96]
            send1[member ^ me, rs, :] = other[96 * i : 96 * i + 96].astype(BF16)

    def mlp(jj, carry):
        j = 2 * jj
        wu = jnp.concatenate([wts[10 + j], wts[11 + j]], axis=1)
        wd = jnp.concatenate([wts[14 + j], wts[15 + j]], axis=0)
        u = mm(minp[...], wu)
        c = math.sqrt(2.0 / math.pi)
        u2 = u * u
        t = jnp.tanh(c * (u + 0.044715 * (u2 * u)))
        half = 0.5 * (1.0 + t)
        act = (u * half).astype(BF16)
        slope = half + 0.5 * u * (1.0 - t * t) * (c * (1.0 + 3.0 * 0.044715 * u2))
        mo[...] += mm(act, wd)
        gmo = gmx[...]
        gp = (mm(gmo, wd, 1, 1) * slope).astype(BF16)
        gd = mm(act, gmo, 0, 0)
        gu = mm(minp[...], gp, 0, 0)
        for i in range(2):
            put(gd[i * D : (i + 1) * D], (3, 1), j + i)
            put(gu[:, i * D : (i + 1) * D], (2, 0), j + i)
        gmi[...] += mm(gp, wu, 1, 1)
        return carry

    lax.fori_loop(0, FF // D // 2, mlp, 0)

    gmod[...] = jnp.zeros_like(gmod)
    for l in range(lat):
        rs = slice(l * SEQ, (l + 1) * SEQ)
        up = cot[rs, :].astype(F32)
        blend[rs, :] = (aa_s[rs, :] + mod(5, l) * mo[rs, :]).astype(BF16)
        gmod[5, l : l + 1, :] = jnp.sum(up * mo[rs, :], axis=0, keepdims=True)
        xhat, rstd = layer_norm(aa_s[rs, :])
        g = gmi[rs, :]
        gmod[3, l : l + 1, :] = jnp.sum(g, axis=0, keepdims=True)
        gmod[4, l : l + 1, :] = jnp.sum(g * xhat, axis=0, keepdims=True)
        ga = up + layer_norm_grad(xhat, rstd, g * (1.0 + mod(4, l)))
        gafter[rs, :] = ga
        gmod[2, l : l + 1, :] = jnp.sum(ga * ao_s[rs, :], axis=0, keepdims=True)
        minp[rs, :] = (ga * mod(2, l)).astype(BF16)
    gao = minp[...]
    gout[...] = mm(amix[...], gao, 0, 0)
    gmx[...] = mm(gao, wts[9], 1, 1).astype(BF16)


def main_call(sidx, table, tokens, cotangent, bufs, fast):
    rows = tokens.shape[0]
    lat = rows // SEQ
    sd = jax.ShapeDtypeStruct
    outs = (
        sd((rows, D), BF16),
        sd((3, rows, D), BF16),
        sd((lat * HEADS, SEQ, SEQ), F32),
        sd((rows, D), BF16),
        sd((rows, D), F32),
        sd((rows, D), BF16),
        sd((6, 8, D), F32),
        sd((6, 8, D), F32),
        sd((16, D), F32),
        sd((3, D, D), BF16),
        sd((D, D), F32),
        sd((4, D, D), F32),
        sd((4, D, D), BF16),
    )
    return pl.pallas_call(
        functools.partial(main_kernel, len(bufs), fast, rows),
        out_shape=outs,
        in_specs=[sspec(), vspec(), hspec(), hspec(), hspec()] + [vspec()] * (len(bufs) - 1),
        out_specs=(vspec(),) * len(outs),
        scratch_shapes=[
            pltpu.VMEM((NBLOCKS, D, D), BF16),
            pltpu.VMEM((rows, D), F32),
            pltpu.VMEM((rows, D), F32),
            pltpu.VMEM((rows, D), BF16),
            pltpu.VMEM((rows, D), BF16),
            pltpu.VMEM((rows, D), F32),
            pltpu.VMEM((rows, D), F32),
            pltpu.VMEM((rows, D), BF16),
            pltpu.VMEM((rows, D), BF16),
            pltpu.VMEM(bufs[0].shape if fast else (16, D), BF16),
            pltpu.SemaphoreType.DMA((3,)),
        ],
        compiler_params=params_of(30),
        cost_estimate=pl.CostEstimate(flops=20_000_000_000, bytes_accessed=30_000_000, transcendentals=0),
        name="main",
    )(sidx, table, *(in_hbm(x) for x in (tokens, cotangent, bufs[0])), *bufs[1:])


def heads_kernel(rows, qkv, probs, gmx, gqkv):
    lat = rows // SEQ
    low = lax.broadcasted_iota(jnp.int32, (SEQ, 128), 1) < HD
    zero = jnp.zeros((SEQ, 128), BF16)

    def back(l, carry):
        rs = pl.ds(pl.multiple_of(l * SEQ, SEQ), SEQ)
        for hp in range(HEADS // 2):
            cs = slice(hp * 128, hp * 128 + 128)
            q, k, v = qkv[0, rs, cs], qkv[1, rs, cs], qkv[2, rs, cs]
            g = gmx[rs, cs]
            res = []
            for h in range(2):
                p = probs[l * HEADS + hp * 2 + h]
                gm = jnp.where(low if h == 0 else jnp.logical_not(low), g, zero)
                gv = mm(p.astype(BF16), g, 0, 0)
                gpr = mm(gm, v, 1, 1)
                dots = jnp.sum(p * gpr, axis=-1, keepdims=True)
                gs = (p * (gpr - dots) * HD ** (-0.5)).astype(BF16)
                res.append((mm(gs, k), mm(gs, q, 0, 0), gv))
            for j in range(3):
                gqkv[j, rs, cs] = jnp.where(low, res[0][j], res[1][j]).astype(BF16)
        return carry

    lax.fori_loop(0, lat, back, 0)


def heads_call(qkv, probs, gmx):
    rows = gmx.shape[0]
    return pl.pallas_call(
        functools.partial(heads_kernel, rows),
        out_shape=jax.ShapeDtypeStruct((3, rows, D), BF16),
        in_specs=[vspec()] * 3,
        out_specs=vspec(),
        compiler_params=params_of(4),
        cost_estimate=pl.CostEstimate(flops=6_000_000_000, bytes_accessed=6_000_000, transcendentals=0),
        name="heads",
    )(qkv, probs, gmx)


def input_kernel(rows, s_ref, tok, gqkv, ai, gafter, mods, gmod1, silu, wqkv, gout, gtok, keep2, send2, keep, srow):
    me, core = s_ref[0], s_ref[1]
    lat = rows // SEQ
    gai = None
    for j in range(4):
        if j < 3:
            part = mm(gqkv[j], wqkv[j], 1, 1)
            gai = part if gai is None else gai + part
            value = mm(ai[...], gqkv[j], 0, 0)
        else:
            value = gout[...]
        mine, other = by_core(value, core)
        for m in range(4):
            rs = slice(48 * j, 48 * j + 48)
            keep2[m ^ me, rs, :] = mine[48 * m : 48 * m + 48]
            send2[m ^ me, rs, :] = other[48 * m : 48 * m + 48].astype(BF16)
    srow[...] = jnp.zeros_like(srow)
    for l in range(lat):
        rs = slice(l * SEQ, (l + 1) * SEQ)
        xhat, rstd = layer_norm(tok[rs, :].astype(F32))
        g = gai[rs, :]
        srow[l : l + 1, :] = jnp.sum(g, axis=0, keepdims=True)
        srow[lat + l : lat + l + 1, :] = jnp.sum(g * xhat, axis=0, keepdims=True)
        gtok[rs, :] = gafter[rs, :] + layer_norm_grad(xhat, rstd, g * (1.0 + mods[1, l : l + 1, :]))
        for b in range(2, 6):
            srow[lat * b + l : lat * b + l + 1, :] = gmod1[b, l : l + 1, :]
        srow[lat * 6 + l : lat * 6 + l + 1, :] = silu[l : l + 1, :]
    keep[...] = srow[...].astype(BF16)


def input_call(sidx, tokens, gqkv, ai, gafter, mods, gmod1, silu, wqkv, gout):
    rows = tokens.shape[0]
    sd = jax.ShapeDtypeStruct
    outs = (sd((rows, D), F32), sd((4, D // 2, D), F32), sd((4, D // 2, D), BF16), sd((KEPT_ROWS, D), BF16))
    return pl.pallas_call(
        functools.partial(input_kernel, rows),
        out_shape=outs,
        in_specs=[sspec()] + [vspec()] * 9,
        out_specs=(vspec(),) * 4,
        scratch_shapes=[pltpu.VMEM((KEPT_ROWS, D), F32)],
        compiler_params=params_of(6),
        cost_estimate=pl.CostEstimate(flops=6_000_000_000, bytes_accessed=6_000_000, transcendentals=0),
        name="input",
    )(sidx, tokens, gqkv, ai, gafter, mods, gmod1, silu, wqkv, gout)


def split(x):
    hi = x.astype(BF16)
    return hi, (x - hi.astype(F32)).astype(BF16)


POLY = (COEFF_C, COEFF_B, COEFF_A)
PLAIN = (1.0, 0.0, 0.0)
STEPS = (
    (0, 0, 2, 1, POLY),
    (2, 0, 3, 2, PLAIN),
    (3, 2, 0, 2, PLAIN),
    (0, 0, 1, 1, POLY),
    (1, 2, 2, 3, PLAIN),
    (1, 0, 3, 2, PLAIN),
    (3, 1, 0, 2, PLAIN),
    (0, 0, 1, 3, POLY),
    (1, 2, 2, 3, PLAIN),
)


def step_tables():
    ints = jnp.array([x for st in STEPS for x in st[:4]], jnp.int32)
    coeffs = jnp.array([x for st in STEPS for x in st[4]], F32)
    return ints, coeffs


HALF = 256


def symmetric(lhs, rhs):
    left = mm(lhs, rhs[:, :HALF])
    corner = mm(lhs[HALF:], rhs[:, HALF:])
    return jnp.concatenate([left, jnp.concatenate([left[HALF:].T, corner], axis=0)], axis=1)


def either(flipped, tall, wide):
    if flipped is None:
        wide()
    else:
        pl.when(flipped)(tall)
        pl.when(jnp.logical_not(flipped))(wide)


def newton_schulz(ints, coeffs, mat_ref, upd_ref, bufs, npairs, flipped, factor):
    bufs[0] = jnp.zeros((D, D), F32)

    def gram(b, carry):
        x0, x1 = mat_ref[2 * b].astype(BF16), mat_ref[2 * b + 1].astype(BF16)

        def tall():
            x = jnp.concatenate([x0, x1], axis=0)
            bufs[0, :, :HALF] += mm(x, x[:, :HALF], 0, 0)
            bufs[0, HALF:, HALF:] += mm(x[:, HALF:], x[:, HALF:], 0, 0)

        def wide():
            x = jnp.concatenate([x0, x1], axis=1)
            bufs[0, :, :HALF] += mm(x, x[:HALF], 1, 1)
            bufs[0, HALF:, HALF:] += mm(x[HALF:], x[HALF:], 1, 1)

        either(flipped, tall, wide)

        return carry

    lax.fori_loop(0, npairs, gram, 0)
    bufs[0, :HALF, HALF:] = bufs[0, HALF:, :HALF].T
    g = bufs[0]
    ri = lax.broadcasted_iota(jnp.int32, (D, D), 0)
    ci = lax.broadcasted_iota(jnp.int32, (D, D), 1)
    eye = jnp.where(ri == ci, 1.0, 0.0)
    diag = jnp.sum(g * eye, axis=1, keepdims=True)
    total = jnp.sum(diag, axis=0, keepdims=True)
    inv = 1.0 / (jnp.sqrt(total) + 1e-07)
    bufs[0] = g * (inv * inv)

    def step(k, carry):
        i, j, d, passes = (ints[4 * k + n] for n in range(4))

        def product(count):
            x = bufs[i]
            xh, xl = split(x)
            yh, yl = split(bufs[j])
            lhs = (xh, xl, xh)[:count]
            rhs = (yh, yh, yl)[:count]
            prod = symmetric(jnp.concatenate(lhs, axis=1), jnp.concatenate(rhs, axis=0))
            r0 = lax.broadcasted_iota(jnp.int32, (D, D), 0)
            r1 = lax.broadcasted_iota(jnp.int32, (D, D), 1)
            ident = jnp.where(r0 == r1, coeffs[3 * k + 2], 0.0)
            bufs[d] = coeffs[3 * k] * prod + (coeffs[3 * k + 1] * x + ident)

        for count in (1, 2, 3):
            pl.when(passes == count)(functools.partial(product, count))
        return carry

    lax.fori_loop(0, len(STEPS), step, 0)
    bufs[0] = bufs[2] * (inv * factor)

    def apply(b, carry):
        wh, wl = split(bufs[0])
        xs = [mat_ref[2 * b + i] for i in range(2)]

        def tall():
            for i in range(2):
                x = xs[i].astype(BF16)
                upd_ref[2 * b + i] = mm(
                    jnp.concatenate([x, x], axis=1), jnp.concatenate([wh, wl], axis=0)
                )

        def wide():
            x = jnp.concatenate([xs[0].astype(BF16), xs[1].astype(BF16)], axis=1)
            out = mm(jnp.concatenate([wh, wl], axis=1), jnp.concatenate([x, x], axis=0))
            upd_ref[2 * b] = out[:, :D]
            upd_ref[2 * b + 1] = out[:, D:]

        either(flipped, tall, wide)
        return carry

    lax.fori_loop(0, npairs, apply, 0)


def take_first(s_ref, chunks, dst):
    me, core, zed = s_ref[0], s_ref[1], s_ref[2]
    for c, ref in enumerate(chunks):
        for y in range(2):
            part = ((me // 2) ^ 1) ^ y
            rs = pl.ds(pl.multiple_of((core ^ c) * 192 + part * 96, 96), 96)
            for z in range(4):
                dst[zed ^ z, rs, :] = ref[y, z].astype(F32)


def take_second(s_ref, chunks, dst):
    me, core, zed = s_ref[0], s_ref[1], s_ref[2]
    for c, ref in enumerate(chunks):
        for m in range(4):
            rs = pl.ds(pl.multiple_of((core ^ c) * 192 + (me ^ m) * 48, 48), 48)
            for z in range(4):
                dst[zed ^ z, rs, :] = ref[m, z].astype(F32)


def adaln_grads(kept, grd, kf):
    ndev = 2 * kept[0].shape[0] // KEPT_ROWS
    for i, ref in enumerate(kept):
        n = ref.shape[0]
        for j in range(3):
            kf[j, i * n : (i + 1) * n, :] = ref[:, 128 * j : 128 * j + 128].astype(F32)

    def rows(first):
        part = [kf[j, pl.ds(first, ndev, stride=KEPT_ROWS), :] for j in range(3)]
        return jnp.concatenate(part, axis=1).astype(BF16)

    sil = jnp.concatenate([rows(12), rows(13)], axis=0)
    for b in range(6):
        gm = jnp.concatenate([rows(2 * b), rows(2 * b + 1)], axis=0)
        grd[b] = mm(sil, gm, 0, 0)


def add_momentum(t, target, mom, grd, mat, base=0):
    first = MATS[target][2]
    for _, block, r0, n, _, frow, stride in [p for p in shard_pieces(t, 4) if p[0] == target]:
        b = block - first
        for j in range(3):
            cs = slice(128 * j, 128 * j + 128)
            m = mom[pl.ds(frow + j, n, stride=stride), :]
            mat[b, r0 : r0 + n, cs] = MOMENTUM_RATE * m + grd[base + b, r0 : r0 + n, cs]


def add_foreign(s_ref, t, target, foreign, grd, mat):
    core = s_ref[1]
    half = foreign[0].shape[0]
    for _, block, r0, n, crow, _, _ in [p for p in shard_pieces(t ^ 1, 4) if p[0] == target]:
        b = block - MATS[target][2]
        cuts = sorted({crow, crow + n} | {c for c in (half,) if crow < c < crow + n})
        for lo, hi in zip(cuts[:-1], cuts[1:]):
            h = lo // half
            for mine, src in enumerate(foreign):

                @pl.when(core == (h ^ mine))
                def _(b=b, r0=r0, lo=lo, hi=hi, h=h, crow=crow, src=src):
                    dst = slice(r0 + lo - crow, r0 + hi - crow)
                    m = src[lo - h * half : hi - h * half, :].astype(F32)
                    mat[b, dst, :] = MOMENTUM_RATE * m + grd[b, dst, :]


TAIL = 48


def ns_a_kernel(s_ref, ints, coeffs, mom, fx0, fx1, kz0, kz1, ch0, ch1, upd, grd, tail, mat, bufs, kf):
    me = s_ref[0]

    @pl.when(me < 2)
    def _():
        adaln_grads((kz0, kz1), grd, kf)

    @pl.when(me >= 2)
    def _():
        take_first(s_ref, (ch0, ch1), grd)

    for t, target in enumerate((ADALN, ADALN, UP, DOWN)):

        @pl.when(me == t)
        def _(t=t, target=target):
            add_momentum(t, target, mom, grd, mat)
            if target != DOWN:
                add_foreign(s_ref, t, target, (fx0, fx1), grd, mat)

    npairs = jnp.where(me < 2, 3, 2)
    factor = jnp.where(me < 2, update_scale(ADALN), update_scale(UP))
    newton_schulz(ints, coeffs, mat, upd, bufs, npairs, me == 3, factor)

    for b in range(4):
        rs = slice(TAIL * b, TAIL * b + TAIL)
        tail[0, rs, :] = grd[b, D - TAIL :, :].astype(BF16)
        tail[1, rs, :] = upd[b, D - TAIL :, :].astype(BF16)


def ns_a(sidx, tables, mom, foreign, kept, chunks):
    sd = jax.ShapeDtypeStruct((6, D, D), F32)
    return pl.pallas_call(
        ns_a_kernel,
        out_shape=(sd, sd, jax.ShapeDtypeStruct((2, 4 * TAIL, D), BF16)),
        in_specs=[sspec()] * 3 + [vspec()] * 7,
        out_specs=(vspec(),) * 3,
        scratch_shapes=[
            pltpu.VMEM((6, D, D), F32),
            pltpu.VMEM((4, D, D), F32),
            pltpu.VMEM((3, 2 * kept[0].shape[0], 128), F32),
        ],
        compiler_params=params_of(14),
        cost_estimate=pl.CostEstimate(flops=8_000_000_000, bytes_accessed=12_000_000, transcendentals=0),
        name="ns_a",
    )(sidx, *tables, mom, *foreign, *kept, *chunks)


def final_kernel(
    s_ref, ints, coeffs, par, mom, ch0, ch1, upa, grda, tail, ograd, onew, omom,
    upb, gb, mat, bufs, og, on, om, sems
):
    me = s_ref[0]
    inner = jnp.logical_or(me == 1, me == 2)

    @pl.when(inner)
    def _():
        take_second(s_ref, (ch0, ch1), gb)
        for b in range(1, 4):
            mat[b] = jnp.zeros((D, D), F32)

    @pl.when(me == 1)
    def _():
        add_momentum(1, QKV, mom, gb, mat)

    @pl.when(me == 2)
    def _():
        add_momentum(2, OUTW, mom, gb, mat, 3)

    def each(t, body):
        for mat_id, block, r0, n, _, frow, stride in shard_pieces(t, 4):
            b = block - MATS[mat_id][2]
            for j in range(3):
                cs = slice(128 * j, 128 * j + 128)
                fl = pl.ds(frow + j, n, stride=stride)
                if mat_id == UP and t == 3:
                    assert r0 == D - TAIL and n == TAIL
                    ts = slice(TAIL * b, TAIL * b + TAIL)
                    body(fl, lambda: tail[0, ts, cs].astype(F32), lambda: tail[1, ts, cs].astype(F32))
                    continue
                rs = slice(r0, r0 + n)
                if mat_id in (QKV, OUTW):
                    gb_at = b + 3 * (mat_id == OUTW)
                    body(fl, lambda: gb[gb_at, rs, cs], lambda: upb[b, rs, cs])
                else:
                    body(fl, lambda: grda[b, rs, cs], lambda: upa[b, rs, cs])

    def gradient(fl, g, u):
        value = g()
        og[fl, :] = value
        om[fl, :] = MOMENTUM_RATE * mom[fl, :] + value

    def update(fl, g, u):
        on[fl, :] = par[fl, :] - u()

    for t in range(4):
        pl.when(me == t)(functools.partial(each, t, gradient))
    early = [pltpu.make_async_copy(og, ograd, sems.at[0]), pltpu.make_async_copy(om, omom, sems.at[1])]
    for copy in early:
        copy.start()

    @pl.when(inner)
    def _():
        npairs = jnp.where(me == 1, 2, 1)
        factor = jnp.where(me == 1, update_scale(QKV), update_scale(OUTW))
        newton_schulz(ints, coeffs, mat, upb, bufs, npairs, None, factor)

    for t in range(4):
        pl.when(me == t)(functools.partial(each, t, update))
    late = pltpu.make_async_copy(on, onew, sems.at[2])
    late.start()
    for copy in early + [late]:
        copy.wait()


def final_call(sidx, tables, par, mom, chunks, upa, grda, tail):
    sd = jax.ShapeDtypeStruct(par.shape, F32)
    block4 = pltpu.VMEM((4, D, D), F32)
    return pl.pallas_call(
        final_kernel,
        out_shape=(sd, sd, sd),
        in_specs=[sspec()] * 3 + [vspec()] * 7,
        out_specs=(hspec(),) * 3,
        scratch_shapes=[block4] * 4 + [pltpu.VMEM(par.shape, F32)] * 3 + [pltpu.SemaphoreType.DMA((3,))],
        compiler_params=params_of(22),
        cost_estimate=pl.CostEstimate(flops=8_000_000_000, bytes_accessed=24_000_000, transcendentals=0),
        name="finish",
    )(sidx, *tables, par, mom, *chunks, upa, grda, tail)


def swap(x, axis, mask):
    count = lax.axis_size(axis)
    return lax.ppermute(x, axis, [(i, i ^ mask) for i in range(count)])


def more_rows(x, hops):
    for axis, mask in hops:
        x = jnp.concatenate([x, swap(x, axis, mask)], axis=0)
    return x


def wide_sum(parts):
    total = None
    for p in parts:
        total = p.astype(F32) if total is None else total + p.astype(F32)
    return total


def join_kernel(own, other, keep, *msgs):
    n = own.shape[1]
    for m, msg in enumerate(msgs, 1):
        msg[:n, :] = (own[m] + other[m].astype(F32)).astype(BF16)
        msg[n:, :] = keep[...]


def join_call(own, other, keep):
    out = jax.ShapeDtypeStruct((own.shape[1] + keep.shape[0], D), BF16)
    return pl.pallas_call(
        join_kernel,
        out_shape=(out,) * 3,
        in_specs=[vspec()] * 3,
        out_specs=(vspec(),) * 3,
        compiler_params=params_of(4),
        cost_estimate=pl.CostEstimate(flops=0, bytes_accessed=2_000_000, transcendentals=0),
        name="join",
    )(own, other, keep)


def piece_kernel(has_keep, s_ref, own, other, *refs):
    keep = refs[0] if has_keep else None
    got = refs[has_keep : has_keep + 3]
    outs = refs[has_keep + 3 :]
    zed = s_ref[2]
    n = outs[0].shape[0]
    size = 4 * n
    if has_keep:
        rows = outs[4]
        kr = keep.shape[0]
        rows[:kr, :] = keep[...]
        for m in range(3):
            rows[kr * (m + 1) : kr * (m + 2), :] = got[m][size:, :]
    for i in range(4):
        rs = pl.ds(pl.multiple_of((zed ^ i) * n, n), n)
        total = own[0, rs, :] + other[0, rs, :].astype(F32)
        for g in got:
            total = total + g[rs, :].astype(F32)
        if i == 0:
            outs[0][...] = total
        else:
            outs[i][:n, :] = total.astype(BF16)
            if has_keep:
                outs[i][n:, :] = rows[...]


def piece_call(sidx, own, other, got, keep=None):
    size = own.shape[1]
    n = size // 4
    extra = 0 if keep is None else 4 * keep.shape[0]
    sd = jax.ShapeDtypeStruct
    outs = (sd((n, D), F32),) + (sd((n + extra, D), BF16),) * 3
    if extra:
        outs += (sd((extra, D), BF16),)
    kept = [] if keep is None else [keep]
    return pl.pallas_call(
        functools.partial(piece_kernel, len(kept)),
        out_shape=outs,
        in_specs=[sspec()] + [vspec()] * (len(kept) + 5),
        out_specs=(vspec(),) * len(outs),
        compiler_params=params_of(6),
        cost_estimate=pl.CostEstimate(flops=0, bytes_accessed=2_000_000, transcendentals=0),
        name="piece",
    )(sidx, own, other, *kept, *got)


def z_sum(mine, pieces):
    n = mine.shape[0]
    got = []
    for m, piece in enumerate(pieces, 1):
        got.append(swap(piece, "rep", 2 * m))
    total = wide_sum([mine] + [g[:n] for g in got]).astype(BF16)
    return total, [g[n:] for g in got]


def fan(x, axis, masks):
    got = [x]
    for m in masks:
        got.append(swap(x, axis, m))
    return jnp.stack(got)


def fast_device(tokens, conditions, assignment, params, momentum, cotangent):
    return fast_body(tokens, conditions, assignment, params, momentum, cotangent)


def fast_body(tokens, conditions, assignment, params, momentum, cotangent):
    me = lax.axis_index("fsdp")
    rep = lax.axis_index("rep")
    core, zed = rep % 2, rep // 2
    lat = tokens.shape[0]
    rows = lat * SEQ
    par = params.reshape(-1, 128)
    mom = momentum.reshape(-1, 128)
    source = assignment // lat
    apart = ((source // 8) ^ me) + 4 * ((source % 8) ^ rep)
    pick = apart * lat + assignment % lat
    sidx = jnp.concatenate([jnp.stack([me, core, zed]), pick]).astype(jnp.int32)

    hop = swap(conditions, "fsdp", 1)
    top, bottom = prep(sidx, par, 4, 2)
    table = jnp.concatenate([conditions, hop], axis=0)
    table, top, bottom = lax.optimization_barrier((table, top, bottom))
    hop = swap(table, "fsdp", 2)
    x0 = swap(top, "fsdp", 1)
    y1 = swap(bottom, "fsdp", 2)
    x1 = swap(bottom, "fsdp", 1)
    y0 = swap(top, "fsdp", 2)
    table = jnp.concatenate([table, hop], axis=0)
    table = more_rows(table, (("rep", 1),))
    table = more_rows(table, (("rep", 2), ("rep", 4)))
    x0, y1, table = lax.optimization_barrier((x0, y1, table))
    d0 = swap(x0, "fsdp", 2)
    d1 = swap(y1, "fsdp", 1)
    received = (x0, x1, y0, y1, d0, d1)
    (wc,) = prep(sidx, par, 4, 0)
    bufs = (wc,) + received + tuple(swap(r, "rep", 1) for r in received)
    (mh,) = prep(sidx, mom, 4, 1)
    fx0 = swap(mh, "fsdp", 1)

    tok2, cot2 = tokens.reshape(rows, D), cotangent.reshape(rows, D)
    (blend, qkv, probs, ai, gafter, gmx, mods, gmod1, silu, wqkv, gout, keep1, send1) = main_call(
        sidx, table, tok2, cot2, bufs, True
    )
    fx1 = swap(fx0, "rep", 1)

    other = swap(send1, "rep", 1)
    gqkv = heads_call(qkv, probs, gmx)
    got = []
    for m in (1, 2, 3):
        got.append(swap((keep1[m] + other[m].astype(F32)).astype(BF16), "fsdp", m))
    gtok, keep2, send2, keep = input_call(sidx, tok2, gqkv, ai, gafter, mods, gmod1, silu, wqkv, gout)
    mine, *pieces = piece_call(sidx, keep1, other, got)
    total, _ = z_sum(mine, pieces)
    col = fan(total, "rep", (2, 4, 6))
    across = swap(col, "fsdp", 2)
    pair = jnp.stack([col, across])
    pairs = (pair, swap(pair, "rep", 1))

    other = swap(send2, "rep", 1)
    msgs = join_call(keep2, other, keep)
    got = []
    for m in (1, 2, 3):
        got.append(swap(msgs[m - 1], "fsdp", m))
    mine, *pieces, rows2 = piece_call(sidx, keep2, other, got, keep)
    q2, more = z_sum(mine, pieces)
    kz = jnp.concatenate([rows2] + more, axis=0)
    kept = (kz, swap(kz, "rep", 1))
    quad = fan(fan(q2, "rep", (2, 4, 6)), "fsdp", (1, 2, 3))
    quads = (quad, swap(quad, "rep", 1))

    tables = step_tables()
    upa, grda, tail = ns_a(sidx, tables, mom, (fx0, fx1), kept, pairs)
    tail = lax.ppermute(tail, "fsdp", [(2, 3)])
    ograd, onew, omom = final_call(sidx, tables, par, mom, quads, upa, grda, tail)
    shape = tokens.shape
    return (
        blend.reshape(shape),
        gtok.reshape(shape),
        ograd.reshape(-1),
        onew.reshape(-1),
        omom.reshape(-1),
    )


def unpack(flat):
    pieces, offset = [], 0
    for rows_count, cols_count, _, _ in MATS:
        pieces.append(flat[offset : offset + rows_count * cols_count].reshape(rows_count, cols_count))
        offset += rows_count * cols_count
    return pieces


def to_blocks(mats):
    out = []
    for matrix, (rows_count, cols_count, _, by_cols) in zip(mats, MATS):
        if by_cols:
            out.append(matrix.reshape(D, cols_count // D, D).transpose(1, 0, 2))
        else:
            out.append(matrix.reshape(rows_count // D, D, D))
    return jnp.concatenate(out, axis=0)


def from_blocks(blocks, by_cols):
    if by_cols:
        return blocks.transpose(1, 0, 2).reshape(-1)
    return blocks.reshape(-1)


def orthogonalize(matrix):
    flipped = matrix.shape[0] > matrix.shape[1]
    current = matrix.T if flipped else matrix
    current = current / (jnp.sqrt(jnp.sum(current * current)) + 1e-07)
    for _ in range(NS_ITERS):
        square = jnp.dot(current, current.T, precision=lax.Precision.HIGHEST)
        polynomial = COEFF_B * square + COEFF_C * jnp.dot(square, square, precision=lax.Precision.HIGHEST)
        current = COEFF_A * current + jnp.dot(polynomial, current, precision=lax.Precision.HIGHEST)
    return current.T if flipped else current


def scaled_update(matrix, factor):
    return (factor * orthogonalize(matrix)).reshape(-1)


def empty_update(matrix, factor):
    return jnp.zeros((matrix.shape[0] * matrix.shape[1],), F32)


def any_device(tokens, conditions, assignment, params, momentum, cotangent):
    lat = tokens.shape[0]
    rows = lat * SEQ
    table = lax.all_gather(conditions, ("fsdp", "rep"), axis=0, tiled=True)
    gathered = lax.all_gather(params.astype(BF16), "fsdp", axis=0, tiled=True)
    blocks = to_blocks(unpack(gathered))
    me = lax.axis_index("fsdp")
    sidx = jnp.concatenate([jnp.zeros((3,), jnp.int32), assignment.astype(jnp.int32)])
    tok2, cot2 = tokens.reshape(rows, D), cotangent.reshape(rows, D)
    (blend, qkv, probs, ai, gafter, gmx, mods, gmod1, silu, wqkv, gout, keep1, send1) = main_call(
        sidx, table, tok2, cot2, (blocks,), False
    )
    gqkv = heads_call(qkv, probs, gmx)
    gtok, keep2, send2, keep = input_call(sidx, tok2, gqkv, ai, gafter, mods, gmod1, silu, wqkv, gout)
    halves1 = jnp.stack([keep1, send1.astype(F32)]).reshape(2, 4, 4, 96, D)
    up = halves1[:, jnp.array([2, 0])].transpose(2, 0, 1, 3, 4).reshape(4, D, D)
    down = halves1[:, jnp.array([3, 1])].transpose(2, 0, 1, 3, 4).reshape(4, D, D)
    halves2 = jnp.stack([keep2, send2.astype(F32)]).reshape(2, 4, 4, 48, D)
    last = halves2.transpose(2, 0, 1, 3, 4).reshape(4, D, D)
    rest = jnp.concatenate(
        [from_blocks(last[:3], True), last[3].reshape(-1), from_blocks(up, True), down.reshape(-1)]
    )
    kept = lax.all_gather(keep, ("fsdp", "rep"), axis=0, tiled=True).reshape(-1, KEPT_ROWS, D)
    silu_all = kept[:, 6 * lat : 7 * lat].reshape(-1, D)
    mod_all = kept[:, : 6 * lat].reshape(-1, 6, lat, D).transpose(0, 2, 1, 3).reshape(-1, 6 * D)
    adaln = lax.dot_general(silu_all, mod_all, (((0,), (0,)), ((), ())), preferred_element_type=F32)
    shard_len = params.shape[0]
    head = jnp.concatenate([adaln.reshape(-1), jnp.zeros_like(rest)])
    flat = jnp.concatenate([jnp.zeros((D * 6 * D,), F32), rest])
    part = lax.psum_scatter(flat, "fsdp", scatter_dimension=0, tiled=True)
    full_grad = lax.psum(part, "rep") + lax.dynamic_slice_in_dim(head, me * shard_len, shard_len, 0)
    new_momentum = MOMENTUM_RATE * momentum + full_grad
    whole_mom = lax.all_gather(new_momentum, "fsdp", axis=0, tiled=True)
    group_size = lax.axis_size("fsdp")
    updates, offset = [], 0
    for mat, piece in enumerate(unpack(whole_mom)):
        factor = F32(update_scale(mat))
        owner = (offset // shard_len + group_size // 2) % group_size
        updates.append(lax.cond(me == owner, scaled_update, empty_update, piece, factor))
        offset += piece.size
    update = lax.psum_scatter(jnp.concatenate(updates), "fsdp", scatter_dimension=0, tiled=True)
    shape = tokens.shape
    return (blend.reshape(shape), gtok.reshape(shape), full_grad, params - update, new_momentum)


def solution(mesh):
    both = ("fsdp", "rep")
    in_specs = (P(both, None, None), P(both, None), P(both), P("fsdp"), P("fsdp"), P(both, None, None))
    out_specs = (P(both, None, None), P(both, None, None), P("fsdp"), P("fsdp"), P("fsdp"))
    small = dict(mesh.shape) == {"fsdp": 4, "rep": 8}
    return jax.shard_map(
        fast_device if small else any_device,
        mesh=mesh,
        in_specs=in_specs,
        out_specs=out_specs,
        check_vma=False,
    )
```
